32 devices in a mesh: parts: 2 (over x), tile: 16 (over z, y, core).
Axes of the slice: x: 2, y: 2, z: 4, core: 2. Of those that a mesh axis runs over, the one named last changes fastest.
Arguments:
- sections: bfloat16 [4096, 2048], P(('parts', 'tile')), parts along dimension 0, may hold values from -10 to 10
- valid_mask: int32 [32, 16], P(('parts', 'tile')), parts along dimension 0, may hold values 0 or 1
- coarse_offsets: int32 [8, 2], P('parts'), parts along dimension 0, may hold values from -3 to 3
Outputs:
- aligned: bfloat16 [4096, 2048], P(('parts', 'tile')), parts along dimension 0
- node_shift: float32 [2, 32, 16], P(None, ('parts', 'tile')), parts along dimension 1
The draws below stay inside these ranges and needn't reach their ends.
There are 2 independent parts, one for each index of `parts`. The reference program is written for one: setup_inputs(seed, part) draws one part's arguments, and reference() takes and returns one part's arrays. A program takes and returns all parts, laid end to end along the dimension named above; each array names one. Nothing has to cross between parts.
All inputs are finite; a program needn't handle non-finite values. No bound on the sum of `valid_mask` on one device may be relied on, other than what follows from the above.
Results may differ from the reference program's by a relative error of at most 0.002.
Values may be sent and summed in bfloat16 or wider, within the bound.
A program may use at most 64 MiB of HBM per device.

```python
import jax
import jax.numpy as jnp
from jax import lax

SECTIONS = 4
PATCH = 128
PC = 16
HALF = 4
SWEEPS = 3
TPS = 4


def draw_sections(key, part):
    row_count = TPS * PATCH
    col_count = PC * PATCH
    common_key = jax.random.fold_in(key, 11)
    own_key = jax.random.fold_in(key, 12)
    common = jax.random.normal(common_key, (row_count, col_count), jnp.float32)
    own_part = jax.random.normal(own_key, (SECTIONS, row_count, col_count), jnp.float32)
    volume = jnp.clip(0.6 * common[None] + 0.8 * own_part, -6.0, 6.0)
    return volume.reshape(SECTIONS * row_count, col_count).astype(jnp.bfloat16)


def touch_ends(drawn, stream_key, least, largest):
    spot = [jax.random.randint(jax.random.fold_in(stream_key, axis), (), 0, length) for axis, length in enumerate(drawn.shape)]
    widest = drawn.shape.index(max(drawn.shape))
    neighbour = spot[:widest] + [(spot[widest] + 1) % drawn.shape[widest]] + spot[widest + 1:]
    return drawn.at[tuple(spot)].set(least).at[tuple(neighbour)].set(largest)


def setup_inputs(seed: int = 0, part: int = 0) -> dict:
    splits = jax.random.split(jax.random.key(seed), 4)
    part_keys = jax.random.split(jax.random.fold_in(splits[3], part), 4)
    sections = draw_sections(jax.random.fold_in(jax.random.fold_in(splits[3], part), 71), part)
    valid_mask = touch_ends((jax.random.randint(part_keys[1], (SECTIONS * TPS, PC), 0, 4) < 3).astype(jnp.int32), jax.random.fold_in(part_keys[1], 1), 0, 1)
    coarse_offsets = touch_ends(jax.random.randint(part_keys[2], (SECTIONS, 2), -3, 4), jax.random.fold_in(part_keys[2], 1), -3, 3).astype(jnp.int32)
    return {"sections": sections, "valid_mask": valid_mask, "coarse_offsets": coarse_offsets}


highest = lax.Precision.HIGHEST
sharpness = 12.0
anchor_weight = 2.0

def fourier_tables(length):
    index_vector = jnp.arange(length, dtype=jnp.int32)
    phase_index = index_vector[:, None] * index_vector[None, :] % length
    angles = phase_index.astype(jnp.float32) * (2.0 * jnp.pi / length)
    return (jnp.cos(angles), -jnp.sin(angles))

def left_apply(matrix, blocks):
    return jnp.einsum('jk,...kl->...jl', matrix, blocks, precision=highest)

def right_apply(blocks, matrix):
    return jnp.einsum('...jk,kl->...jl', blocks, matrix, precision=highest)

def forward(blocks, cosine_table, sine_table):
    first_re = left_apply(cosine_table, blocks)
    first_im = left_apply(sine_table, blocks)
    out_re = right_apply(first_re, cosine_table) - right_apply(first_im, sine_table)
    out_im = right_apply(first_re, sine_table) + right_apply(first_im, cosine_table)
    return (out_re, out_im)

def centred(blocks):
    mean_level = lax.optimization_barrier(jnp.mean(blocks, axis=(-2, -1), keepdims=True))
    centre = blocks - mean_level
    spread = jnp.sqrt(lax.optimization_barrier(jnp.mean(centre * centre, axis=(-2, -1), keepdims=True)) + 1e-05)
    return (centre, mean_level, spread)

def window_tables(offset, length):
    shift_values = offset + jnp.arange(-HALF, HALF + 1, dtype=jnp.int32)
    frequency = jnp.arange(length, dtype=jnp.int32)
    phase_index = jnp.mod(shift_values[:, None] * frequency[None, :], length)
    angles = phase_index.astype(jnp.float32) * (2.0 * jnp.pi / length)
    return (jnp.cos(angles), jnp.sin(angles), shift_values.astype(jnp.float32))

def estimate_flow(own_re, own_im, own_spread, prev_re, prev_im, prev_spread, offset_pair):
    length = PATCH
    cross_re = own_re * prev_re + own_im * prev_im
    cross_im = own_im * prev_re - own_re * prev_im
    row_cos, row_sin, row_shifts = window_tables(offset_pair[0], length)
    col_cos, col_sin, col_shifts = window_tables(offset_pair[1], length)
    half_re = left_apply(row_cos, cross_re) - left_apply(row_sin, cross_im)
    half_im = left_apply(row_cos, cross_im) + left_apply(row_sin, cross_re)
    correlation = jnp.einsum('...jk,lk->...jl', half_re, col_cos, precision=highest) - jnp.einsum('...jk,lk->...jl', half_im, col_sin, precision=highest)
    similarity = correlation / (float(length) ** 4 * own_spread * prev_spread)
    weights = jnp.exp(sharpness * similarity)
    weight_sum = lax.optimization_barrier(jnp.sum(weights, axis=(-2, -1), keepdims=True))
    chance = weights / weight_sum
    flow_rows = lax.optimization_barrier(jnp.sum(chance * row_shifts[:, None], axis=(-2, -1)))
    flow_cols = lax.optimization_barrier(jnp.sum(chance * col_shifts[None, :], axis=(-2, -1)))
    return jnp.stack([flow_rows, flow_cols], axis=0)

def warp_patches(spec_re, spec_im, mean_level, shift_rows, shift_cols, cosine_table, sine_table):
    length = PATCH
    frequency = jnp.arange(length, dtype=jnp.int32)
    signed_freq = jnp.where(frequency < length // 2, frequency, frequency - length).astype(jnp.float32)
    phase_angle = 2.0 * jnp.pi / length * (signed_freq[:, None] * shift_rows[..., None, None] + signed_freq[None, :] * shift_cols[..., None, None])
    turn_cos = jnp.cos(phase_angle)
    turn_sin = jnp.sin(phase_angle)
    moved_re = spec_re * turn_cos - spec_im * turn_sin
    moved_im = spec_re * turn_sin + spec_im * turn_cos
    back_re = cosine_table
    back_im = -sine_table
    inner_re = left_apply(back_re, moved_re) - left_apply(back_im, moved_im)
    inner_im = left_apply(back_re, moved_im) + left_apply(back_im, moved_re)
    restored = right_apply(inner_re, back_re) - right_apply(inner_im, back_im)
    return restored / float(length * length) + mean_level

def relax_mesh(flow_nodes, mask_float):
    weight = anchor_weight * mask_float
    padded_ones = jnp.pad(jnp.ones_like(mask_float), 1)
    neighbour_count = padded_ones[:-2, 1:-1] + padded_ones[2:, 1:-1] + padded_ones[1:-1, :-2] + padded_ones[1:-1, 2:]
    node_shift = flow_nodes * mask_float
    for sweep_index in range(SWEEPS):
        padded = jnp.pad(node_shift, ((0, 0), (1, 1), (1, 1)))
        neighbours = padded[:, :-2, 1:-1] + padded[:, 2:, 1:-1] + padded[:, 1:-1, :-2] + padded[:, 1:-1, 2:]
        node_shift = (weight * flow_nodes + neighbours) / (weight + neighbour_count)
    return node_shift

def to_patches(strip):
    return strip.astype(jnp.float32).reshape(-1, PATCH, PC, PATCH).transpose(0, 2, 1, 3)

def from_patches(patches):
    return patches.transpose(0, 2, 1, 3).reshape(-1, PC * PATCH)

def reference(sections, valid_mask, coarse_offsets):
    half_rows = TPS // 2
    sections = jnp.roll(sections, -half_rows * PATCH, axis=0)
    valid_mask = jnp.roll(valid_mask, -half_rows, axis=0)
    cosine_table, sine_table = fourier_tables(PATCH)
    strip_rows = TPS * PATCH
    aligned_list = [sections[:strip_rows]]
    shift_list = [jnp.zeros((2, TPS, PC), jnp.float32)]
    previous = sections[:strip_rows]
    for section_index in range(1, SECTIONS):
        current = to_patches(sections[section_index * strip_rows:(section_index + 1) * strip_rows])
        own_centre, own_level, own_spread = centred(current)
        own_re, own_im = forward(own_centre, cosine_table, sine_table)
        prev_patches = to_patches(lax.optimization_barrier(previous))
        prev_centre, prev_level, prev_spread = centred(prev_patches)
        prev_re, prev_im = forward(prev_centre, cosine_table, sine_table)
        flow_nodes = estimate_flow(own_re, own_im, own_spread, prev_re, prev_im, prev_spread, coarse_offsets[section_index])
        mask_float = valid_mask[section_index * TPS:(section_index + 1) * TPS].astype(jnp.float32)
        node_shift = relax_mesh(flow_nodes, mask_float)
        warped = warp_patches(own_re, own_im, own_level, node_shift[0], node_shift[1], cosine_table, sine_table).astype(jnp.bfloat16)
        strip = from_patches(warped)
        previous = strip
        aligned_list.append(strip)
        shift_list.append(node_shift)
    aligned_all = jnp.roll(jnp.concatenate(aligned_list, axis=0), half_rows * PATCH, axis=0)
    shift_all = jnp.roll(jnp.concatenate(shift_list, axis=1), half_rows, axis=1)
    return (aligned_all, shift_all)
```

```python
import functools

import jax
import jax.numpy as jnp
import numpy as np
from jax import lax
from jax.experimental import pallas as pl
from jax.experimental.pallas import tpu as pltpu
from jax.sharding import PartitionSpec as P

SECTIONS = 4
PATCH = 128
HALF = 4
SWEEPS = 3
REACH = 3
WINDOW = 2 * HALF + 1
PADDED = 16
LANES = 128
CHUNK = 2
PIECES = 2

sharpness = 12.0
anchor_weight = 2.0
MESH = pl.DeviceIdType.MESH
f32 = jnp.float32
bf16 = jnp.bfloat16


def split(value):
    high = value.astype(bf16)
    return high, (value - high.astype(f32)).astype(bf16)


def mm(a, b):
    return jnp.dot(a, b, preferred_element_type=f32)


def mm_nt(a, b):
    return lax.dot_general(a, b, (((1,), (1,)), ((), ())), preferred_element_type=f32)


def constants():
    n = PATCH
    k = np.arange(n)
    angle = 2 * np.pi * ((k[:, None] * k[None, :]) % n) / n
    cosine, sine = np.cos(angle), np.sin(angle)
    left = []
    for table in (cosine, sine):
        high = np.asarray(table, bf16)
        low = np.asarray(table - high.astype(np.float64), bf16)
        left.append(np.concatenate([high, low], axis=1))
    left = np.concatenate(left, axis=0)
    right = np.block([[cosine, -sine], [-sine, -cosine]])
    right = np.asarray(right, bf16)
    u = np.arange(-HALF - REACH, -HALF - REACH + 24)
    window_angle = 2 * np.pi * ((u[:, None] * k[None, :]) % n) / n
    window = np.stack([np.cos(window_angle), np.sin(window_angle)])
    window = window.astype(np.float32)
    half_angle = np.pi * k / n
    sign = 1.0 - 2.0 * (k % 2)
    warp = np.zeros((8, n), np.float32)
    warp[:4] = np.stack([np.sin(half_angle), np.cos(half_angle), sign, k])
    parity = (sign[:, None] * sign[None, :]).astype(np.float32)
    return left, right, window, warp, parity


def turn(value):
    small = (value - jnp.round(value)) * np.pi
    square = small * small
    sine = small * (1.0 + square * (-1 / 6 + square * (1 / 120 + square * (
        -1 / 5040 + square * (1 / 362880 - square * (1 / 39916800))))))
    cosine = 1.0 + square * (-1 / 2 + square * (1 / 24 + square * (-1 / 720 + square * (
        1 / 40320 + square * (-1 / 3628800 + square * (1 / 479001600))))))
    return 1.0 - 2.0 * (sine * sine), 2.0 * (sine * cosine)


def shift_terms(d):
    whole = jnp.round(d)
    frac = d - whole
    odd = jnp.abs(whole - 2.0 * jnp.round(whole * 0.5))
    sine = jnp.sin(jnp.pi * frac)
    signed = jnp.where(odd > 0.5, -sine, sine) * (1.0 / PATCH)
    angle = d * (np.pi / PATCH)
    tangent = jnp.sin(angle) / jnp.cos(angle)
    small = frac * (np.pi / PATCH)
    tiny = jnp.abs(frac) < 1e-6
    peak = jnp.where(
        tiny, 1.0, sine * jnp.cos(small) / jnp.where(tiny, 1.0, PATCH * jnp.sin(small))
    )
    return tangent, signed, peak, whole


def kernel_rows(terms, tables):
    columns = jnp.transpose(terms)[:LANES]
    sine, cosine, parity, gap = [tables[i : i + 1, :] for i in range(4)]
    found = []
    for base, forward in ((0, False), (4, True)):
        tangent, signed, peak, whole = [columns[:, base + i : base + i + 1] for i in range(4)]
        if forward:
            bottom = cosine * tangent + sine
            top = cosine - sine * tangent
            centre = jnp.where(whole > 0, PATCH - whole, -whole)
        else:
            bottom = cosine * tangent - sine
            top = cosine + sine * tangent
            centre = jnp.where(whole < 0, whole + PATCH, whole)
        found.append(jnp.where(gap == centre, peak, (signed * parity) * (top / bottom)))
    corner = columns[:, 1:2] * columns[:, 5:6]
    return found[0], found[1], corner


def circulant(row):
    spread = jnp.broadcast_to(row, (PATCH, PATCH))
    return split(pltpu.roll(spread, 0, 1, stride=1, stride_axis=0))


def warp_patch(patch, rows, i, checker, parity):
    left = circulant(rows[0][i : i + 1, :])
    right = circulant(rows[1][i : i + 1, :])
    both = mm(patch, jnp.concatenate(right, axis=1))
    high, low = split(both[:, :PATCH] + both[:, PATCH:])
    lower = jnp.concatenate([high, jnp.zeros_like(low)], axis=1)
    inner = jnp.concatenate([jnp.concatenate([high, low], axis=1), lower], axis=0)
    moved = mm(jnp.concatenate(left, axis=1), inner)
    corner = (rows[2][i : i + 1, :] * checker) * parity
    return (moved[:, :PATCH] + moved[:, PATCH:]) - corner


def total(value):
    return jnp.sum(jnp.sum(value, axis=0, keepdims=True), axis=1, keepdims=True)


def term_rows(d_rows, d_cols):
    both = jnp.concatenate([d_rows, d_cols], axis=0)
    tangent, signed, peak, whole = shift_terms(both)
    pieces = [t[i : i + 1] for i in range(2) for t in (tangent, signed, peak, whole)]
    return jnp.concatenate(pieces, axis=0)


def patch_slices(width):
    return [slice(i * PATCH, (i + 1) * PATCH) for i in range(width // PATCH)]


def chain_kernel(
    tile_count,
    grid_cols,
    offsets_in,
    mask_in,
    left_in,
    right_in,
    window_in,
    strip,
    out_ref,
    left_ref,
    right_ref,
    window,
    offsets,
    mask_ref,
    load_sem,
    own_raw,
    prev_raw,
    next_raw,
    own_re,
    own_im,
    down_cross,
    up_cross,
    stats,
    mask_tile,
    mask_slots,
    flow_tile,
    flow_slots,
    shift_ref,
    bulk_send,
    bulk_recv,
    mask_send,
    mask_recv,
    flow_send,
    flow_recv,
):
    per_section = tile_count // SECTIONS
    me = lax.axis_index("tile")
    lead = per_section // 2
    rotated = lax.rem(me + tile_count - lead, tile_count)
    group = rotated // per_section
    row = lax.rem(rotated, per_section)
    chunks, width = own_raw.shape[0], own_raw.shape[2]
    pair = width // PATCH
    nodes = chunks * pair
    half = lax.rem(group, 2)
    base = half * nodes

    def device(section, line):
        return lax.rem(section * per_section + line + lead, tile_count)

    def mate(line_step):
        return lax.rem(row + line_step, per_section)

    barrier = pltpu.get_barrier_semaphore()
    for step in range(1, tile_count):
        peer = lax.rem(me + step, tile_count)
        pl.semaphore_signal(barrier, inc=1, device_id={"tile": peer}, device_id_type=MESH)

    def columns(side, chunk):
        start = pl.multiple_of((side * chunks + chunk) * width, LANES)
        return strip.at[:, pl.ds(start, width)]

    loads = [
        pltpu.make_async_copy(source, target, load_sem.at[i])
        for i, (source, target) in enumerate(
            [(mask_in, mask_ref), (offsets_in, offsets), (window_in, window)]
            + [(left_in, left_ref), (right_in, right_ref)]
            + [(columns(half, q), own_raw.at[q]) for q in range(chunks)]
        )
    ]
    for copy in loads:
        copy.start()
    loads[0].wait()
    shape = (2 * per_section, LANES)
    sub = lax.broadcasted_iota(jnp.int32, shape, 0)
    lane = lax.broadcasted_iota(jnp.int32, shape, 1)
    sub_row = lax.rem(sub, per_section)
    mask_tile[...] = jnp.zeros(shape, f32)
    mask_tile[0:1, 0:grid_cols] = mask_ref[...].astype(f32)
    mask_row = mask_tile[0:1, :]
    mask_tile[...] = jnp.where(sub_row == row, mask_row, 0.0)
    mask_slots[1, row] = mask_tile[...]
    shift_ref[...] = jnp.zeros((2,) + shape, f32)

    pl.semaphore_wait(barrier, tile_count - 1)

    def bulk(way, chunk):
        peer = lax.rem(me + (per_section if way else tile_count - per_section), tile_count)
        return pltpu.make_async_remote_copy(
            src_ref=columns(1 - half, chunk),
            dst_ref=(prev_raw if way else next_raw).at[chunk],
            send_sem=bulk_send.at[way, chunk],
            recv_sem=bulk_recv.at[1 - way, chunk],
            device_id={"tile": peer},
            device_id_type=MESH,
        )

    def start_bulk(way):
        for chunk in range(chunks):
            bulk(way, chunk).start()

    def end_bulk(way):
        for chunk in range(chunks):
            bulk(way, chunk).wait_send()

    @pl.when(jnp.logical_or(group == 1, group == 2))
    def _():
        start_bulk(0)

    @pl.when(group <= 1)
    def _():
        start_bulk(1)

    def mask_copy(ahead, step):
        return pltpu.make_async_remote_copy(
            src_ref=mask_tile,
            dst_ref=mask_slots.at[1 - ahead, row],
            send_sem=mask_send.at[ahead, step],
            recv_sem=mask_recv.at[1 - ahead, row],
            device_id={"tile": device(group + ahead, mate(step))},
            device_id_type=MESH,
        )

    for step in range(1, per_section):
        mask_copy(0, step).start()

    @pl.when(group < SECTIONS - 1)
    def _():
        for step in range(per_section):
            mask_copy(1, step).start()

    for copy in loads[1:]:
        copy.wait()

    eight = lax.broadcasted_iota(jnp.int32, (8, LANES), 0)

    def spectra(pixels, kind, first_node):
        table = left_ref[...]
        first = mm(table, jnp.concatenate([pixels, pixels], axis=0))
        found = []
        for i in range(pair):
            s = slice(i * PATCH, (i + 1) * PATCH)
            level = jnp.sum(first[0:1, s], axis=1, keepdims=True) * (1.0 / PATCH)
            top = jnp.where(eight == 0, first[0:8, s] - level, first[0:8, s])
            body = jnp.concatenate([top, first[8:PATCH, s]], axis=0)
            halves = jnp.concatenate([body, first[PATCH:, s]], axis=1).astype(bf16)
            both = mm(halves, right_ref[...])
            real, imag = both[:, :PATCH], both[:, PATCH:]
            energy = real * real + imag * imag
            middle = slice(PATCH // 2, PATCH // 2 + 1)
            node = first_node + i
            stats[kind, 0, node : node + 1] = jnp.sum(energy, axis=0, keepdims=True)
            stats[kind, 1, node : node + 1] = energy[middle]
            stats[kind, 2, node : node + 1] = real[middle]
            found.append((real, imag))
        return found

    def cross(a, b):
        real = a[0] * b[0] + a[1] * b[1]
        imag = a[1] * b[0] - a[0] * b[1]
        return jnp.concatenate([real, imag], axis=1).astype(bf16)

    for q in range(chunks):
        for i, (real, imag) in enumerate(spectra(own_raw[q], 0, q * pair)):
            own_re[q * pair + i] = real
            own_im[q * pair + i] = imag

    def arrived(way, chunk):
        buffer = (next_raw if way else prev_raw).at[chunk]
        pltpu.make_async_copy(buffer, buffer, bulk_recv.at[way, chunk]).wait()

    def own(node):
        return own_re[node], own_im[node]

    up_ok = (sub_row > 0).astype(f32)
    down_ok = (sub_row < per_section - 1).astype(f32)
    left_ok = jnp.logical_and(lane > 0, lane < grid_cols).astype(f32)
    right_ok = (lane < grid_cols - 1).astype(f32)
    count = up_ok + down_ok + left_ok + right_ok

    def relax(flow, mask):
        weight = anchor_weight * mask
        pull = weight * flow
        scale = 1.0 / (weight + count)
        d = flow * mask
        for _ in range(SWEEPS):
            near = (
                up_ok * pltpu.roll(d, 1, 0)
                + down_ok * pltpu.roll(d, 2 * per_section - 1, 0)
                + left_ok * pltpu.roll(d, 1, 1)
                + right_ok * pltpu.roll(d, LANES - 1, 1)
            )
            d = (pull + near) * scale
        return jnp.where(lane < grid_cols, d, 0.0)

    node_sub = lax.broadcasted_iota(jnp.int32, (nodes, LANES), 0)
    node_lane = lax.broadcasted_iota(jnp.int32, (nodes, LANES), 1)
    diagonal = node_lane == base + node_sub
    nyquist = node_lane == PATCH // 2
    frequency = jnp.where(node_lane < PATCH // 2, node_lane, node_lane - PATCH).astype(f32)
    frequency = frequency * (1.0 / PATCH)
    corr_row = lax.broadcasted_iota(jnp.int32, (PADDED, PADDED), 0)
    corr_col = lax.broadcasted_iota(jnp.int32, (PADDED, PADDED), 1)
    inside = jnp.logical_and(corr_row < WINDOW, corr_col < WINDOW)
    gather_sub = lax.broadcasted_iota(jnp.int32, (2 * nodes, nodes * PADDED), 0)
    gather_lane = lax.broadcasted_iota(jnp.int32, (2 * nodes, nodes * PADDED), 1)
    middle = slice(PATCH // 2, PATCH // 2 + 1)

    def column(d, which):
        line = jnp.sum(jnp.where(sub == row + which * per_section, d, 0.0), axis=0, keepdims=True)
        return jnp.sum(jnp.where(diagonal, line, 0.0), axis=1, keepdims=True)

    def flows(section, crosses, kind_a, kind_b, d):
        row_offset = offsets[0, section]
        col_offset = offsets[1, section]
        turned = []
        for which in range(2):
            cosine, sine = turn(frequency * column(d, which))
            turned.append((cosine, jnp.where(nyquist, 0.0, sine), cosine[:, middle], sine[:, middle]))
        (cos_y, sin_y, end_cy, end_sy), (cos_x, sin_x, end_cx, end_sx) = turned
        total_a = jnp.sum(stats[kind_a, 0], axis=1, keepdims=True)
        edge_col = stats[kind_b, 0]
        total_b = jnp.sum(edge_col, axis=1, keepdims=True)
        edge_row = jnp.sum(stats[kind_b, 1], axis=1, keepdims=True)
        tip_a = stats[kind_a, 2][:, middle]
        tip_b = stats[kind_b, 2][:, middle]
        tip = tip_b * tip_b
        end_both = end_cy * end_cx - end_sy * end_sx
        lost = (
            (edge_row - tip) * (end_sy * end_sy)
            + (edge_col[:, middle] - tip) * (end_sx * end_sx)
            + tip * (1.0 - end_both * end_both)
        )
        size = 1.0 / float(PATCH) ** 4
        variance_a = total_a * size + 1e-05
        variance_b = jnp.maximum((total_b - lost) * size, 0.0) + 1e-05
        scales = (sharpness * size) * lax.rsqrt(variance_a * variance_b)
        corners = end_sy * end_sx * tip_a * tip_b
        row_cos = window[0, pl.ds(row_offset + REACH, PADDED), :]
        row_sin = window[1, pl.ds(row_offset + REACH, PADDED), :]
        col_cos = window[0, pl.ds(col_offset + REACH, PADDED), :]
        col_sin = window[1, pl.ds(col_offset + REACH, PADDED), :]
        col_high, col_low = split(jnp.concatenate([col_cos, -col_sin], axis=1))
        moved = []
        for i in range(nodes):
            c, s = cos_y[i : i + 1], sin_y[i : i + 1]
            table = jnp.concatenate(
                [row_cos * c + row_sin * s, row_sin * c - row_cos * s], axis=0
            )
            parts = mm(jnp.concatenate(split(table), axis=0), crosses[i])
            parts = parts[: 2 * PADDED] + parts[2 * PADDED :]
            real = parts[:PADDED, :PATCH] - parts[PADDED:, PATCH:]
            imag = parts[:PADDED, PATCH:] + parts[PADDED:, :PATCH]
            c, s = cos_x[i : i + 1], sin_x[i : i + 1]
            moved.append(
                jnp.concatenate([real * c + imag * s, imag * c - real * s], axis=1)
            )
        high, low = split(jnp.concatenate(moved, axis=0))
        correlation = mm_nt(
            jnp.concatenate([high, low, high], axis=1),
            jnp.concatenate([col_high, col_high, col_low], axis=1),
        )
        odd = (corr_row + corr_col + (row_offset + col_offset + 2 * REACH)) & 1
        parity = 1.0 - 2.0 * odd.astype(f32)
        weights = []
        for i in range(nodes):
            here = correlation[i * PADDED : (i + 1) * PADDED] - corners[i : i + 1] * parity
            weights.append(jnp.where(inside, jnp.exp(here * scales[i : i + 1]), 0.0))
        high, low = split(jnp.concatenate(weights, axis=0))
        shifts = (lax.rem(gather_lane, PADDED) - HALF + row_offset).astype(f32)
        gather = jnp.where(gather_sub < nodes, 1.0, shifts)
        block = gather_lane // PADDED == lax.rem(gather_sub, nodes)
        gather = jnp.where(block, gather, 0.0).astype(bf16)
        sums = mm(
            jnp.concatenate([gather, gather], axis=1), jnp.concatenate([high, low], axis=0)
        )
        plain = sums[:nodes]
        across = lax.broadcasted_iota(jnp.int32, (nodes, PADDED), 1) - HALF + col_offset
        inverse = 1.0 / jnp.sum(plain, axis=1, keepdims=True)
        flow_row = jnp.sum(sums[nodes:], axis=1, keepdims=True) * inverse
        flow_col = jnp.sum(plain * across.astype(f32), axis=1, keepdims=True) * inverse
        line_row = jnp.sum(jnp.where(diagonal, flow_row, 0.0), axis=0, keepdims=True)
        line_col = jnp.sum(jnp.where(diagonal, flow_col, 0.0), axis=0, keepdims=True)
        tile = jnp.where(sub == row, line_row, 0.0)
        return jnp.where(sub == row + per_section, line_col, tile)

    def flow_copy(phase, ahead, step):
        part = 1 - phase
        slot = 1 - ahead
        return pltpu.make_async_remote_copy(
            src_ref=flow_tile.at[phase],
            dst_ref=flow_slots.at[slot, part, row],
            send_sem=flow_send.at[phase, ahead, step],
            recv_sem=flow_recv.at[slot, part, row],
            device_id={"tile": device(group + phase + ahead, mate(step))},
            device_id_type=MESH,
        )

    def each_flow(phase, act):
        for step in range(1 - phase, per_section):
            act(flow_copy(phase, 0, step))

        @pl.when(group + phase + 1 < SECTIONS)
        def _():
            for step in range(per_section):
                act(flow_copy(phase, 1, step))

    def take(slots, sems, slot, part, line):
        buffer = slots.at[slot, part, line]
        pltpu.make_async_copy(buffer, buffer, sems.at[slot, part, line]).wait()

    def gathered(slot):
        flow = jnp.zeros(shape, f32)
        mask = jnp.zeros(shape, f32)
        for part in range(2):
            for step in range(1 if slot == 1 and part == 1 else 0, per_section):
                take(flow_slots, flow_recv, slot, part, mate(step))
            for line in range(per_section):
                flow = flow + flow_slots[slot, part, line]
        for line in range(per_section):
            mask = mask + mask_slots[slot, line]
        return relax(flow, mask)

    @pl.when(group >= 1)
    def _():
        for q in range(chunks):
            arrived(0, q)
            if q == 0:

                @pl.when(group == SECTIONS - 1)
                def _():
                    start_bulk(0)

            for i, found in enumerate(spectra(prev_raw[q], 1, q * pair)):
                down_cross[q * pair + i] = cross(own(q * pair + i), found)
        end_bulk(0)

        @pl.when(group == 2)
        def _():
            start_bulk(1)

        for step in range(per_section):
            pltpu.make_async_copy(
                mask_slots.at[0, mate(step)], mask_slots.at[0, mate(step)], mask_recv.at[0, mate(step)]
            ).wait()

        @pl.when(group >= 2)
        def _():
            shift_ref[0] = gathered(0)

        tile = flows(group, down_cross, 0, 1, shift_ref[0])
        flow_tile[0] = tile
        flow_slots[1, 1, row] = tile
        each_flow(0, lambda copy: copy.start())

    @pl.when(group < SECTIONS - 1)
    def _():
        for q in range(chunks):
            arrived(1, q)
            for i, found in enumerate(spectra(next_raw[q], 2, q * pair)):
                up_cross[q * pair + i] = cross(found, own(q * pair + i))

    for step in range(1, per_section):
        pltpu.make_async_copy(
            mask_slots.at[1, mate(step)], mask_slots.at[1, mate(step)], mask_recv.at[1, mate(step)]
        ).wait()

    @pl.when(group >= 1)
    def _():
        shift_ref[1] = gathered(1)

    @pl.when(group < SECTIONS - 1)
    def _():
        flow_tile[1] = flows(group + 1, up_cross, 2, 0, shift_ref[1])
        each_flow(1, lambda copy: copy.start())

    home = shift_ref[1]
    out_row = jnp.sum(jnp.where(sub == row, home, 0.0), axis=0, keepdims=True)
    out_col = jnp.sum(jnp.where(sub == row + per_section, home, 0.0), axis=0, keepdims=True)
    out_ref[...] = jnp.concatenate([out_row, out_col], axis=0)

    for step in range(1, per_section):
        mask_copy(0, step).wait_send()

    @pl.when(group < SECTIONS - 1)
    def _():
        for step in range(per_section):
            mask_copy(1, step).wait_send()
        end_bulk(1)
        each_flow(1, lambda copy: copy.wait_send())

    @pl.when(group >= 1)
    def _():
        each_flow(0, lambda copy: copy.wait_send())


def warp_kernel(
    shift_ref, strip_in, warp_tables, parity_ref, out, node_ref, strip, result, sems
):
    pieces = strip.shape[0]
    width = strip.shape[2]
    loads, stores = [], []
    for k in range(pieces):
        where = pl.ds(k * width, width)
        loads.append(pltpu.make_async_copy(strip_in.at[:, where], strip.at[k], sems.at[k]))
        stores.append(
            pltpu.make_async_copy(result.at[k], out.at[:, where], sems.at[pieces + k])
        )
        loads[k].start()
    nodes = node_ref.shape[2]
    node_ref[0] = shift_ref[0:1, 0:nodes]
    node_ref[1] = shift_ref[1:2, 0:nodes]
    rows = kernel_rows(term_rows(shift_ref[0:1, :], shift_ref[1:2, :]), warp_tables[...])
    parity = parity_ref[...]
    for k in range(pieces):
        loads[k].wait()
        for j, s in enumerate(patch_slices(width)):
            i = k * (width // PATCH) + j
            patch = strip[k, :, s]
            checker = total(patch.astype(f32) * parity)
            result[k, :, s] = warp_patch(patch, rows, i, checker, parity).astype(bf16)
        stores[k].start()
    for copy in stores:
        copy.wait()


def shards(tile_count, sections, valid_mask, coarse_offsets):
    per_section = tile_count // SECTIONS
    grid_cols = valid_mask.shape[1]
    width = CHUNK * PATCH
    chunks = sections.shape[1] // (2 * width)
    nodes = chunks * CHUNK
    tile_shape = (2 * per_section, LANES)
    vmem = pl.BlockSpec(memory_space=pltpu.VMEM)
    left, right, window, warp_tables, parity = constants()
    hbm = pl.BlockSpec(memory_space=pltpu.HBM)
    raw = pltpu.VMEM((chunks, PATCH, width), bf16)
    spectrum = pltpu.VMEM((nodes, PATCH, PATCH), f32)
    crossed = pltpu.VMEM((nodes, PATCH, 2 * PATCH), bf16)
    dma = pltpu.SemaphoreType.DMA
    shift = pl.pallas_call(
        functools.partial(chain_kernel, tile_count, grid_cols),
        out_shape=jax.ShapeDtypeStruct((2, LANES), f32),
        in_specs=[hbm] * 6,
        out_specs=vmem,
        scratch_shapes=[
            pltpu.VMEM(left.shape, bf16),
            pltpu.VMEM(right.shape, bf16),
            pltpu.VMEM(window.shape, f32),
            pltpu.SMEM(coarse_offsets.shape[::-1], jnp.int32),
            pltpu.VMEM(valid_mask.shape, jnp.int32),
            dma((5 + chunks,)),
            raw,
            raw,
            raw,
            spectrum,
            spectrum,
            crossed,
            crossed,
            pltpu.VMEM((3, 3, nodes, LANES), f32),
            pltpu.VMEM(tile_shape, f32),
            pltpu.VMEM((2, per_section) + tile_shape, f32),
            pltpu.VMEM((2,) + tile_shape, f32),
            pltpu.VMEM((2, 2, per_section) + tile_shape, f32),
            pltpu.VMEM((2,) + tile_shape, f32),
            dma((2, chunks)),
            dma((2, chunks)),
            dma((2, per_section)),
            dma((2, per_section)),
            dma((2, 2, per_section)),
            dma((2, 2, per_section)),
        ],
        compiler_params=pltpu.CompilerParams(
            collective_id=0, has_side_effects=True
        ),
        name="chain",
    )(coarse_offsets.T, valid_mask, left, right, window, sections)
    return pl.pallas_call(
        warp_kernel,
        out_shape=(
            jax.ShapeDtypeStruct(sections.shape, bf16),
            jax.ShapeDtypeStruct((2, 1, grid_cols), f32),
        ),
        in_specs=[vmem, hbm, vmem, vmem],
        out_specs=(hbm, vmem),
        scratch_shapes=[
            pltpu.VMEM((PIECES, PATCH, sections.shape[1] // PIECES), bf16),
            pltpu.VMEM((PIECES, PATCH, sections.shape[1] // PIECES), bf16),
            pltpu.SemaphoreType.DMA((2 * PIECES,)),
        ],
        name="warp",
    )(shift, sections, warp_tables, parity)


def solution(mesh):
    placed = (P(("parts", "tile"), None), P(("parts", "tile"), None), P("parts", None))
    return jax.shard_map(
        functools.partial(shards, mesh.shape["tile"]),
        mesh=mesh,
        in_specs=placed,
        out_specs=(P(("parts", "tile"), None), P(None, ("parts", "tile"), None)),
        check_vma=False,
    )
```

```python
import functools

import jax
import jax.numpy as jnp
import numpy as np
from jax import lax
from jax.experimental import pallas as pl
from jax.experimental.pallas import tpu as pltpu
from jax.sharding import PartitionSpec as P

SECTIONS = 4
PATCH = 128
HALF = 4
SWEEPS = 3
REACH = 3
WINDOW = 2 * HALF + 1
PADDED = 16
LANES = 128
CHUNK = 2
PACE = 2900
REST = 1500
PIECES = 2

sharpness = 12.0
anchor_weight = 2.0
MESH = pl.DeviceIdType.MESH
f32 = jnp.float32
bf16 = jnp.bfloat16


def split(value):
    high = value.astype(bf16)
    return high, (value - high.astype(f32)).astype(bf16)


def mm(a, b):
    return jnp.dot(a, b, preferred_element_type=f32)


def mm_nt(a, b):
    return lax.dot_general(a, b, (((1,), (1,)), ((), ())), preferred_element_type=f32)


def constants():
    n = PATCH
    k = np.arange(n)
    angle = 2 * np.pi * ((k[:, None] * k[None, :]) % n) / n
    cosine, sine = np.cos(angle), np.sin(angle)
    left = []
    for table in (cosine, sine):
        high = np.asarray(table, bf16)
        low = np.asarray(table - high.astype(np.float64), bf16)
        left.append(np.concatenate([high, low], axis=1))
    left = np.concatenate(left, axis=0)
    right = np.block([[cosine, -sine], [-sine, -cosine]])
    right = np.asarray(right, bf16)
    u = np.arange(-HALF - REACH, -HALF - REACH + 24)
    window_angle = 2 * np.pi * ((u[:, None] * k[None, :]) % n) / n
    window = np.stack([np.cos(window_angle), np.sin(window_angle)])
    window = window.astype(np.float32)
    half_angle = np.pi * k / n
    sign = 1.0 - 2.0 * (k % 2)
    warp = np.zeros((8, n), np.float32)
    warp[:4] = np.stack([np.sin(half_angle), np.cos(half_angle), sign, k])
    parity = (sign[:, None] * sign[None, :]).astype(np.float32)
    return left, right, window, warp, parity


def turn(value):
    small = (value - jnp.round(value)) * np.pi
    square = small * small
    sine = small * (1.0 + square * (-1 / 6 + square * (1 / 120 + square * (
        -1 / 5040 + square * (1 / 362880 - square * (1 / 39916800))))))
    cosine = 1.0 + square * (-1 / 2 + square * (1 / 24 + square * (-1 / 720 + square * (
        1 / 40320 + square * (-1 / 3628800 + square * (1 / 479001600))))))
    return 1.0 - 2.0 * (sine * sine), 2.0 * (sine * cosine)


def shift_terms(d):
    whole = jnp.round(d)
    frac = d - whole
    odd = jnp.abs(whole - 2.0 * jnp.round(whole * 0.5))
    sine = jnp.sin(jnp.pi * frac)
    signed = jnp.where(odd > 0.5, -sine, sine) * (1.0 / PATCH)
    angle = d * (np.pi / PATCH)
    tangent = jnp.sin(angle) / jnp.cos(angle)
    small = frac * (np.pi / PATCH)
    tiny = jnp.abs(frac) < 1e-6
    peak = jnp.where(
        tiny, 1.0, sine * jnp.cos(small) / jnp.where(tiny, 1.0, PATCH * jnp.sin(small))
    )
    return tangent, signed, peak, whole


def kernel_rows(terms, tables):
    columns = jnp.transpose(terms)[:LANES]
    sine, cosine, parity, gap = [tables[i : i + 1, :] for i in range(4)]
    found = []
    for base, forward in ((0, False), (4, True)):
        tangent, signed, peak, whole = [columns[:, base + i : base + i + 1] for i in range(4)]
        if forward:
            bottom = cosine * tangent + sine
            top = cosine - sine * tangent
            centre = jnp.where(whole > 0, PATCH - whole, -whole)
        else:
            bottom = cosine * tangent - sine
            top = cosine + sine * tangent
            centre = jnp.where(whole < 0, whole + PATCH, whole)
        found.append(jnp.where(gap == centre, peak, (signed * parity) * (top / bottom)))
    corner = columns[:, 1:2] * columns[:, 5:6]
    return found[0], found[1], corner


def circulant(row):
    spread = jnp.broadcast_to(row, (PATCH, PATCH))
    return split(pltpu.roll(spread, 0, 1, stride=1, stride_axis=0))


def warp_patch(patch, rows, i, checker, parity):
    left = circulant(rows[0][i : i + 1, :])
    right = circulant(rows[1][i : i + 1, :])
    both = mm(patch, jnp.concatenate(right, axis=1))
    high, low = split(both[:, :PATCH] + both[:, PATCH:])
    lower = jnp.concatenate([high, jnp.zeros_like(low)], axis=1)
    inner = jnp.concatenate([jnp.concatenate([high, low], axis=1), lower], axis=0)
    moved = mm(jnp.concatenate(left, axis=1), inner)
    corner = (rows[2][i : i + 1, :] * checker) * parity
    return (moved[:, :PATCH] + moved[:, PATCH:]) - corner


def total(value):
    return jnp.sum(jnp.sum(value, axis=0, keepdims=True), axis=1, keepdims=True)


def term_rows(d_rows, d_cols):
    both = jnp.concatenate([d_rows, d_cols], axis=0)
    tangent, signed, peak, whole = shift_terms(both)
    pieces = [t[i : i + 1] for i in range(2) for t in (tangent, signed, peak, whole)]
    return jnp.concatenate(pieces, axis=0)


def patch_slices(width):
    return [slice(i * PATCH, (i + 1) * PATCH) for i in range(width // PATCH)]


def chain_kernel(
    tile_count,
    grid_cols,
    offsets_in,
    mask_in,
    left_in,
    right_in,
    window_in,
    strip,
    out_ref,
    left_ref,
    right_ref,
    window,
    offsets,
    mask_ref,
    load_sem,
    own_raw,
    prev_raw,
    next_raw,
    own_re,
    own_im,
    down_cross,
    up_cross,
    stats,
    mask_tile,
    mask_slots,
    flow_tile,
    flow_slots,
    shift_ref,
    bulk_send,
    bulk_recv,
    mask_send,
    mask_recv,
    flow_send,
    flow_recv,
    go_sem,
    relay_raw,
    relay_send,
    relay_recv,
):
    per_section = tile_count // SECTIONS
    me = lax.axis_index("tile")
    lead = per_section // 2
    rotated = lax.rem(me + tile_count - lead, tile_count)
    group = rotated // per_section
    row = lax.rem(rotated, per_section)
    chunks, width = own_raw.shape[0], own_raw.shape[2]
    pair = width // PATCH
    nodes = chunks * pair
    half = lax.rem(group, 2)
    base = half * nodes

    def device(section, line):
        return lax.rem(section * per_section + line + lead, tile_count)

    def mate(line_step):
        return lax.rem(row + line_step, per_section)

    barrier = pltpu.get_barrier_semaphore()
    for step in range(1, tile_count):
        peer = lax.rem(me + step, tile_count)
        pl.semaphore_signal(barrier, inc=1, device_id={"tile": peer}, device_id_type=MESH)

    def columns(side, chunk):
        start = pl.multiple_of((side * chunks + chunk) * width, LANES)
        return strip.at[:, pl.ds(start, width)]

    loads = [
        pltpu.make_async_copy(source, target, load_sem.at[i])
        for i, (source, target) in enumerate(
            [(mask_in, mask_ref), (offsets_in, offsets), (window_in, window)]
            + [(left_in, left_ref), (right_in, right_ref)]
            + [(columns(half, q), own_raw.at[q]) for q in range(chunks)]
        )
    ]
    for copy in loads:
        copy.start()
    loads[0].wait()
    shape = (2 * per_section, LANES)
    sub = lax.broadcasted_iota(jnp.int32, shape, 0)
    lane = lax.broadcasted_iota(jnp.int32, shape, 1)
    sub_row = lax.rem(sub, per_section)
    mask_tile[...] = jnp.zeros(shape, f32)
    mask_tile[0:1, 0:grid_cols] = mask_ref[...].astype(f32)
    mask_row = mask_tile[0:1, :]
    mask_tile[...] = jnp.where(sub_row == row, mask_row, 0.0)
    mask_slots[1, row] = mask_tile[...]
    shift_ref[...] = jnp.zeros((2,) + shape, f32)

    pl.semaphore_wait(barrier, tile_count - 1)

    def bulk(way, chunk):
        peer = lax.rem(me + (per_section if way else tile_count - per_section), tile_count)
        return pltpu.make_async_remote_copy(
            src_ref=columns(1 - half, chunk),
            dst_ref=(prev_raw if way else next_raw).at[chunk],
            send_sem=bulk_send.at[way, chunk],
            recv_sem=bulk_recv.at[1 - way, chunk],
            device_id={"tile": peer},
            device_id_type=MESH,
        )

    def start_bulk(way, first=0, last=chunks):
        for chunk in range(first, last):
            bulk(way, chunk).start()

    straight = chunks // 2
    apart = per_section - per_section // 2
    wrapped = row >= apart

    def detour(way):
        for k in range(chunks - straight):
            pltpu.make_async_remote_copy(
                src_ref=columns(1 - half, straight + k),
                dst_ref=relay_raw.at[k],
                send_sem=bulk_send.at[way, straight + k],
                recv_sem=relay_recv.at[k],
                device_id={"tile": device(SECTIONS - 1 if way else 0, row - apart)},
                device_id_type=MESH,
            ).start()

    def onward(way, k):
        return pltpu.make_async_remote_copy(
            src_ref=relay_raw.at[k],
            dst_ref=(prev_raw if way else next_raw).at[straight + k],
            send_sem=relay_send.at[k],
            recv_sem=bulk_recv.at[1 - way, straight + k],
            device_id={"tile": device(SECTIONS - 1 if way else 2, row + apart)},
            device_id_type=MESH,
        )

    def forward(way, k):
        pltpu.make_async_copy(relay_raw.at[k], relay_raw.at[k], relay_recv.at[k]).wait()
        onward(way, k).start()

    def release():
        pl.semaphore_signal(
            go_sem,
            inc=1,
            device_id={"tile": device(SECTIONS - 1, row)},
            device_id_type=MESH,
        )

    def end_bulk(way):
        for chunk in range(chunks):
            bulk(way, chunk).wait_send()

    @pl.when(jnp.logical_or(group == 1, group == 2))
    def _():
        start_bulk(0)

    @pl.when(group <= 1)
    def _():
        start_bulk(1)

    for way in range(2):
        mine = group == SECTIONS - 1 - way

        @pl.when(jnp.logical_and(mine, wrapped))
        def _():
            detour(way)

        @pl.when(jnp.logical_and(mine, jnp.logical_not(wrapped)))
        def _():
            start_bulk(way)

    def mask_copy(ahead, step):
        return pltpu.make_async_remote_copy(
            src_ref=mask_tile,
            dst_ref=mask_slots.at[1 - ahead, row],
            send_sem=mask_send.at[ahead, step],
            recv_sem=mask_recv.at[1 - ahead, row],
            device_id={"tile": device(group + ahead, mate(step))},
            device_id_type=MESH,
        )

    for step in range(1, per_section):
        mask_copy(0, step).start()

    @pl.when(group < SECTIONS - 1)
    def _():
        for step in range(per_section):
            mask_copy(1, step).start()

    for copy in loads[1:]:
        copy.wait()

    eight = lax.broadcasted_iota(jnp.int32, (8, LANES), 0)

    def spectra(pixels, kind, first_node):
        table = left_ref[...]
        first = mm(table, jnp.concatenate([pixels, pixels], axis=0))
        found = []
        for i in range(pair):
            s = slice(i * PATCH, (i + 1) * PATCH)
            level = jnp.sum(first[0:1, s], axis=1, keepdims=True) * (1.0 / PATCH)
            top = jnp.where(eight == 0, first[0:8, s] - level, first[0:8, s])
            body = jnp.concatenate([top, first[8:PATCH, s]], axis=0)
            halves = jnp.concatenate([body, first[PATCH:, s]], axis=1).astype(bf16)
            both = mm(halves, right_ref[...])
            real, imag = both[:, :PATCH], both[:, PATCH:]
            energy = real * real + imag * imag
            middle = slice(PATCH // 2, PATCH // 2 + 1)
            node = first_node + i
            stats[kind, 0, node : node + 1] = jnp.sum(energy, axis=0, keepdims=True)
            stats[kind, 1, node : node + 1] = energy[middle]
            stats[kind, 2, node : node + 1] = real[middle]
            found.append((real, imag))
        return found

    def cross(a, b):
        real = a[0] * b[0] + a[1] * b[1]
        imag = a[1] * b[0] - a[0] * b[1]
        return jnp.concatenate([real, imag], axis=1).astype(bf16)

    for q in range(chunks):
        for i, (real, imag) in enumerate(spectra(own_raw[q], 0, q * pair)):
            own_re[q * pair + i] = real
            own_im[q * pair + i] = imag

    def arrived(way, chunk):
        buffer = (next_raw if way else prev_raw).at[chunk]
        pltpu.make_async_copy(buffer, buffer, bulk_recv.at[way, chunk]).wait()

    def own(node):
        return own_re[node], own_im[node]

    up_ok = (sub_row > 0).astype(f32)
    down_ok = (sub_row < per_section - 1).astype(f32)
    left_ok = jnp.logical_and(lane > 0, lane < grid_cols).astype(f32)
    right_ok = (lane < grid_cols - 1).astype(f32)
    count = up_ok + down_ok + left_ok + right_ok

    def relax(flow, mask):
        weight = anchor_weight * mask
        pull = weight * flow
        scale = 1.0 / (weight + count)
        d = flow * mask
        for _ in range(SWEEPS):
            near = (
                up_ok * pltpu.roll(d, 1, 0)
                + down_ok * pltpu.roll(d, 2 * per_section - 1, 0)
                + left_ok * pltpu.roll(d, 1, 1)
                + right_ok * pltpu.roll(d, LANES - 1, 1)
            )
            d = (pull + near) * scale
        return jnp.where(lane < grid_cols, d, 0.0)

    node_sub = lax.broadcasted_iota(jnp.int32, (nodes, LANES), 0)
    node_lane = lax.broadcasted_iota(jnp.int32, (nodes, LANES), 1)
    diagonal = node_lane == base + node_sub
    nyquist = node_lane == PATCH // 2
    frequency = jnp.where(node_lane < PATCH // 2, node_lane, node_lane - PATCH).astype(f32)
    frequency = frequency * (1.0 / PATCH)
    corr_row = lax.broadcasted_iota(jnp.int32, (PADDED, PADDED), 0)
    corr_col = lax.broadcasted_iota(jnp.int32, (PADDED, PADDED), 1)
    inside = jnp.logical_and(corr_row < WINDOW, corr_col < WINDOW)
    gather_sub = lax.broadcasted_iota(jnp.int32, (2 * nodes, nodes * PADDED), 0)
    gather_lane = lax.broadcasted_iota(jnp.int32, (2 * nodes, nodes * PADDED), 1)
    middle = slice(PATCH // 2, PATCH // 2 + 1)

    def column(d, which):
        line = jnp.sum(jnp.where(sub == row + which * per_section, d, 0.0), axis=0, keepdims=True)
        return jnp.sum(jnp.where(diagonal, line, 0.0), axis=1, keepdims=True)

    def flows(section, crosses, kind_a, kind_b, d):
        row_offset = offsets[0, section]
        col_offset = offsets[1, section]
        turned = []
        for which in range(2):
            cosine, sine = turn(frequency * column(d, which))
            turned.append((cosine, jnp.where(nyquist, 0.0, sine), cosine[:, middle], sine[:, middle]))
        (cos_y, sin_y, end_cy, end_sy), (cos_x, sin_x, end_cx, end_sx) = turned
        total_a = jnp.sum(stats[kind_a, 0], axis=1, keepdims=True)
        edge_col = stats[kind_b, 0]
        total_b = jnp.sum(edge_col, axis=1, keepdims=True)
        edge_row = jnp.sum(stats[kind_b, 1], axis=1, keepdims=True)
        tip_a = stats[kind_a, 2][:, middle]
        tip_b = stats[kind_b, 2][:, middle]
        tip = tip_b * tip_b
        end_both = end_cy * end_cx - end_sy * end_sx
        lost = (
            (edge_row - tip) * (end_sy * end_sy)
            + (edge_col[:, middle] - tip) * (end_sx * end_sx)
            + tip * (1.0 - end_both * end_both)
        )
        size = 1.0 / float(PATCH) ** 4
        variance_a = total_a * size + 1e-05
        variance_b = jnp.maximum((total_b - lost) * size, 0.0) + 1e-05
        scales = (sharpness * size) * lax.rsqrt(variance_a * variance_b)
        corners = end_sy * end_sx * tip_a * tip_b
        row_cos = window[0, pl.ds(row_offset + REACH, PADDED), :]
        row_sin = window[1, pl.ds(row_offset + REACH, PADDED), :]
        col_cos = window[0, pl.ds(col_offset + REACH, PADDED), :]
        col_sin = window[1, pl.ds(col_offset + REACH, PADDED), :]
        col_high, col_low = split(jnp.concatenate([col_cos, -col_sin], axis=1))
        moved = []
        for i in range(nodes):
            c, s = cos_y[i : i + 1], sin_y[i : i + 1]
            table = jnp.concatenate(
                [row_cos * c + row_sin * s, row_sin * c - row_cos * s], axis=0
            )
            parts = mm(jnp.concatenate(split(table), axis=0), crosses[i])
            parts = parts[: 2 * PADDED] + parts[2 * PADDED :]
            real = parts[:PADDED, :PATCH] - parts[PADDED:, PATCH:]
            imag = parts[:PADDED, PATCH:] + parts[PADDED:, :PATCH]
            c, s = cos_x[i : i + 1], sin_x[i : i + 1]
            moved.append(
                jnp.concatenate([real * c + imag * s, imag * c - real * s], axis=1)
            )
        high, low = split(jnp.concatenate(moved, axis=0))
        correlation = mm_nt(
            jnp.concatenate([high, low, high], axis=1),
            jnp.concatenate([col_high, col_high, col_low], axis=1),
        )
        odd = (corr_row + corr_col + (row_offset + col_offset + 2 * REACH)) & 1
        parity = 1.0 - 2.0 * odd.astype(f32)
        weights = []
        for i in range(nodes):
            here = correlation[i * PADDED : (i + 1) * PADDED] - corners[i : i + 1] * parity
            weights.append(jnp.where(inside, jnp.exp(here * scales[i : i + 1]), 0.0))
        high, low = split(jnp.concatenate(weights, axis=0))
        shifts = (lax.rem(gather_lane, PADDED) - HALF + row_offset).astype(f32)
        gather = jnp.where(gather_sub < nodes, 1.0, shifts)
        block = gather_lane // PADDED == lax.rem(gather_sub, nodes)
        gather = jnp.where(block, gather, 0.0).astype(bf16)
        sums = mm(
            jnp.concatenate([gather, gather], axis=1), jnp.concatenate([high, low], axis=0)
        )
        plain = sums[:nodes]
        across = lax.broadcasted_iota(jnp.int32, (nodes, PADDED), 1) - HALF + col_offset
        inverse = 1.0 / jnp.sum(plain, axis=1, keepdims=True)
        flow_row = jnp.sum(sums[nodes:], axis=1, keepdims=True) * inverse
        flow_col = jnp.sum(plain * across.astype(f32), axis=1, keepdims=True) * inverse
        line_row = jnp.sum(jnp.where(diagonal, flow_row, 0.0), axis=0, keepdims=True)
        line_col = jnp.sum(jnp.where(diagonal, flow_col, 0.0), axis=0, keepdims=True)
        tile = jnp.where(sub == row, line_row, 0.0)
        return jnp.where(sub == row + per_section, line_col, tile)

    def flow_copy(phase, ahead, step):
        part = 1 - phase
        slot = 1 - ahead
        return pltpu.make_async_remote_copy(
            src_ref=flow_tile.at[phase],
            dst_ref=flow_slots.at[slot, part, row],
            send_sem=flow_send.at[phase, ahead, step],
            recv_sem=flow_recv.at[slot, part, row],
            device_id={"tile": device(group + phase + ahead, mate(step))},
            device_id_type=MESH,
        )

    def each_flow(phase, act):
        for step in range(1 - phase, per_section):
            act(flow_copy(phase, 0, step))

        @pl.when(group + phase + 1 < SECTIONS)
        def _():
            for step in range(per_section):
                act(flow_copy(phase, 1, step))

    def take(slots, sems, slot, part, line):
        buffer = slots.at[slot, part, line]
        pltpu.make_async_copy(buffer, buffer, sems.at[slot, part, line]).wait()

    def gathered(slot):
        flow = jnp.zeros(shape, f32)
        mask = jnp.zeros(shape, f32)
        for part in range(2):
            for step in range(1 if slot == 1 and part == 1 else 0, per_section):
                take(flow_slots, flow_recv, slot, part, mate(step))
            for line in range(per_section):
                flow = flow + flow_slots[slot, part, line]
        for line in range(per_section):
            mask = mask + mask_slots[slot, line]
        return relax(flow, mask)

    @pl.when(group == SECTIONS - 1)
    def _():
        pl.semaphore_wait(go_sem, 1)

        @pl.when(wrapped)
        def _():
            for chunk in range(straight):
                if chunk:
                    pl.delay(PACE)
                bulk(0, chunk).start()

        @pl.when(jnp.logical_not(wrapped))
        def _():
            for k in range(chunks - straight):
                if k:
                    pl.delay(PACE)
                forward(1, k)

    @pl.when(group >= 1)
    def _():
        for q in range(chunks):
            arrived(0, q)
            for i, found in enumerate(spectra(prev_raw[q], 1, q * pair)):
                down_cross[q * pair + i] = cross(own(q * pair + i), found)

        @pl.when(group == 1)
        def _():
            end_bulk(0)

        @pl.when(group == 2)
        def _():
            end_bulk(0)

        @pl.when(jnp.logical_and(group == 2, wrapped))
        def _():
            for chunk in range(straight):
                if chunk:
                    pl.delay(PACE)
                bulk(1, chunk).start()

        for step in range(per_section):
            pltpu.make_async_copy(
                mask_slots.at[0, mate(step)], mask_slots.at[0, mate(step)], mask_recv.at[0, mate(step)]
            ).wait()

        @pl.when(group >= 2)
        def _():
            shift_ref[0] = gathered(0)

        tile = flows(group, down_cross, 0, 1, shift_ref[0])
        flow_tile[0] = tile
        flow_slots[1, 1, row] = tile
        each_flow(0, lambda copy: copy.start())

    @pl.when(group < SECTIONS - 1)
    def _():
        for q in range(chunks):
            arrived(1, q)
            if q == chunks - 1:

                @pl.when(group == 0)
                def _():
                    release()

                @pl.when(jnp.logical_and(group == 0, jnp.logical_not(wrapped)))
                def _():
                    for k in range(chunks - straight - 1):
                        forward(0, k)

            for i, found in enumerate(spectra(next_raw[q], 2, q * pair)):
                up_cross[q * pair + i] = cross(found, own(q * pair + i))

    for step in range(1, per_section):
        pltpu.make_async_copy(
            mask_slots.at[1, mate(step)], mask_slots.at[1, mate(step)], mask_recv.at[1, mate(step)]
        ).wait()

    @pl.when(group >= 1)
    def _():
        shift_ref[1] = gathered(1)

    @pl.when(group < SECTIONS - 1)
    def _():
        flow_tile[1] = flows(group + 1, up_cross, 2, 0, shift_ref[1])
        each_flow(1, lambda copy: copy.start())

        @pl.when(jnp.logical_and(group == 0, jnp.logical_not(wrapped)))
        def _():
            pl.delay(REST)
            forward(0, chunks - straight - 1)

    home = shift_ref[1]
    out_row = jnp.sum(jnp.where(sub == row, home, 0.0), axis=0, keepdims=True)
    out_col = jnp.sum(jnp.where(sub == row + per_section, home, 0.0), axis=0, keepdims=True)
    out_ref[...] = jnp.concatenate([out_row, out_col], axis=0)

    for step in range(1, per_section):
        mask_copy(0, step).wait_send()

    @pl.when(group < SECTIONS - 1)
    def _():
        for step in range(per_section):
            mask_copy(1, step).wait_send()

        end_bulk(1)
        each_flow(1, lambda copy: copy.wait_send())

    @pl.when(group >= 1)
    def _():
        each_flow(0, lambda copy: copy.wait_send())

    @pl.when(group == SECTIONS - 1)
    def _():
        end_bulk(0)

    for way, section in ((0, 0), (1, SECTIONS - 1)):

        @pl.when(jnp.logical_and(group == section, jnp.logical_not(wrapped)))
        def _():
            for k in range(chunks - straight):
                onward(way, k).wait_send()


def warp_kernel(
    shift_ref, strip_in, warp_tables, parity_ref, out, node_ref, strip, result, sems
):
    pieces = strip.shape[0]
    width = strip.shape[2]
    loads, stores = [], []
    for k in range(pieces):
        where = pl.ds(k * width, width)
        loads.append(pltpu.make_async_copy(strip_in.at[:, where], strip.at[k], sems.at[k]))
        stores.append(
            pltpu.make_async_copy(result.at[k], out.at[:, where], sems.at[pieces + k])
        )
        loads[k].start()
    nodes = node_ref.shape[2]
    node_ref[0] = shift_ref[0:1, 0:nodes]
    node_ref[1] = shift_ref[1:2, 0:nodes]
    rows = kernel_rows(term_rows(shift_ref[0:1, :], shift_ref[1:2, :]), warp_tables[...])
    parity = parity_ref[...]
    for k in range(pieces):
        loads[k].wait()
        for j, s in enumerate(patch_slices(width)):
            i = k * (width // PATCH) + j
            patch = strip[k, :, s]
            checker = total(patch.astype(f32) * parity)
            result[k, :, s] = warp_patch(patch, rows, i, checker, parity).astype(bf16)
        stores[k].start()
    for copy in stores:
        copy.wait()


def shards(tile_count, sections, valid_mask, coarse_offsets):
    per_section = tile_count // SECTIONS
    grid_cols = valid_mask.shape[1]
    width = CHUNK * PATCH
    chunks = sections.shape[1] // (2 * width)
    nodes = chunks * CHUNK
    tile_shape = (2 * per_section, LANES)
    vmem = pl.BlockSpec(memory_space=pltpu.VMEM)
    left, right, window, warp_tables, parity = constants()
    hbm = pl.BlockSpec(memory_space=pltpu.HBM)
    raw = pltpu.VMEM((chunks, PATCH, width), bf16)
    spectrum = pltpu.VMEM((nodes, PATCH, PATCH), f32)
    crossed = pltpu.VMEM((nodes, PATCH, 2 * PATCH), bf16)
    dma = pltpu.SemaphoreType.DMA
    shift = pl.pallas_call(
        functools.partial(chain_kernel, tile_count, grid_cols),
        out_shape=jax.ShapeDtypeStruct((2, LANES), f32),
        in_specs=[hbm] * 6,
        out_specs=vmem,
        scratch_shapes=[
            pltpu.VMEM(left.shape, bf16),
            pltpu.VMEM(right.shape, bf16),
            pltpu.VMEM(window.shape, f32),
            pltpu.SMEM(coarse_offsets.shape[::-1], jnp.int32),
            pltpu.VMEM(valid_mask.shape, jnp.int32),
            dma((5 + chunks,)),
            raw,
            raw,
            raw,
            spectrum,
            spectrum,
            crossed,
            crossed,
            pltpu.VMEM((3, 3, nodes, LANES), f32),
            pltpu.VMEM(tile_shape, f32),
            pltpu.VMEM((2, per_section) + tile_shape, f32),
            pltpu.VMEM((2,) + tile_shape, f32),
            pltpu.VMEM((2, 2, per_section) + tile_shape, f32),
            pltpu.VMEM((2,) + tile_shape, f32),
            dma((2, chunks)),
            dma((2, chunks)),
            dma((2, per_section)),
            dma((2, per_section)),
            dma((2, 2, per_section)),
            dma((2, 2, per_section)),
            pltpu.SemaphoreType.REGULAR,
            pltpu.VMEM((chunks - chunks // 2, PATCH, width), bf16),
            dma((chunks - chunks // 2,)),
            dma((chunks - chunks // 2,)),
        ],
        compiler_params=pltpu.CompilerParams(
            collective_id=0, has_side_effects=True
        ),
        name="chain",
    )(coarse_offsets.T, valid_mask, left, right, window, sections)
    return pl.pallas_call(
        warp_kernel,
        out_shape=(
            jax.ShapeDtypeStruct(sections.shape, bf16),
            jax.ShapeDtypeStruct((2, 1, grid_cols), f32),
        ),
        in_specs=[vmem, hbm, vmem, vmem],
        out_specs=(hbm, vmem),
        scratch_shapes=[
            pltpu.VMEM((PIECES, PATCH, sections.shape[1] // PIECES), bf16),
            pltpu.VMEM((PIECES, PATCH, sections.shape[1] // PIECES), bf16),
            pltpu.SemaphoreType.DMA((2 * PIECES,)),
        ],
        name="warp",
    )(shift, sections, warp_tables, parity)


def solution(mesh):
    placed = (P(("parts", "tile"), None), P(("parts", "tile"), None), P("parts", None))
    return jax.shard_map(
        functools.partial(shards, mesh.shape["tile"]),
        mesh=mesh,
        in_specs=placed,
        out_specs=(P(("parts", "tile"), None), P(None, ("parts", "tile"), None)),
        check_vma=False,
    )
```

```python
import functools

import jax
import jax.numpy as jnp
import numpy as np
from jax import lax
from jax.experimental import pallas as pl
from jax.experimental.pallas import tpu as pltpu
from jax.sharding import PartitionSpec as P

SECTIONS = 4
PATCH = 128
HALF = 4
SWEEPS = 3
REACH = 3
WINDOW = 2 * HALF + 1
PADDED = 16
LANES = 128
CHUNK = 2
HUB = 2
REST = 2500
PIECES = 2

sharpness = 12.0
anchor_weight = 2.0
MESH = pl.DeviceIdType.MESH
f32 = jnp.float32
bf16 = jnp.bfloat16


def split(value):
    high = value.astype(bf16)
    return high, (value - high.astype(f32)).astype(bf16)


def mm(a, b):
    return jnp.dot(a, b, preferred_element_type=f32)


def mm_nt(a, b):
    return lax.dot_general(a, b, (((1,), (1,)), ((), ())), preferred_element_type=f32)


def constants():
    n = PATCH
    k = np.arange(n)
    angle = 2 * np.pi * ((k[:, None] * k[None, :]) % n) / n
    cosine, sine = np.cos(angle), np.sin(angle)
    left = []
    for table in (cosine, sine):
        high = np.asarray(table, bf16)
        low = np.asarray(table - high.astype(np.float64), bf16)
        left.append(np.concatenate([high, low], axis=1))
    left = np.concatenate(left, axis=0)
    right = np.block([[cosine, -sine], [-sine, -cosine]])
    right = np.asarray(right, bf16)
    u = np.arange(-HALF - REACH, -HALF - REACH + 24)
    window_angle = 2 * np.pi * ((u[:, None] * k[None, :]) % n) / n
    window = np.stack([np.cos(window_angle), np.sin(window_angle)])
    window = window.astype(np.float32)
    half_angle = np.pi * k / n
    sign = 1.0 - 2.0 * (k % 2)
    warp = np.zeros((8, n), np.float32)
    warp[:4] = np.stack([np.sin(half_angle), np.cos(half_angle), sign, k])
    parity = (sign[:, None] * sign[None, :]).astype(np.float32)
    return left, right, window, warp, parity


def turn(value):
    small = (value - jnp.round(value)) * np.pi
    square = small * small
    sine = small * (1.0 + square * (-1 / 6 + square * (1 / 120 + square * (
        -1 / 5040 + square * (1 / 362880 - square * (1 / 39916800))))))
    cosine = 1.0 + square * (-1 / 2 + square * (1 / 24 + square * (-1 / 720 + square * (
        1 / 40320 + square * (-1 / 3628800 + square * (1 / 479001600))))))
    return 1.0 - 2.0 * (sine * sine), 2.0 * (sine * cosine)


def shift_terms(d):
    whole = jnp.round(d)
    frac = d - whole
    odd = jnp.abs(whole - 2.0 * jnp.round(whole * 0.5))
    sine = jnp.sin(jnp.pi * frac)
    signed = jnp.where(odd > 0.5, -sine, sine) * (1.0 / PATCH)
    angle = d * (np.pi / PATCH)
    tangent = jnp.sin(angle) / jnp.cos(angle)
    small = frac * (np.pi / PATCH)
    tiny = jnp.abs(frac) < 1e-6
    peak = jnp.where(
        tiny, 1.0, sine * jnp.cos(small) / jnp.where(tiny, 1.0, PATCH * jnp.sin(small))
    )
    return tangent, signed, peak, whole


def kernel_rows(terms, tables):
    columns = jnp.transpose(terms)[:LANES]
    sine, cosine, parity, gap = [tables[i : i + 1, :] for i in range(4)]
    found = []
    for base, forward in ((0, False), (4, True)):
        tangent, signed, peak, whole = [columns[:, base + i : base + i + 1] for i in range(4)]
        if forward:
            bottom = cosine * tangent + sine
            top = cosine - sine * tangent
            centre = jnp.where(whole > 0, PATCH - whole, -whole)
        else:
            bottom = cosine * tangent - sine
            top = cosine + sine * tangent
            centre = jnp.where(whole < 0, whole + PATCH, whole)
        found.append(jnp.where(gap == centre, peak, (signed * parity) * (top / bottom)))
    corner = columns[:, 1:2] * columns[:, 5:6]
    return found[0], found[1], corner


def circulant(row):
    spread = jnp.broadcast_to(row, (PATCH, PATCH))
    return split(pltpu.roll(spread, 0, 1, stride=1, stride_axis=0))


def warp_patch(patch, rows, i, checker, parity):
    left = circulant(rows[0][i : i + 1, :])
    right = circulant(rows[1][i : i + 1, :])
    both = mm(patch, jnp.concatenate(right, axis=1))
    high, low = split(both[:, :PATCH] + both[:, PATCH:])
    lower = jnp.concatenate([high, jnp.zeros_like(low)], axis=1)
    inner = jnp.concatenate([jnp.concatenate([high, low], axis=1), lower], axis=0)
    moved = mm(jnp.concatenate(left, axis=1), inner)
    corner = (rows[2][i : i + 1, :] * checker) * parity
    return (moved[:, :PATCH] + moved[:, PATCH:]) - corner


def total(value):
    return jnp.sum(jnp.sum(value, axis=0, keepdims=True), axis=1, keepdims=True)


def term_rows(d_rows, d_cols):
    both = jnp.concatenate([d_rows, d_cols], axis=0)
    tangent, signed, peak, whole = shift_terms(both)
    pieces = [t[i : i + 1] for i in range(2) for t in (tangent, signed, peak, whole)]
    return jnp.concatenate(pieces, axis=0)


def patch_slices(width):
    return [slice(i * PATCH, (i + 1) * PATCH) for i in range(width // PATCH)]


def chain_kernel(
    tile_count,
    grid_cols,
    offsets_in,
    mask_in,
    left_in,
    right_in,
    window_in,
    strip,
    out_ref,
    left_ref,
    right_ref,
    window,
    offsets,
    mask_ref,
    load_sem,
    own_raw,
    prev_raw,
    next_raw,
    own_re,
    own_im,
    down_cross,
    up_cross,
    stats,
    mask_tile,
    mask_slots,
    flow_tile,
    flow_slots,
    shift_ref,
    bulk_send,
    bulk_recv,
    mask_send,
    mask_recv,
    flow_send,
    flow_recv,
    go_sem,
    all_sem,
    relay_raw,
    relay_send,
    relay_recv,
):
    per_section = tile_count // SECTIONS
    me = lax.axis_index("tile")
    lead = per_section // 2
    rotated = lax.rem(me + tile_count - lead, tile_count)
    group = rotated // per_section
    row = lax.rem(rotated, per_section)
    chunks, width = own_raw.shape[0], own_raw.shape[2]
    pair = width // PATCH
    nodes = chunks * pair
    half = lax.rem(group, 2)
    base = half * nodes

    def device(section, line):
        return lax.rem(section * per_section + line + lead, tile_count)

    def mate(line_step):
        return lax.rem(row + line_step, per_section)

    barrier = pltpu.get_barrier_semaphore()

    def signal(sem, section, line):
        pl.semaphore_signal(
            sem, inc=1, device_id={"tile": device(section, line)}, device_id_type=MESH
        )

    @pl.when(group <= 1)
    def _():
        signal(barrier, 1 - group, row)

    @pl.when(group == HUB)
    def _():
        signal(barrier, SECTIONS - 1, row)
        for step in range(1, per_section):
            signal(barrier, HUB, mate(step))

    @pl.when(group != HUB)
    def _():
        for step in range(per_section):
            signal(barrier, HUB, mate(step))

    def columns(side, chunk):
        start = pl.multiple_of((side * chunks + chunk) * width, LANES)
        return strip.at[:, pl.ds(start, width)]

    loads = [
        pltpu.make_async_copy(source, target, load_sem.at[i])
        for i, (source, target) in enumerate(
            [(mask_in, mask_ref), (offsets_in, offsets), (window_in, window)]
            + [(left_in, left_ref), (right_in, right_ref)]
            + [(columns(half, q), own_raw.at[q]) for q in range(chunks)]
        )
    ]
    for copy in loads:
        copy.start()
    pl.semaphore_wait(barrier, jnp.where(group == HUB, tile_count - 1, 1))

    def bulk(way, chunk):
        peer = lax.rem(me + (per_section if way else tile_count - per_section), tile_count)
        return pltpu.make_async_remote_copy(
            src_ref=columns(1 - half, chunk),
            dst_ref=(prev_raw if way else next_raw).at[chunk],
            send_sem=bulk_send.at[way, chunk],
            recv_sem=bulk_recv.at[1 - way, chunk],
            device_id={"tile": peer},
            device_id_type=MESH,
        )

    def start_bulk(way, first=0, last=chunks):
        for chunk in range(first, last):
            bulk(way, chunk).start()

    relayed = (chunks // 2, chunks // 2)
    apart = per_section - per_section // 2
    wrapped = row >= apart

    def detour(way):
        for k in range(relayed[way]):
            pltpu.make_async_remote_copy(
                src_ref=columns(1 - half, k),
                dst_ref=relay_raw.at[k],
                send_sem=bulk_send.at[way, k],
                recv_sem=relay_recv.at[k],
                device_id={"tile": device(SECTIONS - 1 if way else 0, row - apart)},
                device_id_type=MESH,
            ).start()

    def onward(way, k):
        return pltpu.make_async_remote_copy(
            src_ref=relay_raw.at[k],
            dst_ref=(prev_raw if way else next_raw).at[k],
            send_sem=relay_send.at[k],
            recv_sem=bulk_recv.at[1 - way, k],
            device_id={"tile": device(SECTIONS - 1 if way else 2, row + apart)},
            device_id_type=MESH,
        )

    def forward(way, k):
        pltpu.make_async_copy(relay_raw.at[k], relay_raw.at[k], relay_recv.at[k]).wait()
        onward(way, k).start()

    def release():
        signal(go_sem, SECTIONS - 1, row)

    def end_bulk(way):
        for chunk in range(chunks):
            bulk(way, chunk).wait_send()

    @pl.when(group == HUB)
    def _():
        for section in range(SECTIONS):
            if section != HUB:
                signal(all_sem, section, row)

    @pl.when(jnp.logical_or(group == 1, group == 2))
    def _():
        start_bulk(0)

    @pl.when(group == 0)
    def _():
        start_bulk(1)

    for way in range(2):

        @pl.when(jnp.logical_and(group == SECTIONS - 1 - way, jnp.logical_not(wrapped)))
        def _():
            start_bulk(way)

    def mask_copy(ahead, step):
        return pltpu.make_async_remote_copy(
            src_ref=mask_tile,
            dst_ref=mask_slots.at[1 - ahead, row],
            send_sem=mask_send.at[ahead, step],
            recv_sem=mask_recv.at[1 - ahead, row],
            device_id={"tile": device(group + ahead, mate(step))},
            device_id_type=MESH,
        )

    loads[0].wait()
    shape = (2 * per_section, LANES)
    sub = lax.broadcasted_iota(jnp.int32, shape, 0)
    lane = lax.broadcasted_iota(jnp.int32, shape, 1)
    sub_row = lax.rem(sub, per_section)
    mask_tile[...] = jnp.zeros(shape, f32)
    mask_tile[0:1, 0:grid_cols] = mask_ref[...].astype(f32)
    mask_row = mask_tile[0:1, :]
    mask_tile[...] = jnp.where(sub_row == row, mask_row, 0.0)
    mask_slots[1, row] = mask_tile[...]
    shift_ref[...] = jnp.zeros((2,) + shape, f32)

    for copy in loads[1:]:
        copy.wait()

    eight = lax.broadcasted_iota(jnp.int32, (8, LANES), 0)

    def spectra(pixels, kind, first_node):
        table = left_ref[...]
        first = mm(table, jnp.concatenate([pixels, pixels], axis=0))
        found = []
        for i in range(pair):
            s = slice(i * PATCH, (i + 1) * PATCH)
            level = jnp.sum(first[0:1, s], axis=1, keepdims=True) * (1.0 / PATCH)
            top = jnp.where(eight == 0, first[0:8, s] - level, first[0:8, s])
            body = jnp.concatenate([top, first[8:PATCH, s]], axis=0)
            halves = jnp.concatenate([body, first[PATCH:, s]], axis=1).astype(bf16)
            both = mm(halves, right_ref[...])
            real, imag = both[:, :PATCH], both[:, PATCH:]
            energy = real * real + imag * imag
            middle = slice(PATCH // 2, PATCH // 2 + 1)
            node = first_node + i
            stats[kind, 0, node : node + 1] = jnp.sum(energy, axis=0, keepdims=True)
            stats[kind, 1, node : node + 1] = energy[middle]
            stats[kind, 2, node : node + 1] = real[middle]
            found.append((real, imag))
        return found

    def cross(a, b):
        real = a[0] * b[0] + a[1] * b[1]
        imag = a[1] * b[0] - a[0] * b[1]
        return jnp.concatenate([real, imag], axis=1).astype(bf16)

    for q in range(chunks):
        for i, (real, imag) in enumerate(spectra(own_raw[q], 0, q * pair)):
            own_re[q * pair + i] = real
            own_im[q * pair + i] = imag

    @pl.when(group != HUB)
    def _():
        pl.semaphore_wait(all_sem, 1)

    for step in range(1, per_section):
        mask_copy(0, step).start()

    @pl.when(group < SECTIONS - 1)
    def _():
        for step in range(per_section):
            mask_copy(1, step).start()

    @pl.when(group == 1)
    def _():
        start_bulk(1)

    for way in range(2):

        @pl.when(jnp.logical_and(group == SECTIONS - 1 - way, wrapped))
        def _():
            detour(way)

    def arrived(way, chunk):
        buffer = (next_raw if way else prev_raw).at[chunk]
        pltpu.make_async_copy(buffer, buffer, bulk_recv.at[way, chunk]).wait()

    def own(node):
        return own_re[node], own_im[node]

    up_ok = (sub_row > 0).astype(f32)
    down_ok = (sub_row < per_section - 1).astype(f32)
    left_ok = jnp.logical_and(lane > 0, lane < grid_cols).astype(f32)
    right_ok = (lane < grid_cols - 1).astype(f32)
    count = up_ok + down_ok + left_ok + right_ok

    def relax(flow, mask):
        weight = anchor_weight * mask
        pull = weight * flow
        scale = 1.0 / (weight + count)
        d = flow * mask
        for _ in range(SWEEPS):
            near = (
                up_ok * pltpu.roll(d, 1, 0)
                + down_ok * pltpu.roll(d, 2 * per_section - 1, 0)
                + left_ok * pltpu.roll(d, 1, 1)
                + right_ok * pltpu.roll(d, LANES - 1, 1)
            )
            d = (pull + near) * scale
        return jnp.where(lane < grid_cols, d, 0.0)

    node_sub = lax.broadcasted_iota(jnp.int32, (nodes, LANES), 0)
    node_lane = lax.broadcasted_iota(jnp.int32, (nodes, LANES), 1)
    diagonal = node_lane == base + node_sub
    nyquist = node_lane == PATCH // 2
    frequency = jnp.where(node_lane < PATCH // 2, node_lane, node_lane - PATCH).astype(f32)
    frequency = frequency * (1.0 / PATCH)
    corr_row = lax.broadcasted_iota(jnp.int32, (PADDED, PADDED), 0)
    corr_col = lax.broadcasted_iota(jnp.int32, (PADDED, PADDED), 1)
    inside = jnp.logical_and(corr_row < WINDOW, corr_col < WINDOW)
    gather_sub = lax.broadcasted_iota(jnp.int32, (2 * nodes, nodes * PADDED), 0)
    gather_lane = lax.broadcasted_iota(jnp.int32, (2 * nodes, nodes * PADDED), 1)
    middle = slice(PATCH // 2, PATCH // 2 + 1)

    def column(d, which):
        line = jnp.sum(jnp.where(sub == row + which * per_section, d, 0.0), axis=0, keepdims=True)
        return jnp.sum(jnp.where(diagonal, line, 0.0), axis=1, keepdims=True)

    def flows(section, crosses, kind_a, kind_b, d):
        row_offset = offsets[0, section]
        col_offset = offsets[1, section]
        turned = []
        for which in range(2):
            cosine, sine = turn(frequency * column(d, which))
            turned.append((cosine, jnp.where(nyquist, 0.0, sine), cosine[:, middle], sine[:, middle]))
        (cos_y, sin_y, end_cy, end_sy), (cos_x, sin_x, end_cx, end_sx) = turned
        total_a = jnp.sum(stats[kind_a, 0], axis=1, keepdims=True)
        edge_col = stats[kind_b, 0]
        total_b = jnp.sum(edge_col, axis=1, keepdims=True)
        edge_row = jnp.sum(stats[kind_b, 1], axis=1, keepdims=True)
        tip_a = stats[kind_a, 2][:, middle]
        tip_b = stats[kind_b, 2][:, middle]
        tip = tip_b * tip_b
        end_both = end_cy * end_cx - end_sy * end_sx
        lost = (
            (edge_row - tip) * (end_sy * end_sy)
            + (edge_col[:, middle] - tip) * (end_sx * end_sx)
            + tip * (1.0 - end_both * end_both)
        )
        size = 1.0 / float(PATCH) ** 4
        variance_a = total_a * size + 1e-05
        variance_b = jnp.maximum((total_b - lost) * size, 0.0) + 1e-05
        scales = (sharpness * size) * lax.rsqrt(variance_a * variance_b)
        corners = end_sy * end_sx * tip_a * tip_b
        row_cos = window[0, pl.ds(row_offset + REACH, PADDED), :]
        row_sin = window[1, pl.ds(row_offset + REACH, PADDED), :]
        col_cos = window[0, pl.ds(col_offset + REACH, PADDED), :]
        col_sin = window[1, pl.ds(col_offset + REACH, PADDED), :]
        col_high, col_low = split(jnp.concatenate([col_cos, -col_sin], axis=1))
        moved = []
        for i in range(nodes):
            c, s = cos_y[i : i + 1], sin_y[i : i + 1]
            table = jnp.concatenate(
                [row_cos * c + row_sin * s, row_sin * c - row_cos * s], axis=0
            )
            parts = mm(jnp.concatenate(split(table), axis=0), crosses[i])
            parts = parts[: 2 * PADDED] + parts[2 * PADDED :]
            real = parts[:PADDED, :PATCH] - parts[PADDED:, PATCH:]
            imag = parts[:PADDED, PATCH:] + parts[PADDED:, :PATCH]
            c, s = cos_x[i : i + 1], sin_x[i : i + 1]
            moved.append(
                jnp.concatenate([real * c + imag * s, imag * c - real * s], axis=1)
            )
        high, low = split(jnp.concatenate(moved, axis=0))
        correlation = mm_nt(
            jnp.concatenate([high, low, high], axis=1),
            jnp.concatenate([col_high, col_high, col_low], axis=1),
        )
        odd = (corr_row + corr_col + (row_offset + col_offset + 2 * REACH)) & 1
        parity = 1.0 - 2.0 * odd.astype(f32)
        weights = []
        for i in range(nodes):
            here = correlation[i * PADDED : (i + 1) * PADDED] - corners[i : i + 1] * parity
            weights.append(jnp.where(inside, jnp.exp(here * scales[i : i + 1]), 0.0))
        high, low = split(jnp.concatenate(weights, axis=0))
        shifts = (lax.rem(gather_lane, PADDED) - HALF + row_offset).astype(f32)
        gather = jnp.where(gather_sub < nodes, 1.0, shifts)
        block = gather_lane // PADDED == lax.rem(gather_sub, nodes)
        gather = jnp.where(block, gather, 0.0).astype(bf16)
        sums = mm(
            jnp.concatenate([gather, gather], axis=1), jnp.concatenate([high, low], axis=0)
        )
        plain = sums[:nodes]
        across = lax.broadcasted_iota(jnp.int32, (nodes, PADDED), 1) - HALF + col_offset
        inverse = 1.0 / jnp.sum(plain, axis=1, keepdims=True)
        flow_row = jnp.sum(sums[nodes:], axis=1, keepdims=True) * inverse
        flow_col = jnp.sum(plain * across.astype(f32), axis=1, keepdims=True) * inverse
        line_row = jnp.sum(jnp.where(diagonal, flow_row, 0.0), axis=0, keepdims=True)
        line_col = jnp.sum(jnp.where(diagonal, flow_col, 0.0), axis=0, keepdims=True)
        tile = jnp.where(sub == row, line_row, 0.0)
        return jnp.where(sub == row + per_section, line_col, tile)

    def flow_copy(phase, ahead, step):
        part = 1 - phase
        slot = 1 - ahead
        return pltpu.make_async_remote_copy(
            src_ref=flow_tile.at[phase],
            dst_ref=flow_slots.at[slot, part, row],
            send_sem=flow_send.at[phase, ahead, step],
            recv_sem=flow_recv.at[slot, part, row],
            device_id={"tile": device(group + phase + ahead, mate(step))},
            device_id_type=MESH,
        )

    def each_flow(phase, act):
        for step in range(1 - phase, per_section):
            act(flow_copy(phase, 0, step))

        @pl.when(group + phase + 1 < SECTIONS)
        def _():
            for step in range(per_section):
                act(flow_copy(phase, 1, step))

    def take(slots, sems, slot, part, line):
        buffer = slots.at[slot, part, line]
        pltpu.make_async_copy(buffer, buffer, sems.at[slot, part, line]).wait()

    def gathered(slot):
        flow = jnp.zeros(shape, f32)
        mask = jnp.zeros(shape, f32)
        for part in range(2):
            for step in range(1 if slot == 1 and part == 1 else 0, per_section):
                take(flow_slots, flow_recv, slot, part, mate(step))
            for line in range(per_section):
                flow = flow + flow_slots[slot, part, line]
        for line in range(per_section):
            mask = mask + mask_slots[slot, line]
        return relax(flow, mask)

    @pl.when(group == SECTIONS - 1)
    def _():

        @pl.when(wrapped)
        def _():
            pl.semaphore_wait(go_sem, 1)
            start_bulk(0, relayed[0])


    @pl.when(group >= 1)
    def _():
        for q in range(chunks):
            arrived(0, q)
            for i, found in enumerate(spectra(prev_raw[q], 1, q * pair)):
                down_cross[q * pair + i] = cross(own(q * pair + i), found)

        @pl.when(group == 1)
        def _():
            end_bulk(0)

        @pl.when(group == 2)
        def _():
            end_bulk(0)

        @pl.when(jnp.logical_and(group == 2, wrapped))
        def _():
            start_bulk(1, relayed[1])

        @pl.when(jnp.logical_and(group == SECTIONS - 1, jnp.logical_not(wrapped)))
        def _():
            for k in range(relayed[1]):
                forward(1, k)


        for step in range(per_section):
            pltpu.make_async_copy(
                mask_slots.at[0, mate(step)], mask_slots.at[0, mate(step)], mask_recv.at[0, mate(step)]
            ).wait()

        @pl.when(group >= 2)
        def _():
            shift_ref[0] = gathered(0)

        tile = flows(group, down_cross, 0, 1, shift_ref[0])
        flow_tile[0] = tile
        flow_slots[1, 1, row] = tile
        each_flow(0, lambda copy: copy.start())

    @pl.when(group < SECTIONS - 1)
    def _():
        for q in range(chunks):
            arrived(1, q)
            for i, found in enumerate(spectra(next_raw[q], 2, q * pair)):
                up_cross[q * pair + i] = cross(found, own(q * pair + i))

    for step in range(1, per_section):
        pltpu.make_async_copy(
            mask_slots.at[1, mate(step)], mask_slots.at[1, mate(step)], mask_recv.at[1, mate(step)]
        ).wait()

    @pl.when(group >= 1)
    def _():
        shift_ref[1] = gathered(1)

    @pl.when(group < SECTIONS - 1)
    def _():
        flow_tile[1] = flows(group + 1, up_cross, 2, 0, shift_ref[1])
        each_flow(1, lambda copy: copy.start())

        @pl.when(jnp.logical_and(group == 0, jnp.logical_not(wrapped)))
        def _():
            pl.delay(REST)
            for k in range(relayed[0]):
                forward(0, k)

        @pl.when(jnp.logical_and(group == 0, wrapped))
        def _():
            release()

    home = shift_ref[1]
    out_row = jnp.sum(jnp.where(sub == row, home, 0.0), axis=0, keepdims=True)
    out_col = jnp.sum(jnp.where(sub == row + per_section, home, 0.0), axis=0, keepdims=True)
    out_ref[...] = jnp.concatenate([out_row, out_col], axis=0)

    for step in range(1, per_section):
        mask_copy(0, step).wait_send()

    @pl.when(group < SECTIONS - 1)
    def _():
        for step in range(per_section):
            mask_copy(1, step).wait_send()

        end_bulk(1)
        each_flow(1, lambda copy: copy.wait_send())

    @pl.when(group >= 1)
    def _():
        each_flow(0, lambda copy: copy.wait_send())

    @pl.when(group == SECTIONS - 1)
    def _():
        end_bulk(0)

    for way, section in ((0, 0), (1, SECTIONS - 1)):

        @pl.when(jnp.logical_and(group == section, jnp.logical_not(wrapped)))
        def _():
            for k in range(relayed[way]):
                onward(way, k).wait_send()


def warp_kernel(
    shift_ref, strip_in, warp_tables, parity_ref, out, node_ref, strip, result, sems
):
    pieces = strip.shape[0]
    width = strip.shape[2]
    loads, stores = [], []
    for k in range(pieces):
        where = pl.ds(k * width, width)
        loads.append(pltpu.make_async_copy(strip_in.at[:, where], strip.at[k], sems.at[k]))
        stores.append(
            pltpu.make_async_copy(result.at[k], out.at[:, where], sems.at[pieces + k])
        )
        loads[k].start()
    nodes = node_ref.shape[2]
    node_ref[0] = shift_ref[0:1, 0:nodes]
    node_ref[1] = shift_ref[1:2, 0:nodes]
    rows = kernel_rows(term_rows(shift_ref[0:1, :], shift_ref[1:2, :]), warp_tables[...])
    parity = parity_ref[...]
    for k in range(pieces):
        loads[k].wait()
        for j, s in enumerate(patch_slices(width)):
            i = k * (width // PATCH) + j
            patch = strip[k, :, s]
            checker = total(patch.astype(f32) * parity)
            result[k, :, s] = warp_patch(patch, rows, i, checker, parity).astype(bf16)
        stores[k].start()
    for copy in stores:
        copy.wait()


def shards(tile_count, sections, valid_mask, coarse_offsets):
    per_section = tile_count // SECTIONS
    grid_cols = valid_mask.shape[1]
    width = CHUNK * PATCH
    chunks = sections.shape[1] // (2 * width)
    nodes = chunks * CHUNK
    tile_shape = (2 * per_section, LANES)
    vmem = pl.BlockSpec(memory_space=pltpu.VMEM)
    left, right, window, warp_tables, parity = constants()
    hbm = pl.BlockSpec(memory_space=pltpu.HBM)
    raw = pltpu.VMEM((chunks, PATCH, width), bf16)
    spectrum = pltpu.VMEM((nodes, PATCH, PATCH), f32)
    crossed = pltpu.VMEM((nodes, PATCH, 2 * PATCH), bf16)
    dma = pltpu.SemaphoreType.DMA
    shift = pl.pallas_call(
        functools.partial(chain_kernel, tile_count, grid_cols),
        out_shape=jax.ShapeDtypeStruct((2, LANES), f32),
        in_specs=[hbm] * 6,
        out_specs=vmem,
        scratch_shapes=[
            pltpu.VMEM(left.shape, bf16),
            pltpu.VMEM(right.shape, bf16),
            pltpu.VMEM(window.shape, f32),
            pltpu.SMEM(coarse_offsets.shape[::-1], jnp.int32),
            pltpu.VMEM(valid_mask.shape, jnp.int32),
            dma((5 + chunks,)),
            raw,
            raw,
            raw,
            spectrum,
            spectrum,
            crossed,
            crossed,
            pltpu.VMEM((3, 3, nodes, LANES), f32),
            pltpu.VMEM(tile_shape, f32),
            pltpu.VMEM((2, per_section) + tile_shape, f32),
            pltpu.VMEM((2,) + tile_shape, f32),
            pltpu.VMEM((2, 2, per_section) + tile_shape, f32),
            pltpu.VMEM((2,) + tile_shape, f32),
            dma((2, chunks)),
            dma((2, chunks)),
            dma((2, per_section)),
            dma((2, per_section)),
            dma((2, 2, per_section)),
            dma((2, 2, per_section)),
            pltpu.SemaphoreType.REGULAR,
            pltpu.SemaphoreType.REGULAR,
            raw,
            dma((chunks,)),
            dma((chunks,)),
        ],
        compiler_params=pltpu.CompilerParams(
            collective_id=0, has_side_effects=True
        ),
        name="chain",
    )(coarse_offsets.T, valid_mask, left, right, window, sections)
    return pl.pallas_call(
        warp_kernel,
        out_shape=(
            jax.ShapeDtypeStruct(sections.shape, bf16),
            jax.ShapeDtypeStruct((2, 1, grid_cols), f32),
        ),
        in_specs=[vmem, hbm, vmem, vmem],
        out_specs=(hbm, vmem),
        scratch_shapes=[
            pltpu.VMEM((PIECES, PATCH, sections.shape[1] // PIECES), bf16),
            pltpu.VMEM((PIECES, PATCH, sections.shape[1] // PIECES), bf16),
            pltpu.SemaphoreType.DMA((2 * PIECES,)),
        ],
        name="warp",
    )(shift, sections, warp_tables, parity)


def solution(mesh):
    placed = (P(("parts", "tile"), None), P(("parts", "tile"), None), P("parts", None))
    return jax.shard_map(
        functools.partial(shards, mesh.shape["tile"]),
        mesh=mesh,
        in_specs=placed,
        out_specs=(P(("parts", "tile"), None), P(None, ("parts", "tile"), None)),
        check_vma=False,
    )
```

```python
import functools

import jax
import jax.numpy as jnp
import numpy as np
from jax import lax
from jax.experimental import pallas as pl
from jax.experimental.pallas import tpu as pltpu
from jax.sharding import PartitionSpec as P

SECTIONS = 4
PATCH = 128
HALF = 4
SWEEPS = 3
REACH = 3
WINDOW = 2 * HALF + 1
PADDED = 16
LANES = 128
CHUNK = 2
HUB = 2
REST = 2500
PIECES = 2

sharpness = 12.0
anchor_weight = 2.0
MESH = pl.DeviceIdType.MESH
f32 = jnp.float32
bf16 = jnp.bfloat16


def split(value):
    high = value.astype(bf16)
    return high, (value - high.astype(f32)).astype(bf16)


def mm(a, b):
    return jnp.dot(a, b, preferred_element_type=f32)


def mm_nt(a, b):
    return lax.dot_general(a, b, (((1,), (1,)), ((), ())), preferred_element_type=f32)


def constants():
    n = PATCH
    k = np.arange(n)
    angle = 2 * np.pi * ((k[:, None] * k[None, :]) % n) / n
    cosine, sine = np.cos(angle), np.sin(angle)
    left = []
    for table in (cosine, sine):
        high = np.asarray(table, bf16)
        low = np.asarray(table - high.astype(np.float64), bf16)
        left.append(np.concatenate([high, low], axis=1))
    left = np.concatenate(left, axis=0)
    right = np.block([[cosine, -sine], [-sine, -cosine]])
    right = np.asarray(right, bf16)
    u = np.arange(-HALF - REACH, -HALF - REACH + 24)
    window_angle = 2 * np.pi * ((u[:, None] * k[None, :]) % n) / n
    window = np.stack([np.cos(window_angle), np.sin(window_angle)])
    window = window.astype(np.float32)
    half_angle = np.pi * k / n
    sign = 1.0 - 2.0 * (k % 2)
    warp = np.zeros((8, n), np.float32)
    warp[:4] = np.stack([np.sin(half_angle), np.cos(half_angle), sign, k])
    parity = (sign[:, None] * sign[None, :]).astype(np.float32)
    return left, right, window, warp, parity


def turn(value):
    small = (value - jnp.round(value)) * np.pi
    square = small * small
    sine = small * (1.0 + square * (-1 / 6 + square * (1 / 120 + square * (
        -1 / 5040 + square * (1 / 362880 - square * (1 / 39916800))))))
    cosine = 1.0 + square * (-1 / 2 + square * (1 / 24 + square * (-1 / 720 + square * (
        1 / 40320 + square * (-1 / 3628800 + square * (1 / 479001600))))))
    return 1.0 - 2.0 * (sine * sine), 2.0 * (sine * cosine)


def shift_terms(d):
    whole = jnp.round(d)
    frac = d - whole
    odd = jnp.abs(whole - 2.0 * jnp.round(whole * 0.5))
    sine = jnp.sin(jnp.pi * frac)
    signed = jnp.where(odd > 0.5, -sine, sine) * (1.0 / PATCH)
    angle = d * (np.pi / PATCH)
    tangent = jnp.sin(angle) / jnp.cos(angle)
    small = frac * (np.pi / PATCH)
    tiny = jnp.abs(frac) < 1e-6
    peak = jnp.where(
        tiny, 1.0, sine * jnp.cos(small) / jnp.where(tiny, 1.0, PATCH * jnp.sin(small))
    )
    return tangent, signed, peak, whole


def kernel_rows(terms, tables, patches):
    columns = jnp.transpose(terms)[:patches]
    sine, cosine, parity, gap = [tables[i : i + 1, :] for i in range(4)]
    found = []
    for base, forward in ((0, False), (4, True)):
        tangent, signed, peak, whole = [columns[:, base + i : base + i + 1] for i in range(4)]
        if forward:
            bottom = cosine * tangent + sine
            top = cosine - sine * tangent
            centre = jnp.where(whole > 0, PATCH - whole, -whole)
        else:
            bottom = cosine * tangent - sine
            top = cosine + sine * tangent
            centre = jnp.where(whole < 0, whole + PATCH, whole)
        found.append(jnp.where(gap == centre, peak, (signed * parity) * (top / bottom)))
    corner = columns[:, 1:2] * columns[:, 5:6]
    return found[0], found[1], corner


def circulant(row):
    spread = jnp.broadcast_to(row, (PATCH, PATCH))
    return split(pltpu.roll(spread, 0, 1, stride=1, stride_axis=0))


def warp_patch(patch, left_row, right_row):
    left = circulant(left_row)
    right = circulant(right_row)
    both = mm(patch, jnp.concatenate(right, axis=1))
    high, low = split(both[:, :PATCH] + both[:, PATCH:])
    lower = jnp.concatenate([high, jnp.zeros_like(low)], axis=1)
    inner = jnp.concatenate([jnp.concatenate([high, low], axis=1), lower], axis=0)
    moved = mm(jnp.concatenate(left, axis=1), inner)
    return moved[:, :PATCH] + moved[:, PATCH:]


def term_rows(d_rows, d_cols):
    both = jnp.concatenate([d_rows, d_cols], axis=0)
    tangent, signed, peak, whole = shift_terms(both)
    pieces = [t[i : i + 1] for i in range(2) for t in (tangent, signed, peak, whole)]
    return jnp.concatenate(pieces, axis=0)


def chain_kernel(
    tile_count,
    grid_cols,
    offsets_in,
    mask_in,
    left_in,
    right_in,
    window_in,
    warp_in,
    parity_in,
    strip,
    out,
    node_ref,
    left_ref,
    right_ref,
    window,
    warp_tables,
    parity_ref,
    whole,
    check,
    offsets,
    mask_ref,
    load_sem,
    own_raw,
    prev_raw,
    next_raw,
    own_re,
    own_im,
    down_cross,
    up_cross,
    stats,
    mask_tile,
    mask_slots,
    flow_tile,
    flow_slots,
    shift_ref,
    bulk_send,
    bulk_recv,
    mask_send,
    mask_recv,
    flow_send,
    flow_recv,
    go_sem,
    all_sem,
    relay_raw,
    relay_send,
    relay_recv,
):
    per_section = tile_count // SECTIONS
    me = lax.axis_index("tile")
    lead = per_section // 2
    rotated = lax.rem(me + tile_count - lead, tile_count)
    group = rotated // per_section
    row = lax.rem(rotated, per_section)
    chunks, width = own_raw.shape[0], own_raw.shape[2]
    pair = width // PATCH
    nodes = chunks * pair
    half = lax.rem(group, 2)
    base = half * nodes
    piece = whole.shape[2]
    patches = PIECES * piece // PATCH

    def device(section, line):
        return lax.rem(section * per_section + line + lead, tile_count)

    def mate(line_step):
        return lax.rem(row + line_step, per_section)

    barrier = pltpu.get_barrier_semaphore()

    def signal(sem, section, line):
        pl.semaphore_signal(
            sem, inc=1, device_id={"tile": device(section, line)}, device_id_type=MESH
        )

    @pl.when(group <= 1)
    def _():
        signal(barrier, 1 - group, row)

    @pl.when(group == HUB)
    def _():
        signal(barrier, SECTIONS - 1, row)
        for step in range(1, per_section):
            signal(barrier, HUB, mate(step))

    @pl.when(group != HUB)
    def _():
        for step in range(per_section):
            signal(barrier, HUB, mate(step))

    def columns(side, chunk):
        start = pl.multiple_of((side * chunks + chunk) * width, LANES)
        return strip.at[:, pl.ds(start, width)]

    loads = [
        pltpu.make_async_copy(source, target, load_sem.at[i])
        for i, (source, target) in enumerate(
            [(mask_in, mask_ref), (offsets_in, offsets), (window_in, window)]
            + [(left_in, left_ref), (right_in, right_ref)]
            + [(warp_in, warp_tables), (parity_in, parity_ref)]
            + [(columns(half, q), own_raw.at[q]) for q in range(chunks)]
            + [(strip.at[:, pl.ds(k * piece, piece)], whole.at[k]) for k in range(PIECES)]
        )
    ]
    for copy in loads:
        copy.start()
    pl.semaphore_wait(barrier, jnp.where(group == HUB, tile_count - 1, 1))

    def bulk(way, chunk):
        peer = lax.rem(me + (per_section if way else tile_count - per_section), tile_count)
        return pltpu.make_async_remote_copy(
            src_ref=columns(1 - half, chunk),
            dst_ref=(prev_raw if way else next_raw).at[chunk],
            send_sem=bulk_send.at[way, chunk],
            recv_sem=bulk_recv.at[1 - way, chunk],
            device_id={"tile": peer},
            device_id_type=MESH,
        )

    def start_bulk(way, first=0, last=chunks):
        for chunk in range(first, last):
            bulk(way, chunk).start()

    relayed = (chunks // 2, chunks // 2)
    apart = per_section - per_section // 2
    wrapped = row >= apart

    def detour(way):
        for k in range(relayed[way]):
            pltpu.make_async_remote_copy(
                src_ref=columns(1 - half, k),
                dst_ref=relay_raw.at[k],
                send_sem=bulk_send.at[way, k],
                recv_sem=relay_recv.at[k],
                device_id={"tile": device(SECTIONS - 1 if way else 0, row - apart)},
                device_id_type=MESH,
            ).start()

    def onward(way, k):
        return pltpu.make_async_remote_copy(
            src_ref=relay_raw.at[k],
            dst_ref=(prev_raw if way else next_raw).at[k],
            send_sem=relay_send.at[k],
            recv_sem=bulk_recv.at[1 - way, k],
            device_id={"tile": device(SECTIONS - 1 if way else 2, row + apart)},
            device_id_type=MESH,
        )

    def forward(way, k):
        pltpu.make_async_copy(relay_raw.at[k], relay_raw.at[k], relay_recv.at[k]).wait()
        onward(way, k).start()

    def release():
        signal(go_sem, SECTIONS - 1, row)

    def end_bulk(way):
        for chunk in range(chunks):
            bulk(way, chunk).wait_send()

    @pl.when(group == HUB)
    def _():
        for section in range(SECTIONS):
            if section != HUB:
                signal(all_sem, section, row)

    @pl.when(jnp.logical_or(group == 1, group == 2))
    def _():
        start_bulk(0)

    @pl.when(group == 0)
    def _():
        start_bulk(1)

    for way in range(2):

        @pl.when(jnp.logical_and(group == SECTIONS - 1 - way, jnp.logical_not(wrapped)))
        def _():
            start_bulk(way)

    def mask_copy(ahead, step):
        return pltpu.make_async_remote_copy(
            src_ref=mask_tile,
            dst_ref=mask_slots.at[1 - ahead, row],
            send_sem=mask_send.at[ahead, step],
            recv_sem=mask_recv.at[1 - ahead, row],
            device_id={"tile": device(group + ahead, mate(step))},
            device_id_type=MESH,
        )

    loads[0].wait()
    shape = (2 * per_section, LANES)
    sub = lax.broadcasted_iota(jnp.int32, shape, 0)
    lane = lax.broadcasted_iota(jnp.int32, shape, 1)
    sub_row = lax.rem(sub, per_section)
    mask_tile[...] = jnp.zeros(shape, f32)
    mask_tile[0:1, 0:grid_cols] = mask_ref[...].astype(f32)
    mask_row = mask_tile[0:1, :]
    mask_tile[...] = jnp.where(sub_row == row, mask_row, 0.0)
    mask_slots[1, row] = mask_tile[...]
    shift_ref[...] = jnp.zeros((2,) + shape, f32)

    for copy in loads[1:-PIECES]:
        copy.wait()

    eight = lax.broadcasted_iota(jnp.int32, (8, LANES), 0)

    def spectra(pixels, kind, first_node):
        table = left_ref[...]
        first = mm(table, jnp.concatenate([pixels, pixels], axis=0))
        found = []
        for i in range(pair):
            s = slice(i * PATCH, (i + 1) * PATCH)
            level = jnp.sum(first[0:1, s], axis=1, keepdims=True) * (1.0 / PATCH)
            top = jnp.where(eight == 0, first[0:8, s] - level, first[0:8, s])
            body = jnp.concatenate([top, first[8:PATCH, s]], axis=0)
            halves = jnp.concatenate([body, first[PATCH:, s]], axis=1).astype(bf16)
            both = mm(halves, right_ref[...])
            real, imag = both[:, :PATCH], both[:, PATCH:]
            energy = real * real + imag * imag
            middle = slice(PATCH // 2, PATCH // 2 + 1)
            node = first_node + i
            stats[kind, 0, node : node + 1] = jnp.sum(energy, axis=0, keepdims=True)
            stats[kind, 1, node : node + 1] = energy[middle]
            stats[kind, 2, node : node + 1] = real[middle]
            found.append((real, imag))
        return found

    def cross(a, b):
        real = a[0] * b[0] + a[1] * b[1]
        imag = a[1] * b[0] - a[0] * b[1]
        return jnp.concatenate([real, imag], axis=1).astype(bf16)

    for q in range(chunks):
        for i, (real, imag) in enumerate(spectra(own_raw[q], 0, q * pair)):
            own_re[q * pair + i] = real
            own_im[q * pair + i] = imag

    @pl.when(group != HUB)
    def _():
        pl.semaphore_wait(all_sem, 1)

    for step in range(1, per_section):
        mask_copy(0, step).start()

    @pl.when(group < SECTIONS - 1)
    def _():
        for step in range(per_section):
            mask_copy(1, step).start()

    @pl.when(group == 1)
    def _():
        start_bulk(1)

    for way in range(2):

        @pl.when(jnp.logical_and(group == SECTIONS - 1 - way, wrapped))
        def _():
            detour(way)

    def arrived(way, chunk):
        buffer = (next_raw if way else prev_raw).at[chunk]
        pltpu.make_async_copy(buffer, buffer, bulk_recv.at[way, chunk]).wait()

    def own(node):
        return own_re[node], own_im[node]

    up_ok = (sub_row > 0).astype(f32)
    down_ok = (sub_row < per_section - 1).astype(f32)
    left_ok = jnp.logical_and(lane > 0, lane < grid_cols).astype(f32)
    right_ok = (lane < grid_cols - 1).astype(f32)
    count = up_ok + down_ok + left_ok + right_ok

    def relax(flow, mask):
        weight = anchor_weight * mask
        pull = weight * flow
        scale = 1.0 / (weight + count)
        d = flow * mask
        for _ in range(SWEEPS):
            near = (
                up_ok * pltpu.roll(d, 1, 0)
                + down_ok * pltpu.roll(d, 2 * per_section - 1, 0)
                + left_ok * pltpu.roll(d, 1, 1)
                + right_ok * pltpu.roll(d, LANES - 1, 1)
            )
            d = (pull + near) * scale
        return jnp.where(lane < grid_cols, d, 0.0)

    node_sub = lax.broadcasted_iota(jnp.int32, (nodes, LANES), 0)
    node_lane = lax.broadcasted_iota(jnp.int32, (nodes, LANES), 1)
    diagonal = node_lane == base + node_sub
    nyquist = node_lane == PATCH // 2
    frequency = jnp.where(node_lane < PATCH // 2, node_lane, node_lane - PATCH).astype(f32)
    frequency = frequency * (1.0 / PATCH)
    corr_row = lax.broadcasted_iota(jnp.int32, (PADDED, PADDED), 0)
    corr_col = lax.broadcasted_iota(jnp.int32, (PADDED, PADDED), 1)
    inside = jnp.logical_and(corr_row < WINDOW, corr_col < WINDOW)
    gather_sub = lax.broadcasted_iota(jnp.int32, (2 * nodes, nodes * PADDED), 0)
    gather_lane = lax.broadcasted_iota(jnp.int32, (2 * nodes, nodes * PADDED), 1)
    middle = slice(PATCH // 2, PATCH // 2 + 1)

    def column(d, which):
        line = jnp.sum(jnp.where(sub == row + which * per_section, d, 0.0), axis=0, keepdims=True)
        return jnp.sum(jnp.where(diagonal, line, 0.0), axis=1, keepdims=True)

    def flows(section, crosses, kind_a, kind_b, d):
        row_offset = offsets[0, section]
        col_offset = offsets[1, section]
        turned = []
        for which in range(2):
            cosine, sine = turn(frequency * column(d, which))
            turned.append((cosine, jnp.where(nyquist, 0.0, sine), cosine[:, middle], sine[:, middle]))
        (cos_y, sin_y, end_cy, end_sy), (cos_x, sin_x, end_cx, end_sx) = turned
        total_a = jnp.sum(stats[kind_a, 0], axis=1, keepdims=True)
        edge_col = stats[kind_b, 0]
        total_b = jnp.sum(edge_col, axis=1, keepdims=True)
        edge_row = jnp.sum(stats[kind_b, 1], axis=1, keepdims=True)
        tip_a = stats[kind_a, 2][:, middle]
        tip_b = stats[kind_b, 2][:, middle]
        tip = tip_b * tip_b
        end_both = end_cy * end_cx - end_sy * end_sx
        lost = (
            (edge_row - tip) * (end_sy * end_sy)
            + (edge_col[:, middle] - tip) * (end_sx * end_sx)
            + tip * (1.0 - end_both * end_both)
        )
        size = 1.0 / float(PATCH) ** 4
        variance_a = total_a * size + 1e-05
        variance_b = jnp.maximum((total_b - lost) * size, 0.0) + 1e-05
        scales = (sharpness * size) * lax.rsqrt(variance_a * variance_b)
        corners = end_sy * end_sx * tip_a * tip_b
        row_cos = window[0, pl.ds(row_offset + REACH, PADDED), :]
        row_sin = window[1, pl.ds(row_offset + REACH, PADDED), :]
        col_cos = window[0, pl.ds(col_offset + REACH, PADDED), :]
        col_sin = window[1, pl.ds(col_offset + REACH, PADDED), :]
        col_high, col_low = split(jnp.concatenate([col_cos, -col_sin], axis=1))
        moved = []
        for i in range(nodes):
            c, s = cos_y[i : i + 1], sin_y[i : i + 1]
            table = jnp.concatenate(
                [row_cos * c + row_sin * s, row_sin * c - row_cos * s], axis=0
            )
            parts = mm(jnp.concatenate(split(table), axis=0), crosses[i])
            parts = parts[: 2 * PADDED] + parts[2 * PADDED :]
            real = parts[:PADDED, :PATCH] - parts[PADDED:, PATCH:]
            imag = parts[:PADDED, PATCH:] + parts[PADDED:, :PATCH]
            c, s = cos_x[i : i + 1], sin_x[i : i + 1]
            moved.append(
                jnp.concatenate([real * c + imag * s, imag * c - real * s], axis=1)
            )
        high, low = split(jnp.concatenate(moved, axis=0))
        correlation = mm_nt(
            jnp.concatenate([high, low, high], axis=1),
            jnp.concatenate([col_high, col_high, col_low], axis=1),
        )
        odd = (corr_row + corr_col + (row_offset + col_offset + 2 * REACH)) & 1
        parity = 1.0 - 2.0 * odd.astype(f32)
        weights = []
        for i in range(nodes):
            here = correlation[i * PADDED : (i + 1) * PADDED] - corners[i : i + 1] * parity
            weights.append(jnp.where(inside, jnp.exp(here * scales[i : i + 1]), 0.0))
        high, low = split(jnp.concatenate(weights, axis=0))
        shifts = (lax.rem(gather_lane, PADDED) - HALF + row_offset).astype(f32)
        gather = jnp.where(gather_sub < nodes, 1.0, shifts)
        block = gather_lane // PADDED == lax.rem(gather_sub, nodes)
        gather = jnp.where(block, gather, 0.0).astype(bf16)
        sums = mm(
            jnp.concatenate([gather, gather], axis=1), jnp.concatenate([high, low], axis=0)
        )
        plain = sums[:nodes]
        across = lax.broadcasted_iota(jnp.int32, (nodes, PADDED), 1) - HALF + col_offset
        inverse = 1.0 / jnp.sum(plain, axis=1, keepdims=True)
        flow_row = jnp.sum(sums[nodes:], axis=1, keepdims=True) * inverse
        flow_col = jnp.sum(plain * across.astype(f32), axis=1, keepdims=True) * inverse
        line_row = jnp.sum(jnp.where(diagonal, flow_row, 0.0), axis=0, keepdims=True)
        line_col = jnp.sum(jnp.where(diagonal, flow_col, 0.0), axis=0, keepdims=True)
        tile = jnp.where(sub == row, line_row, 0.0)
        return jnp.where(sub == row + per_section, line_col, tile)

    def flow_copy(phase, ahead, step):
        part = 1 - phase
        slot = 1 - ahead
        return pltpu.make_async_remote_copy(
            src_ref=flow_tile.at[phase],
            dst_ref=flow_slots.at[slot, part, row],
            send_sem=flow_send.at[phase, ahead, step],
            recv_sem=flow_recv.at[slot, part, row],
            device_id={"tile": device(group + phase + ahead, mate(step))},
            device_id_type=MESH,
        )

    def each_flow(phase, act):
        for step in range(1 - phase, per_section):
            act(flow_copy(phase, 0, step))

        @pl.when(group + phase + 1 < SECTIONS)
        def _():
            for step in range(per_section):
                act(flow_copy(phase, 1, step))

    def take(slots, sems, slot, part, line):
        buffer = slots.at[slot, part, line]
        pltpu.make_async_copy(buffer, buffer, sems.at[slot, part, line]).wait()

    def gathered(slot):
        flow = jnp.zeros(shape, f32)
        mask = jnp.zeros(shape, f32)
        for part in range(2):
            for step in range(1 if slot == 1 and part == 1 else 0, per_section):
                take(flow_slots, flow_recv, slot, part, mate(step))
            for line in range(per_section):
                flow = flow + flow_slots[slot, part, line]
        for line in range(per_section):
            mask = mask + mask_slots[slot, line]
        return relax(flow, mask)

    @pl.when(group == SECTIONS - 1)
    def _():

        @pl.when(wrapped)
        def _():
            pl.semaphore_wait(go_sem, 1)
            start_bulk(0, relayed[0])


    @pl.when(group >= 1)
    def _():
        for q in range(chunks):
            arrived(0, q)
            for i, found in enumerate(spectra(prev_raw[q], 1, q * pair)):
                down_cross[q * pair + i] = cross(own(q * pair + i), found)

        @pl.when(group == 1)
        def _():
            end_bulk(0)

        @pl.when(group == 2)
        def _():
            end_bulk(0)

        @pl.when(jnp.logical_and(group == 2, wrapped))
        def _():
            start_bulk(1, relayed[1])

        @pl.when(jnp.logical_and(group == SECTIONS - 1, jnp.logical_not(wrapped)))
        def _():
            for k in range(relayed[1]):
                forward(1, k)


        for step in range(per_section):
            pltpu.make_async_copy(
                mask_slots.at[0, mate(step)], mask_slots.at[0, mate(step)], mask_recv.at[0, mate(step)]
            ).wait()

        @pl.when(group >= 2)
        def _():
            shift_ref[0] = gathered(0)

        tile = flows(group, down_cross, 0, 1, shift_ref[0])
        flow_tile[0] = tile
        flow_slots[1, 1, row] = tile
        each_flow(0, lambda copy: copy.start())

    @pl.when(group < SECTIONS - 1)
    def _():
        for q in range(chunks):
            arrived(1, q)
            for i, found in enumerate(spectra(next_raw[q], 2, q * pair)):
                up_cross[q * pair + i] = cross(found, own(q * pair + i))

    def part(i):
        k, j = divmod(i, piece // PATCH)
        return whole[k, :, j * PATCH : (j + 1) * PATCH]

    for copy in loads[-PIECES:]:
        copy.wait()
    for i in range(patches):
        check[i : i + 1] = jnp.sum(part(i).astype(f32) * parity_ref[...], axis=0, keepdims=True)
    sums = jnp.sum(check[...], axis=1, keepdims=True)
    check[...] = jnp.broadcast_to(sums, check.shape)

    for step in range(1, per_section):
        pltpu.make_async_copy(
            mask_slots.at[1, mate(step)], mask_slots.at[1, mate(step)], mask_recv.at[1, mate(step)]
        ).wait()

    @pl.when(group >= 1)
    def _():
        shift_ref[1] = gathered(1)

    @pl.when(group < SECTIONS - 1)
    def _():
        flow_tile[1] = flows(group + 1, up_cross, 2, 0, shift_ref[1])
        each_flow(1, lambda copy: copy.start())

        @pl.when(jnp.logical_and(group == 0, jnp.logical_not(wrapped)))
        def _():
            pl.delay(REST)
            for k in range(relayed[0]):
                forward(0, k)

        @pl.when(jnp.logical_and(group == 0, wrapped))
        def _():
            release()

    home = shift_ref[1]
    lines = [
        jnp.sum(jnp.where(sub == row + which * per_section, home, 0.0), axis=0, keepdims=True)
        for which in range(2)
    ]
    for which in range(2):
        node_ref[which] = lines[which][:, :grid_cols]
    rows = kernel_rows(term_rows(lines[0], lines[1]), warp_tables[...], patches)
    corner = rows[2] * check[:, 0:1]
    for k in range(PIECES):
        for j in range(piece // PATCH):
            i = k * (piece // PATCH) + j
            moved = warp_patch(part(i), rows[0][i : i + 1], rows[1][i : i + 1])
            out[:, i * PATCH : (i + 1) * PATCH] = (
                moved - corner[i : i + 1] * parity_ref[...]
            ).astype(bf16)

    for step in range(1, per_section):
        mask_copy(0, step).wait_send()

    @pl.when(group < SECTIONS - 1)
    def _():
        for step in range(per_section):
            mask_copy(1, step).wait_send()

        end_bulk(1)
        each_flow(1, lambda copy: copy.wait_send())

    @pl.when(group >= 1)
    def _():
        each_flow(0, lambda copy: copy.wait_send())

    @pl.when(group == SECTIONS - 1)
    def _():
        end_bulk(0)

    for way, section in ((0, 0), (1, SECTIONS - 1)):

        @pl.when(jnp.logical_and(group == section, jnp.logical_not(wrapped)))
        def _():
            for k in range(relayed[way]):
                onward(way, k).wait_send()


def store_kernel(aligned, shift, out, shift_out, sems):
    stores = [
        pltpu.make_async_copy(shift, shift_out, sems.at[0]),
        pltpu.make_async_copy(aligned, out, sems.at[1]),
    ]
    for copy in stores:
        copy.start()
    for copy in stores:
        copy.wait()


def shards(tile_count, sections, valid_mask, coarse_offsets):
    per_section = tile_count // SECTIONS
    grid_cols = valid_mask.shape[1]
    width = CHUNK * PATCH
    chunks = sections.shape[1] // (2 * width)
    nodes = chunks * CHUNK
    tile_shape = (2 * per_section, LANES)
    vmem = pl.BlockSpec(memory_space=pltpu.VMEM)
    left, right, window, warp_tables, parity = constants()
    hbm = pl.BlockSpec(memory_space=pltpu.HBM)
    raw = pltpu.VMEM((chunks, PATCH, width), bf16)
    spectrum = pltpu.VMEM((nodes, PATCH, PATCH), f32)
    crossed = pltpu.VMEM((nodes, PATCH, 2 * PATCH), bf16)
    dma = pltpu.SemaphoreType.DMA
    patches = sections.shape[1] // PATCH
    pieces = pltpu.VMEM((PIECES, PATCH, sections.shape[1] // PIECES), bf16)
    aligned, shift = pl.pallas_call(
        functools.partial(chain_kernel, tile_count, grid_cols),
        out_shape=(
            pltpu.VMEM(sections.shape, bf16),
            pltpu.VMEM((2, 1, grid_cols), f32),
        ),
        in_specs=[hbm] * 8,
        out_specs=(vmem, vmem),
        scratch_shapes=[
            pltpu.VMEM(left.shape, bf16),
            pltpu.VMEM(right.shape, bf16),
            pltpu.VMEM(window.shape, f32),
            pltpu.VMEM(warp_tables.shape, f32),
            pltpu.VMEM(parity.shape, f32),
            pieces,
            pltpu.VMEM((patches, LANES), f32),
            pltpu.SMEM(coarse_offsets.shape[::-1], jnp.int32),
            pltpu.VMEM(valid_mask.shape, jnp.int32),
            dma((7 + chunks + PIECES,)),
            raw,
            raw,
            raw,
            spectrum,
            spectrum,
            crossed,
            crossed,
            pltpu.VMEM((3, 3, nodes, LANES), f32),
            pltpu.VMEM(tile_shape, f32),
            pltpu.VMEM((2, per_section) + tile_shape, f32),
            pltpu.VMEM((2,) + tile_shape, f32),
            pltpu.VMEM((2, 2, per_section) + tile_shape, f32),
            pltpu.VMEM((2,) + tile_shape, f32),
            dma((2, chunks)),
            dma((2, chunks)),
            dma((2, per_section)),
            dma((2, per_section)),
            dma((2, 2, per_section)),
            dma((2, 2, per_section)),
            pltpu.SemaphoreType.REGULAR,
            pltpu.SemaphoreType.REGULAR,
            raw,
            dma((chunks,)),
            dma((chunks,)),
        ],
        compiler_params=pltpu.CompilerParams(
            collective_id=0, has_side_effects=True
        ),
        name="chain",
    )(coarse_offsets.T, valid_mask, left, right, window, warp_tables, parity, sections)
    return pl.pallas_call(
        store_kernel,
        out_shape=(
            jax.ShapeDtypeStruct(sections.shape, bf16),
            jax.ShapeDtypeStruct((2, 1, grid_cols), f32),
        ),
        in_specs=[vmem, vmem],
        out_specs=(hbm, hbm),
        scratch_shapes=[dma((2,))],
        name="store",
    )(*[pltpu.with_memory_space_constraint(x, pltpu.VMEM) for x in (aligned, shift)])


def solution(mesh):
    placed = (P(("parts", "tile"), None), P(("parts", "tile"), None), P("parts", None))
    return jax.shard_map(
        functools.partial(shards, mesh.shape["tile"]),
        mesh=mesh,
        in_specs=placed,
        out_specs=(P(("parts", "tile"), None), P(None, ("parts", "tile"), None)),
        check_vma=False,
    )
```

```python
import functools

import jax
import jax.numpy as jnp
import numpy as np
from jax import lax
from jax.experimental import pallas as pl
from jax.experimental.pallas import tpu as pltpu
from jax.sharding import PartitionSpec as P

SECTIONS = 4
PATCH = 128
HALF = 4
SWEEPS = 3
REACH = 3
WINDOW = 2 * HALF + 1
PADDED = 16
LANES = 128
CHUNK = 2
HUB = 2
REST = 2500
PIECES = 2

sharpness = 12.0
anchor_weight = 2.0
MESH = pl.DeviceIdType.MESH
f32 = jnp.float32
bf16 = jnp.bfloat16


def split(value):
    high = value.astype(bf16)
    return high, (value - high.astype(f32)).astype(bf16)


def mm(a, b):
    return jnp.dot(a, b, preferred_element_type=f32)


def mm_nt(a, b):
    return lax.dot_general(a, b, (((1,), (1,)), ((), ())), preferred_element_type=f32)


def constants():
    n = PATCH
    k = np.arange(n)
    angle = 2 * np.pi * ((k[:, None] * k[None, :]) % n) / n
    cosine, sine = np.cos(angle), np.sin(angle)
    left = []
    for table in (cosine, sine):
        high = np.asarray(table, bf16)
        low = np.asarray(table - high.astype(np.float64), bf16)
        left.append(np.concatenate([high, low], axis=1))
    left = np.concatenate(left, axis=0)
    right = np.block([[cosine, -sine], [-sine, -cosine]])
    right = np.asarray(right, bf16)
    u = np.arange(-HALF - REACH, -HALF - REACH + 24)
    window_angle = 2 * np.pi * ((u[:, None] * k[None, :]) % n) / n
    window = np.stack([np.cos(window_angle), np.sin(window_angle)])
    window = window.astype(np.float32)
    half_angle = np.pi * k / n
    sign = 1.0 - 2.0 * (k % 2)
    warp = np.zeros((8, n), np.float32)
    warp[:4] = np.stack([np.sin(half_angle), np.cos(half_angle), sign, k])
    parity = (sign[:, None] * sign[None, :]).astype(np.float32)
    return left, right, window, warp, parity


def turn(value):
    small = (value - jnp.round(value)) * np.pi
    square = small * small
    sine = small * (1.0 + square * (-1 / 6 + square * (1 / 120 + square * (
        -1 / 5040 + square * (1 / 362880 - square * (1 / 39916800))))))
    cosine = 1.0 + square * (-1 / 2 + square * (1 / 24 + square * (-1 / 720 + square * (
        1 / 40320 + square * (-1 / 3628800 + square * (1 / 479001600))))))
    return 1.0 - 2.0 * (sine * sine), 2.0 * (sine * cosine)


def shift_terms(d):
    whole = jnp.round(d)
    frac = d - whole
    odd = jnp.abs(whole - 2.0 * jnp.round(whole * 0.5))
    sine = jnp.sin(jnp.pi * frac)
    signed = jnp.where(odd > 0.5, -sine, sine) * (1.0 / PATCH)
    angle = d * (np.pi / PATCH)
    tangent = jnp.sin(angle) / jnp.cos(angle)
    small = frac * (np.pi / PATCH)
    tiny = jnp.abs(frac) < 1e-6
    peak = jnp.where(
        tiny, 1.0, sine * jnp.cos(small) / jnp.where(tiny, 1.0, PATCH * jnp.sin(small))
    )
    return tangent, signed, peak, whole


def kernel_rows(terms, tables, patches):
    columns = jnp.transpose(terms)[:patches]
    sine, cosine, parity, gap = [tables[i : i + 1, :] for i in range(4)]
    found = []
    for base, forward in ((0, False), (4, True)):
        tangent, signed, peak, whole = [columns[:, base + i : base + i + 1] for i in range(4)]
        if forward:
            bottom = cosine * tangent + sine
            top = cosine - sine * tangent
            centre = jnp.where(whole > 0, PATCH - whole, -whole)
        else:
            bottom = cosine * tangent - sine
            top = cosine + sine * tangent
            centre = jnp.where(whole < 0, whole + PATCH, whole)
        found.append(jnp.where(gap == centre, peak, (signed * parity) * (top / bottom)))
    corner = columns[:, 1:2] * columns[:, 5:6]
    return found[0], found[1], corner


def circulant(row):
    spread = jnp.broadcast_to(row, (PATCH, PATCH))
    return split(pltpu.roll(spread, 0, 1, stride=1, stride_axis=0))


def warp_patch(patch, left_row, right_row):
    left = circulant(left_row)
    right = circulant(right_row)
    both = mm(patch, jnp.concatenate(right, axis=1))
    high, low = split(both[:, :PATCH] + both[:, PATCH:])
    lower = jnp.concatenate([high, jnp.zeros_like(low)], axis=1)
    inner = jnp.concatenate([jnp.concatenate([high, low], axis=1), lower], axis=0)
    moved = mm(jnp.concatenate(left, axis=1), inner)
    return moved[:, :PATCH] + moved[:, PATCH:]


def term_rows(d_rows, d_cols):
    both = jnp.concatenate([d_rows, d_cols], axis=0)
    tangent, signed, peak, whole = shift_terms(both)
    pieces = [t[i : i + 1] for i in range(2) for t in (tangent, signed, peak, whole)]
    return jnp.concatenate(pieces, axis=0)


def chain_kernel(
    tile_count,
    grid_cols,
    offsets_in,
    mask_in,
    left_in,
    right_in,
    window_in,
    warp_in,
    parity_in,
    strip,
    out,
    node_ref,
    left_ref,
    right_ref,
    window,
    warp_tables,
    parity_ref,
    whole,
    check,
    offsets,
    mask_ref,
    load_sem,
    own_raw,
    prev_raw,
    next_raw,
    own_re,
    own_im,
    down_cross,
    up_cross,
    stats,
    mask_tile,
    mask_slots,
    flow_tile,
    flow_slots,
    shift_ref,
    bulk_send,
    bulk_recv,
    mask_send,
    mask_recv,
    flow_send,
    flow_recv,
    go_sem,
    all_sem,
    relay_raw,
    relay_send,
    relay_recv,
):
    per_section = tile_count // SECTIONS
    me = lax.axis_index("tile")
    lead = per_section // 2
    rotated = lax.rem(me + tile_count - lead, tile_count)
    group = rotated // per_section
    row = lax.rem(rotated, per_section)
    chunks, width = own_raw.shape[0], own_raw.shape[2]
    pair = width // PATCH
    nodes = chunks * pair
    half = lax.rem(group, 2)
    base = half * nodes
    piece = whole.shape[2]
    patches = PIECES * piece // PATCH

    def device(section, line):
        return lax.rem(section * per_section + line + lead, tile_count)

    def mate(line_step):
        return lax.rem(row + line_step, per_section)

    barrier = pltpu.get_barrier_semaphore()

    def signal(sem, section, line):
        pl.semaphore_signal(
            sem, inc=1, device_id={"tile": device(section, line)}, device_id_type=MESH
        )

    @pl.when(group <= 1)
    def _():
        signal(barrier, 1 - group, row)

    @pl.when(group == HUB)
    def _():
        signal(barrier, SECTIONS - 1, row)
        for step in range(1, per_section):
            signal(barrier, HUB, mate(step))

    @pl.when(group != HUB)
    def _():
        for step in range(per_section):
            signal(barrier, HUB, mate(step))

    def columns(side, chunk):
        start = pl.multiple_of((side * chunks + chunk) * width, LANES)
        return strip.at[:, pl.ds(start, width)]

    loads = [
        pltpu.make_async_copy(source, target, load_sem.at[i])
        for i, (source, target) in enumerate(
            [(mask_in, mask_ref), (offsets_in, offsets), (window_in, window)]
            + [(left_in, left_ref), (right_in, right_ref)]
            + [(warp_in, warp_tables), (parity_in, parity_ref)]
            + [(columns(half, q), own_raw.at[q]) for q in range(chunks)]
            + [(strip.at[:, pl.ds(k * piece, piece)], whole.at[k]) for k in range(PIECES)]
        )
    ]
    for copy in loads:
        copy.start()
    pl.semaphore_wait(barrier, jnp.where(group == HUB, tile_count - 1, 1))

    def bulk(way, chunk):
        peer = lax.rem(me + (per_section if way else tile_count - per_section), tile_count)
        return pltpu.make_async_remote_copy(
            src_ref=columns(1 - half, chunk),
            dst_ref=(prev_raw if way else next_raw).at[chunk],
            send_sem=bulk_send.at[way, chunk],
            recv_sem=bulk_recv.at[1 - way, chunk],
            device_id={"tile": peer},
            device_id_type=MESH,
        )

    def start_bulk(way, first=0, last=chunks):
        for chunk in range(first, last):
            bulk(way, chunk).start()

    relayed = (chunks // 2, chunks // 2)
    apart = per_section - per_section // 2
    wrapped = row >= apart

    def detour(way):
        for k in range(relayed[way]):
            pltpu.make_async_remote_copy(
                src_ref=columns(1 - half, k),
                dst_ref=relay_raw.at[k],
                send_sem=bulk_send.at[way, k],
                recv_sem=relay_recv.at[k],
                device_id={"tile": device(SECTIONS - 1 if way else 0, row - apart)},
                device_id_type=MESH,
            ).start()

    def onward(way, k):
        return pltpu.make_async_remote_copy(
            src_ref=relay_raw.at[k],
            dst_ref=(prev_raw if way else next_raw).at[k],
            send_sem=relay_send.at[k],
            recv_sem=bulk_recv.at[1 - way, k],
            device_id={"tile": device(SECTIONS - 1 if way else 2, row + apart)},
            device_id_type=MESH,
        )

    def forward(way, k):
        pltpu.make_async_copy(relay_raw.at[k], relay_raw.at[k], relay_recv.at[k]).wait()
        onward(way, k).start()

    def release():
        signal(go_sem, SECTIONS - 1, row)

    def end_bulk(way):
        for chunk in range(chunks):
            bulk(way, chunk).wait_send()

    @pl.when(group == HUB)
    def _():
        for section in range(SECTIONS):
            if section != HUB:
                signal(all_sem, section, row)

    @pl.when(jnp.logical_or(group == 1, group == 2))
    def _():
        start_bulk(0)

    @pl.when(group == 0)
    def _():
        start_bulk(1)

    for way in range(2):

        @pl.when(jnp.logical_and(group == SECTIONS - 1 - way, jnp.logical_not(wrapped)))
        def _():
            start_bulk(way)

    def mask_copy(ahead, step):
        return pltpu.make_async_remote_copy(
            src_ref=mask_tile,
            dst_ref=mask_slots.at[1 - ahead, row],
            send_sem=mask_send.at[ahead, step],
            recv_sem=mask_recv.at[1 - ahead, row],
            device_id={"tile": device(group + ahead, mate(step))},
            device_id_type=MESH,
        )

    loads[0].wait()
    shape = (2 * per_section, LANES)
    sub = lax.broadcasted_iota(jnp.int32, shape, 0)
    lane = lax.broadcasted_iota(jnp.int32, shape, 1)
    sub_row = lax.rem(sub, per_section)
    mask_tile[...] = jnp.zeros(shape, f32)
    mask_tile[0:1, 0:grid_cols] = mask_ref[...].astype(f32)
    mask_row = mask_tile[0:1, :]
    mask_tile[...] = jnp.where(sub_row == row, mask_row, 0.0)
    mask_slots[1, row] = mask_tile[...]
    shift_ref[...] = jnp.zeros((2,) + shape, f32)

    for copy in loads[1:-PIECES]:
        copy.wait()

    eight = lax.broadcasted_iota(jnp.int32, (8, LANES), 0)

    def spectra(pixels, kind, first_node):
        table = left_ref[...]
        first = mm(table, jnp.concatenate([pixels, pixels], axis=0))
        found = []
        for i in range(pair):
            s = slice(i * PATCH, (i + 1) * PATCH)
            level = jnp.sum(first[0:1, s], axis=1, keepdims=True) * (1.0 / PATCH)
            top = jnp.where(eight == 0, first[0:8, s] - level, first[0:8, s])
            body = jnp.concatenate([top, first[8:PATCH, s]], axis=0)
            halves = jnp.concatenate([body, first[PATCH:, s]], axis=1).astype(bf16)
            both = mm(halves, right_ref[...])
            real, imag = both[:, :PATCH], both[:, PATCH:]
            energy = real * real + imag * imag
            middle = slice(PATCH // 2, PATCH // 2 + 1)
            node = first_node + i
            stats[kind, 0, node : node + 1] = jnp.sum(energy, axis=0, keepdims=True)
            stats[kind, 1, node : node + 1] = energy[middle]
            stats[kind, 2, node : node + 1] = real[middle]
            found.append((real, imag))
        return found

    def cross(a, b):
        real = a[0] * b[0] + a[1] * b[1]
        imag = a[1] * b[0] - a[0] * b[1]
        return jnp.concatenate([real, imag], axis=1).astype(bf16)

    for q in range(chunks):
        for i, (real, imag) in enumerate(spectra(own_raw[q], 0, q * pair)):
            own_re[q * pair + i] = real
            own_im[q * pair + i] = imag

    def part(i):
        k, j = divmod(i, piece // PATCH)
        return whole[k, :, j * PATCH : (j + 1) * PATCH]

    for copy in loads[-PIECES:]:
        copy.wait()
    for i in range(patches):
        check[i : i + 1] = jnp.sum(part(i).astype(f32) * parity_ref[...], axis=0, keepdims=True)
    sums = jnp.sum(check[...], axis=1, keepdims=True)
    check[...] = jnp.broadcast_to(sums, check.shape)

    @pl.when(group != HUB)
    def _():
        pl.semaphore_wait(all_sem, 1)

    for step in range(1, per_section):
        mask_copy(0, step).start()

    @pl.when(group < SECTIONS - 1)
    def _():
        for step in range(per_section):
            mask_copy(1, step).start()

    @pl.when(group == 1)
    def _():
        start_bulk(1)

    for way in range(2):

        @pl.when(jnp.logical_and(group == SECTIONS - 1 - way, wrapped))
        def _():
            detour(way)

    def arrived(way, chunk):
        buffer = (next_raw if way else prev_raw).at[chunk]
        pltpu.make_async_copy(buffer, buffer, bulk_recv.at[way, chunk]).wait()

    def own(node):
        return own_re[node], own_im[node]

    up_ok = (sub_row > 0).astype(f32)
    down_ok = (sub_row < per_section - 1).astype(f32)
    left_ok = jnp.logical_and(lane > 0, lane < grid_cols).astype(f32)
    right_ok = (lane < grid_cols - 1).astype(f32)
    count = up_ok + down_ok + left_ok + right_ok

    def relax(flow, mask):
        weight = anchor_weight * mask
        pull = weight * flow
        scale = 1.0 / (weight + count)
        d = flow * mask
        for _ in range(SWEEPS):
            near = (
                up_ok * pltpu.roll(d, 1, 0)
                + down_ok * pltpu.roll(d, 2 * per_section - 1, 0)
                + left_ok * pltpu.roll(d, 1, 1)
                + right_ok * pltpu.roll(d, LANES - 1, 1)
            )
            d = (pull + near) * scale
        return jnp.where(lane < grid_cols, d, 0.0)

    node_sub = lax.broadcasted_iota(jnp.int32, (nodes, LANES), 0)
    node_lane = lax.broadcasted_iota(jnp.int32, (nodes, LANES), 1)
    diagonal = node_lane == base + node_sub
    nyquist = node_lane == PATCH // 2
    frequency = jnp.where(node_lane < PATCH // 2, node_lane, node_lane - PATCH).astype(f32)
    frequency = frequency * (1.0 / PATCH)
    corr_row = lax.broadcasted_iota(jnp.int32, (PADDED, PADDED), 0)
    corr_col = lax.broadcasted_iota(jnp.int32, (PADDED, PADDED), 1)
    inside = jnp.logical_and(corr_row < WINDOW, corr_col < WINDOW)
    gather_sub = lax.broadcasted_iota(jnp.int32, (2 * nodes, nodes * PADDED), 0)
    gather_lane = lax.broadcasted_iota(jnp.int32, (2 * nodes, nodes * PADDED), 1)
    middle = slice(PATCH // 2, PATCH // 2 + 1)

    def column(d, which):
        line = jnp.sum(jnp.where(sub == row + which * per_section, d, 0.0), axis=0, keepdims=True)
        return jnp.sum(jnp.where(diagonal, line, 0.0), axis=1, keepdims=True)

    def flows(section, crosses, kind_a, kind_b, d):
        row_offset = offsets[0, section]
        col_offset = offsets[1, section]
        turned = []
        for which in range(2):
            cosine, sine = turn(frequency * column(d, which))
            turned.append((cosine, jnp.where(nyquist, 0.0, sine), cosine[:, middle], sine[:, middle]))
        (cos_y, sin_y, end_cy, end_sy), (cos_x, sin_x, end_cx, end_sx) = turned
        total_a = jnp.sum(stats[kind_a, 0], axis=1, keepdims=True)
        edge_col = stats[kind_b, 0]
        total_b = jnp.sum(edge_col, axis=1, keepdims=True)
        edge_row = jnp.sum(stats[kind_b, 1], axis=1, keepdims=True)
        tip_a = stats[kind_a, 2][:, middle]
        tip_b = stats[kind_b, 2][:, middle]
        tip = tip_b * tip_b
        end_both = end_cy * end_cx - end_sy * end_sx
        lost = (
            (edge_row - tip) * (end_sy * end_sy)
            + (edge_col[:, middle] - tip) * (end_sx * end_sx)
            + tip * (1.0 - end_both * end_both)
        )
        size = 1.0 / float(PATCH) ** 4
        variance_a = total_a * size + 1e-05
        variance_b = jnp.maximum((total_b - lost) * size, 0.0) + 1e-05
        scales = (sharpness * size) * lax.rsqrt(variance_a * variance_b)
        corners = end_sy * end_sx * tip_a * tip_b
        row_cos = window[0, pl.ds(row_offset + REACH, PADDED), :]
        row_sin = window[1, pl.ds(row_offset + REACH, PADDED), :]
        col_cos = window[0, pl.ds(col_offset + REACH, PADDED), :]
        col_sin = window[1, pl.ds(col_offset + REACH, PADDED), :]
        col_high, col_low = split(jnp.concatenate([col_cos, -col_sin], axis=1))
        moved = []
        for i in range(nodes):
            c, s = cos_y[i : i + 1], sin_y[i : i + 1]
            table = jnp.concatenate(
                [row_cos * c + row_sin * s, row_sin * c - row_cos * s], axis=0
            )
            parts = mm(jnp.concatenate(split(table), axis=0), crosses[i])
            parts = parts[: 2 * PADDED] + parts[2 * PADDED :]
            real = parts[:PADDED, :PATCH] - parts[PADDED:, PATCH:]
            imag = parts[:PADDED, PATCH:] + parts[PADDED:, :PATCH]
            c, s = cos_x[i : i + 1], sin_x[i : i + 1]
            moved.append(
                jnp.concatenate([real * c + imag * s, imag * c - real * s], axis=1)
            )
        high, low = split(jnp.concatenate(moved, axis=0))
        correlation = mm_nt(
            jnp.concatenate([high, low, high], axis=1),
            jnp.concatenate([col_high, col_high, col_low], axis=1),
        )
        odd = (corr_row + corr_col + (row_offset + col_offset + 2 * REACH)) & 1
        parity = 1.0 - 2.0 * odd.astype(f32)
        weights = []
        for i in range(nodes):
            here = correlation[i * PADDED : (i + 1) * PADDED] - corners[i : i + 1] * parity
            weights.append(jnp.where(inside, jnp.exp(here * scales[i : i + 1]), 0.0))
        high, low = split(jnp.concatenate(weights, axis=0))
        shifts = (lax.rem(gather_lane, PADDED) - HALF + row_offset).astype(f32)
        gather = jnp.where(gather_sub < nodes, 1.0, shifts)
        block = gather_lane // PADDED == lax.rem(gather_sub, nodes)
        gather = jnp.where(block, gather, 0.0).astype(bf16)
        sums = mm(
            jnp.concatenate([gather, gather], axis=1), jnp.concatenate([high, low], axis=0)
        )
        plain = sums[:nodes]
        across = lax.broadcasted_iota(jnp.int32, (nodes, PADDED), 1) - HALF + col_offset
        inverse = 1.0 / jnp.sum(plain, axis=1, keepdims=True)
        flow_row = jnp.sum(sums[nodes:], axis=1, keepdims=True) * inverse
        flow_col = jnp.sum(plain * across.astype(f32), axis=1, keepdims=True) * inverse
        line_row = jnp.sum(jnp.where(diagonal, flow_row, 0.0), axis=0, keepdims=True)
        line_col = jnp.sum(jnp.where(diagonal, flow_col, 0.0), axis=0, keepdims=True)
        tile = jnp.where(sub == row, line_row, 0.0)
        return jnp.where(sub == row + per_section, line_col, tile)

    def flow_copy(phase, ahead, step):
        part = 1 - phase
        slot = 1 - ahead
        return pltpu.make_async_remote_copy(
            src_ref=flow_tile.at[phase],
            dst_ref=flow_slots.at[slot, part, row],
            send_sem=flow_send.at[phase, ahead, step],
            recv_sem=flow_recv.at[slot, part, row],
            device_id={"tile": device(group + phase + ahead, mate(step))},
            device_id_type=MESH,
        )

    def each_flow(phase, act):
        for step in range(1 - phase, per_section):
            act(flow_copy(phase, 0, step))

        @pl.when(group + phase + 1 < SECTIONS)
        def _():
            for step in range(per_section):
                act(flow_copy(phase, 1, step))

    def take(slots, sems, *where):
        buffer = slots.at[where]
        pltpu.make_async_copy(buffer, buffer, sems.at[where]).wait()

    def masks(slot):
        for step in range(slot, per_section):
            take(mask_slots, mask_recv, slot, mate(step))

    def gathered(slot):
        masks(slot)
        flow = jnp.zeros(shape, f32)
        mask = jnp.zeros(shape, f32)
        for part in range(2):
            for step in range(1 if slot == 1 and part == 1 else 0, per_section):
                take(flow_slots, flow_recv, slot, part, mate(step))
            for line in range(per_section):
                flow = flow + flow_slots[slot, part, line]
        for line in range(per_section):
            mask = mask + mask_slots[slot, line]
        return relax(flow, mask)

    @pl.when(group == SECTIONS - 1)
    def _():

        @pl.when(wrapped)
        def _():
            pl.semaphore_wait(go_sem, 1)
            start_bulk(0, relayed[0])


    @pl.when(group >= 1)
    def _():
        for q in range(chunks):
            arrived(0, q)
            for i, found in enumerate(spectra(prev_raw[q], 1, q * pair)):
                down_cross[q * pair + i] = cross(own(q * pair + i), found)

        @pl.when(jnp.logical_and(group == 2, wrapped))
        def _():
            start_bulk(1, relayed[1])

        @pl.when(jnp.logical_and(group == SECTIONS - 1, jnp.logical_not(wrapped)))
        def _():
            for k in range(relayed[1]):
                forward(1, k)


        @pl.when(group >= 2)
        def _():
            shift_ref[0] = gathered(0)

        tile = flows(group, down_cross, 0, 1, shift_ref[0])
        flow_tile[0] = tile
        flow_slots[1, 1, row] = tile
        each_flow(0, lambda copy: copy.start())

    @pl.when(group < SECTIONS - 1)
    def _():
        for q in range(chunks):
            arrived(1, q)
            for i, found in enumerate(spectra(next_raw[q], 2, q * pair)):
                up_cross[q * pair + i] = cross(found, own(q * pair + i))

    @pl.when(group >= 1)
    def _():
        shift_ref[1] = gathered(1)

    @pl.when(group < SECTIONS - 1)
    def _():
        flow_tile[1] = flows(group + 1, up_cross, 2, 0, shift_ref[1])
        each_flow(1, lambda copy: copy.start())

        @pl.when(jnp.logical_and(group == 0, jnp.logical_not(wrapped)))
        def _():
            pl.delay(REST)
            for k in range(relayed[0]):
                forward(0, k)

        @pl.when(jnp.logical_and(group == 0, wrapped))
        def _():
            release()

    home = shift_ref[1]
    lines = [
        jnp.sum(jnp.where(sub == row + which * per_section, home, 0.0), axis=0, keepdims=True)
        for which in range(2)
    ]
    for which in range(2):
        node_ref[which] = lines[which][:, :grid_cols]
    rows = kernel_rows(term_rows(lines[0], lines[1]), warp_tables[...], patches)
    corner = rows[2] * check[:, 0:1]
    for k in range(PIECES):
        for j in range(piece // PATCH):
            i = k * (piece // PATCH) + j
            moved = warp_patch(part(i), rows[0][i : i + 1], rows[1][i : i + 1])
            out[:, i * PATCH : (i + 1) * PATCH] = (
                moved - corner[i : i + 1] * parity_ref[...]
            ).astype(bf16)

    @pl.when(group == 0)
    def _():
        masks(1)

    @pl.when(group == 1)
    def _():
        masks(0)

    for step in range(1, per_section):
        mask_copy(0, step).wait_send()

    @pl.when(group < SECTIONS - 1)
    def _():
        for step in range(per_section):
            mask_copy(1, step).wait_send()

        end_bulk(1)
        each_flow(1, lambda copy: copy.wait_send())

    @pl.when(group >= 1)
    def _():
        each_flow(0, lambda copy: copy.wait_send())

    @pl.when(group >= 1)
    def _():
        end_bulk(0)

    for way, section in ((0, 0), (1, SECTIONS - 1)):

        @pl.when(jnp.logical_and(group == section, jnp.logical_not(wrapped)))
        def _():
            for k in range(relayed[way]):
                onward(way, k).wait_send()


def store_kernel(aligned, shift, out, shift_out, sems):
    stores = [
        pltpu.make_async_copy(shift, shift_out, sems.at[0]),
        pltpu.make_async_copy(aligned, out, sems.at[1]),
    ]
    for copy in stores:
        copy.start()
    for copy in stores:
        copy.wait()


def shards(tile_count, sections, valid_mask, coarse_offsets):
    per_section = tile_count // SECTIONS
    grid_cols = valid_mask.shape[1]
    width = CHUNK * PATCH
    chunks = sections.shape[1] // (2 * width)
    nodes = chunks * CHUNK
    tile_shape = (2 * per_section, LANES)
    vmem = pl.BlockSpec(memory_space=pltpu.VMEM)
    left, right, window, warp_tables, parity = constants()
    hbm = pl.BlockSpec(memory_space=pltpu.HBM)
    raw = pltpu.VMEM((chunks, PATCH, width), bf16)
    spectrum = pltpu.VMEM((nodes, PATCH, PATCH), f32)
    crossed = pltpu.VMEM((nodes, PATCH, 2 * PATCH), bf16)
    dma = pltpu.SemaphoreType.DMA
    patches = sections.shape[1] // PATCH
    pieces = pltpu.VMEM((PIECES, PATCH, sections.shape[1] // PIECES), bf16)
    aligned, shift = pl.pallas_call(
        functools.partial(chain_kernel, tile_count, grid_cols),
        out_shape=(
            pltpu.VMEM(sections.shape, bf16),
            pltpu.VMEM((2, 1, grid_cols), f32),
        ),
        in_specs=[hbm] * 8,
        out_specs=(vmem, vmem),
        scratch_shapes=[
            pltpu.VMEM(left.shape, bf16),
            pltpu.VMEM(right.shape, bf16),
            pltpu.VMEM(window.shape, f32),
            pltpu.VMEM(warp_tables.shape, f32),
            pltpu.VMEM(parity.shape, f32),
            pieces,
            pltpu.VMEM((patches, LANES), f32),
            pltpu.SMEM(coarse_offsets.shape[::-1], jnp.int32),
            pltpu.VMEM(valid_mask.shape, jnp.int32),
            dma((7 + chunks + PIECES,)),
            raw,
            raw,
            raw,
            spectrum,
            spectrum,
            crossed,
            crossed,
            pltpu.VMEM((3, 3, nodes, LANES), f32),
            pltpu.VMEM(tile_shape, f32),
            pltpu.VMEM((2, per_section) + tile_shape, f32),
            pltpu.VMEM((2,) + tile_shape, f32),
            pltpu.VMEM((2, 2, per_section) + tile_shape, f32),
            pltpu.VMEM((2,) + tile_shape, f32),
            dma((2, chunks)),
            dma((2, chunks)),
            dma((2, per_section)),
            dma((2, per_section)),
            dma((2, 2, per_section)),
            dma((2, 2, per_section)),
            pltpu.SemaphoreType.REGULAR,
            pltpu.SemaphoreType.REGULAR,
            raw,
            dma((chunks,)),
            dma((chunks,)),
        ],
        compiler_params=pltpu.CompilerParams(
            collective_id=0, has_side_effects=True
        ),
        name="chain",
    )(coarse_offsets.T, valid_mask, left, right, window, warp_tables, parity, sections)
    return pl.pallas_call(
        store_kernel,
        out_shape=(
            jax.ShapeDtypeStruct(sections.shape, bf16),
            jax.ShapeDtypeStruct((2, 1, grid_cols), f32),
        ),
        in_specs=[vmem, vmem],
        out_specs=(hbm, hbm),
        scratch_shapes=[dma((2,))],
        name="store",
    )(*[pltpu.with_memory_space_constraint(x, pltpu.VMEM) for x in (aligned, shift)])


def solution(mesh):
    placed = (P(("parts", "tile"), None), P(("parts", "tile"), None), P("parts", None))
    return jax.shard_map(
        functools.partial(shards, mesh.shape["tile"]),
        mesh=mesh,
        in_specs=placed,
        out_specs=(P(("parts", "tile"), None), P(None, ("parts", "tile"), None)),
        check_vma=False,
    )
```

```python
import functools

import jax
import jax.numpy as jnp
import numpy as np
from jax import lax
from jax.experimental import pallas as pl
from jax.experimental.pallas import tpu as pltpu
from jax.sharding import PartitionSpec as P

SECTIONS = 4
PATCH = 128
HALF = 4
SWEEPS = 3
REACH = 3
WINDOW = 2 * HALF + 1
PADDED = 16
LANES = 128
CHUNK = 2
SPAN = 24
HUB = 2
REST = 1700
PIECES = 2

sharpness = 12.0
anchor_weight = 2.0
MESH = pl.DeviceIdType.MESH
f32 = jnp.float32
bf16 = jnp.bfloat16


def split(value):
    high = value.astype(bf16)
    return high, (value - high.astype(f32)).astype(bf16)


def mm(a, b):
    return jnp.dot(a, b, preferred_element_type=f32)


def mm_nt(a, b):
    return lax.dot_general(a, b, (((1,), (1,)), ((), ())), preferred_element_type=f32)


def constants():
    n = PATCH
    k = np.arange(n)
    angle = 2 * np.pi * ((k[:, None] * k[None, :]) % n) / n
    cosine, sine = np.cos(angle), np.sin(angle)
    left = []
    for table in (cosine, sine):
        high = np.asarray(table, bf16)
        low = np.asarray(table - high.astype(np.float64), bf16)
        left.append(np.concatenate([high, low], axis=1))
    left = np.concatenate(left, axis=0)
    right = np.block([[cosine, -sine], [-sine, -cosine]])
    right = np.asarray(right, bf16)
    u = np.arange(-HALF - REACH, -HALF - REACH + SPAN)
    window_angle = 2 * np.pi * ((u[:, None] * k[None, :]) % n) / n
    window = np.stack([np.cos(window_angle), np.sin(window_angle)])
    window = window.astype(np.float32)
    half_angle = np.pi * k / n
    sign = 1.0 - 2.0 * (k % 2)
    warp = np.zeros((8, n), np.float32)
    warp[:4] = np.stack([np.sin(half_angle), np.cos(half_angle), sign, k])
    parity = (sign[:, None] * sign[None, :]).astype(np.float32)
    tables = np.concatenate([window[0], window[1], warp, parity], axis=0)
    return np.stack([left, right]), tables


def turn(value):
    small = (value - jnp.round(value)) * np.pi
    square = small * small
    sine = small * (1.0 + square * (-1 / 6 + square * (1 / 120 + square * (
        -1 / 5040 + square * (1 / 362880 - square * (1 / 39916800))))))
    cosine = 1.0 + square * (-1 / 2 + square * (1 / 24 + square * (-1 / 720 + square * (
        1 / 40320 + square * (-1 / 3628800 + square * (1 / 479001600))))))
    return 1.0 - 2.0 * (sine * sine), 2.0 * (sine * cosine)


def shift_terms(d):
    whole = jnp.round(d)
    frac = d - whole
    odd = jnp.abs(whole - 2.0 * jnp.round(whole * 0.5))
    sine = jnp.sin(jnp.pi * frac)
    signed = jnp.where(odd > 0.5, -sine, sine) * (1.0 / PATCH)
    angle = d * (np.pi / PATCH)
    tangent = jnp.sin(angle) / jnp.cos(angle)
    small = frac * (np.pi / PATCH)
    tiny = jnp.abs(frac) < 1e-6
    peak = jnp.where(
        tiny, 1.0, sine * jnp.cos(small) / jnp.where(tiny, 1.0, PATCH * jnp.sin(small))
    )
    return tangent, signed, peak, whole


def kernel_rows(terms, tables, patches):
    columns = jnp.transpose(terms)[:patches]
    sine, cosine, parity, gap = [tables[i : i + 1, :] for i in range(4)]
    found = []
    for base, forward in ((0, False), (4, True)):
        tangent, signed, peak, whole = [columns[:, base + i : base + i + 1] for i in range(4)]
        if forward:
            bottom = cosine * tangent + sine
            top = cosine - sine * tangent
            centre = jnp.where(whole > 0, PATCH - whole, -whole)
        else:
            bottom = cosine * tangent - sine
            top = cosine + sine * tangent
            centre = jnp.where(whole < 0, whole + PATCH, whole)
        found.append(jnp.where(gap == centre, peak, (signed * parity) * (top / bottom)))
    corner = columns[:, 1:2] * columns[:, 5:6]
    return found[0], found[1], corner


def circulant(row):
    spread = jnp.broadcast_to(row, (PATCH, PATCH))
    return split(pltpu.roll(spread, 0, 1, stride=1, stride_axis=0))


def warp_patch(patch, left_row, right_row):
    left = circulant(left_row)
    right = circulant(right_row)
    both = mm(patch, jnp.concatenate(right, axis=1))
    high, low = split(both[:, :PATCH] + both[:, PATCH:])
    lower = jnp.concatenate([high, jnp.zeros_like(low)], axis=1)
    inner = jnp.concatenate([jnp.concatenate([high, low], axis=1), lower], axis=0)
    moved = mm(jnp.concatenate(left, axis=1), inner)
    return moved[:, :PATCH] + moved[:, PATCH:]


def term_rows(d_rows, d_cols):
    both = jnp.concatenate([d_rows, d_cols], axis=0)
    tangent, signed, peak, whole = shift_terms(both)
    pieces = [t[i : i + 1] for i in range(2) for t in (tangent, signed, peak, whole)]
    return jnp.concatenate(pieces, axis=0)


def chain_kernel(
    tile_count,
    grid_cols,
    offsets_in,
    mask_in,
    dft_in,
    tables_in,
    strip,
    out,
    node_ref,
    dft_ref,
    tables,
    whole,
    check,
    offsets,
    mask_ref,
    load_sem,
    prev_raw,
    next_raw,
    own_re,
    own_im,
    down_cross,
    up_cross,
    stats,
    mask_tile,
    mask_slots,
    flow_tile,
    flow_slots,
    shift_ref,
    bulk_send,
    bulk_recv,
    mask_send,
    mask_recv,
    flow_send,
    flow_recv,
    go_sem,
    all_sem,
    relay_raw,
    relay_send,
    relay_recv,
):
    per_section = tile_count // SECTIONS
    me = lax.axis_index("tile")
    lead = per_section // 2
    rotated = lax.rem(me + tile_count - lead, tile_count)
    group = rotated // per_section
    row = lax.rem(rotated, per_section)
    chunks, width = prev_raw.shape[0], prev_raw.shape[2]
    pair = width // PATCH
    nodes = chunks * pair
    half = lax.rem(group, 2)
    base = half * nodes
    piece = whole.shape[2]
    patches = PIECES * piece // PATCH

    def device(section, line):
        return lax.rem(section * per_section + line + lead, tile_count)

    def mate(line_step):
        return lax.rem(row + line_step, per_section)

    barrier = pltpu.get_barrier_semaphore()

    def signal(sem, section, line):
        pl.semaphore_signal(
            sem, inc=1, device_id={"tile": device(section, line)}, device_id_type=MESH
        )

    @pl.when(group <= 1)
    def _():
        signal(barrier, 1 - group, row)

    @pl.when(group == HUB)
    def _():
        signal(barrier, SECTIONS - 1, row)
        for step in range(1, per_section):
            signal(barrier, HUB, mate(step))

    @pl.when(group != HUB)
    def _():
        for step in range(per_section):
            signal(barrier, HUB, mate(step))

    def columns(side, chunk):
        start = pl.multiple_of((side * chunks + chunk) * width, LANES)
        return strip.at[:, pl.ds(start, width)]

    def strip_half(side):
        return strip.at[:, pl.ds(pl.multiple_of(side * piece, LANES), piece)]

    loads = [
        pltpu.make_async_copy(source, target, load_sem.at[i])
        for i, (source, target) in enumerate(
            [(mask_in, mask_ref), (offsets_in, offsets), (dft_in, dft_ref), (tables_in, tables)]
            + [(strip_half(side), whole.at[side]) for side in (half, 1 - half)]
        )
    ]
    for copy in loads:
        copy.start()
    pl.semaphore_wait(barrier, jnp.where(group == HUB, tile_count - 1, 1))

    def bulk(way, chunk):
        peer = lax.rem(me + (per_section if way else tile_count - per_section), tile_count)
        return pltpu.make_async_remote_copy(
            src_ref=columns(1 - half, chunk),
            dst_ref=(prev_raw if way else next_raw).at[chunk],
            send_sem=bulk_send.at[way],
            recv_sem=bulk_recv.at[1 - way, chunk],
            device_id={"tile": peer},
            device_id_type=MESH,
        )

    def start_bulk(way, first=0, last=chunks):
        for chunk in range(first, last):
            bulk(way, chunk).start()

    relayed = (chunks // 2, chunks // 2)
    apart = per_section - per_section // 2
    wrapped = row >= apart

    def detour(way):
        for k in range(relayed[way]):
            pltpu.make_async_remote_copy(
                src_ref=columns(1 - half, k),
                dst_ref=relay_raw.at[k],
                send_sem=bulk_send.at[way],
                recv_sem=relay_recv,
                device_id={"tile": device(SECTIONS - 1 if way else 0, row - apart)},
                device_id_type=MESH,
            ).start()

    def onward(way, k):
        return pltpu.make_async_remote_copy(
            src_ref=relay_raw.at[k],
            dst_ref=(prev_raw if way else next_raw).at[k],
            send_sem=relay_send,
            recv_sem=bulk_recv.at[1 - way, k],
            device_id={"tile": device(SECTIONS - 1 if way else 2, row + apart)},
            device_id_type=MESH,
        )

    def forward(way):
        arrival = relay_raw.at[pl.ds(0, relayed[way])]
        pltpu.make_async_copy(arrival, arrival, relay_recv).wait()
        for k in range(relayed[way]):
            onward(way, k).start()

    def release():
        signal(go_sem, SECTIONS - 1, row)

    @pl.when(group == HUB)
    def _():
        for section in range(SECTIONS):
            if section != HUB:
                signal(all_sem, section, row)

    @pl.when(jnp.logical_or(group == 1, group == 2))
    def _():
        start_bulk(0)

    @pl.when(group == 0)
    def _():
        start_bulk(1)

    for way in range(2):

        @pl.when(jnp.logical_and(group == SECTIONS - 1 - way, jnp.logical_not(wrapped)))
        def _():
            start_bulk(way)

    def mask_copy(ahead, step):
        return pltpu.make_async_remote_copy(
            src_ref=mask_tile,
            dst_ref=mask_slots.at[1 - ahead, row],
            send_sem=mask_send.at[ahead],
            recv_sem=mask_recv.at[1 - ahead],
            device_id={"tile": device(group + ahead, mate(step))},
            device_id_type=MESH,
        )

    loads[0].wait()
    shape = (2 * per_section, LANES)
    sub = lax.broadcasted_iota(jnp.int32, shape, 0)
    lane = lax.broadcasted_iota(jnp.int32, shape, 1)
    sub_row = lax.rem(sub, per_section)
    mask_tile[...] = jnp.zeros((1, LANES), f32)
    mask_tile[:, 0:grid_cols] = mask_ref[...].astype(f32)
    mask_slots[1, row] = mask_tile[...]
    shift_ref[...] = jnp.zeros((2,) + shape, f32)

    for copy in loads[1:-1]:
        copy.wait()

    eight = lax.broadcasted_iota(jnp.int32, (8, LANES), 0)

    def spectra(pixels, kind, first_node):
        table = dft_ref[0]
        first = mm(table, jnp.concatenate([pixels, pixels], axis=0))
        found = []
        for i in range(pair):
            s = slice(i * PATCH, (i + 1) * PATCH)
            level = jnp.sum(first[0:1, s], axis=1, keepdims=True) * (1.0 / PATCH)
            top = jnp.where(eight == 0, first[0:8, s] - level, first[0:8, s])
            body = jnp.concatenate([top, first[8:PATCH, s]], axis=0)
            halves = jnp.concatenate([body, first[PATCH:, s]], axis=1).astype(bf16)
            both = mm(halves, dft_ref[1])
            real, imag = both[:, :PATCH], both[:, PATCH:]
            energy = real * real + imag * imag
            middle = slice(PATCH // 2, PATCH // 2 + 1)
            node = first_node + i
            stats[kind, 0, node : node + 1] = jnp.sum(energy, axis=0, keepdims=True)
            stats[kind, 1, node : node + 1] = energy[middle]
            stats[kind, 2, node : node + 1] = real[middle]
            found.append((real, imag))
        return found

    def cross(a, b):
        real = a[0] * b[0] + a[1] * b[1]
        imag = a[1] * b[0] - a[0] * b[1]
        return jnp.concatenate([real, imag], axis=1).astype(bf16)

    for q in range(chunks):
        for i, (real, imag) in enumerate(spectra(whole[half, :, q * width : (q + 1) * width], 0, q * pair)):
            own_re[q * pair + i] = real
            own_im[q * pair + i] = imag

    def part(i):
        k, j = divmod(i, piece // PATCH)
        return whole[k, :, j * PATCH : (j + 1) * PATCH]

    loads[-1].wait()
    for i in range(patches):
        check[i : i + 1] = jnp.sum(part(i).astype(f32) * tables[2 * SPAN + 8 :], axis=0, keepdims=True)
    sums = jnp.sum(check[...], axis=1, keepdims=True)
    check[...] = jnp.broadcast_to(sums, check.shape)

    @pl.when(group != HUB)
    def _():
        pl.semaphore_wait(all_sem, 1)

    for step in range(1, per_section):
        mask_copy(0, step).start()

    @pl.when(group < SECTIONS - 1)
    def _():
        for step in range(per_section):
            mask_copy(1, step).start()

    @pl.when(group == 1)
    def _():
        start_bulk(1)

    for way in range(2):

        @pl.when(jnp.logical_and(group == SECTIONS - 1 - way, wrapped))
        def _():
            detour(way)

    def arrived(way, chunk):
        buffer = (next_raw if way else prev_raw).at[chunk]
        pltpu.make_async_copy(buffer, buffer, bulk_recv.at[way, chunk]).wait()

    def own(node):
        return own_re[node], own_im[node]

    up_ok = (sub_row > 0).astype(f32)
    down_ok = (sub_row < per_section - 1).astype(f32)
    left_ok = jnp.logical_and(lane > 0, lane < grid_cols).astype(f32)
    right_ok = (lane < grid_cols - 1).astype(f32)
    count = up_ok + down_ok + left_ok + right_ok

    def relax(flow, mask):
        weight = anchor_weight * mask
        pull = weight * flow
        scale = 1.0 / (weight + count)
        d = flow * mask
        for _ in range(SWEEPS):
            near = (
                up_ok * pltpu.roll(d, 1, 0)
                + down_ok * pltpu.roll(d, 2 * per_section - 1, 0)
                + left_ok * pltpu.roll(d, 1, 1)
                + right_ok * pltpu.roll(d, LANES - 1, 1)
            )
            d = (pull + near) * scale
        return jnp.where(lane < grid_cols, d, 0.0)

    node_sub = lax.broadcasted_iota(jnp.int32, (nodes, LANES), 0)
    node_lane = lax.broadcasted_iota(jnp.int32, (nodes, LANES), 1)
    diagonal = node_lane == base + node_sub
    nyquist = node_lane == PATCH // 2
    frequency = jnp.where(node_lane < PATCH // 2, node_lane, node_lane - PATCH).astype(f32)
    frequency = frequency * (1.0 / PATCH)
    corr_row = lax.broadcasted_iota(jnp.int32, (PADDED, PADDED), 0)
    corr_col = lax.broadcasted_iota(jnp.int32, (PADDED, PADDED), 1)
    inside = jnp.logical_and(corr_row < WINDOW, corr_col < WINDOW)
    gather_sub = lax.broadcasted_iota(jnp.int32, (2 * nodes, nodes * PADDED), 0)
    gather_lane = lax.broadcasted_iota(jnp.int32, (2 * nodes, nodes * PADDED), 1)
    middle = slice(PATCH // 2, PATCH // 2 + 1)

    def column(d, which):
        line = jnp.sum(jnp.where(sub == row + which * per_section, d, 0.0), axis=0, keepdims=True)
        return jnp.sum(jnp.where(diagonal, line, 0.0), axis=1, keepdims=True)

    def flows(section, crosses, kind_a, kind_b, d):
        row_offset = offsets[0, section]
        col_offset = offsets[1, section]
        turned = []
        for which in range(2):
            cosine, sine = turn(frequency * column(d, which))
            turned.append((cosine, jnp.where(nyquist, 0.0, sine), cosine[:, middle], sine[:, middle]))
        (cos_y, sin_y, end_cy, end_sy), (cos_x, sin_x, end_cx, end_sx) = turned
        total_a = jnp.sum(stats[kind_a, 0], axis=1, keepdims=True)
        edge_col = stats[kind_b, 0]
        total_b = jnp.sum(edge_col, axis=1, keepdims=True)
        edge_row = jnp.sum(stats[kind_b, 1], axis=1, keepdims=True)
        tip_a = stats[kind_a, 2][:, middle]
        tip_b = stats[kind_b, 2][:, middle]
        tip = tip_b * tip_b
        end_both = end_cy * end_cx - end_sy * end_sx
        lost = (
            (edge_row - tip) * (end_sy * end_sy)
            + (edge_col[:, middle] - tip) * (end_sx * end_sx)
            + tip * (1.0 - end_both * end_both)
        )
        size = 1.0 / float(PATCH) ** 4
        variance_a = total_a * size + 1e-05
        variance_b = jnp.maximum((total_b - lost) * size, 0.0) + 1e-05
        scales = (sharpness * size) * lax.rsqrt(variance_a * variance_b)
        corners = end_sy * end_sx * tip_a * tip_b
        row_cos = tables[pl.ds(row_offset + REACH, PADDED), :]
        row_sin = tables[pl.ds(row_offset + REACH + SPAN, PADDED), :]
        col_cos = tables[pl.ds(col_offset + REACH, PADDED), :]
        col_sin = tables[pl.ds(col_offset + REACH + SPAN, PADDED), :]
        col_high, col_low = split(jnp.concatenate([col_cos, -col_sin], axis=1))
        moved = []
        for i in range(nodes):
            c, s = cos_y[i : i + 1], sin_y[i : i + 1]
            table = jnp.concatenate(
                [row_cos * c + row_sin * s, row_sin * c - row_cos * s], axis=0
            )
            parts = mm(jnp.concatenate(split(table), axis=0), crosses[i])
            parts = parts[: 2 * PADDED] + parts[2 * PADDED :]
            real = parts[:PADDED, :PATCH] - parts[PADDED:, PATCH:]
            imag = parts[:PADDED, PATCH:] + parts[PADDED:, :PATCH]
            c, s = cos_x[i : i + 1], sin_x[i : i + 1]
            moved.append(
                jnp.concatenate([real * c + imag * s, imag * c - real * s], axis=1)
            )
        high, low = split(jnp.concatenate(moved, axis=0))
        correlation = mm_nt(
            jnp.concatenate([high, low, high], axis=1),
            jnp.concatenate([col_high, col_high, col_low], axis=1),
        )
        odd = (corr_row + corr_col + (row_offset + col_offset + 2 * REACH)) & 1
        parity = 1.0 - 2.0 * odd.astype(f32)
        weights = []
        for i in range(nodes):
            here = correlation[i * PADDED : (i + 1) * PADDED] - corners[i : i + 1] * parity
            weights.append(jnp.where(inside, jnp.exp(here * scales[i : i + 1]), 0.0))
        high, low = split(jnp.concatenate(weights, axis=0))
        shifts = (lax.rem(gather_lane, PADDED) - HALF + row_offset).astype(f32)
        gather = jnp.where(gather_sub < nodes, 1.0, shifts)
        block = gather_lane // PADDED == lax.rem(gather_sub, nodes)
        gather = jnp.where(block, gather, 0.0).astype(bf16)
        sums = mm(
            jnp.concatenate([gather, gather], axis=1), jnp.concatenate([high, low], axis=0)
        )
        plain = sums[:nodes]
        across = lax.broadcasted_iota(jnp.int32, (nodes, PADDED), 1) - HALF + col_offset
        inverse = 1.0 / jnp.sum(plain, axis=1, keepdims=True)
        flow_row = jnp.sum(sums[nodes:], axis=1, keepdims=True) * inverse
        flow_col = jnp.sum(plain * across.astype(f32), axis=1, keepdims=True) * inverse
        line_row = jnp.sum(jnp.where(diagonal, flow_row, 0.0), axis=0, keepdims=True)
        line_col = jnp.sum(jnp.where(diagonal, flow_col, 0.0), axis=0, keepdims=True)
        return line_row, line_col

    def flow_copy(phase, ahead, step):
        part = 1 - phase
        slot = 1 - ahead
        return pltpu.make_async_remote_copy(
            src_ref=flow_tile.at[phase],
            dst_ref=flow_slots.at[slot, part * per_section + row],
            send_sem=flow_send.at[phase, ahead],
            recv_sem=flow_recv.at[slot],
            device_id={"tile": device(group + phase + ahead, mate(step))},
            device_id_type=MESH,
        )

    def send_flow(phase, tile):
        for which in range(2):
            flow_tile[phase, which : which + 1] = tile[which]
            if phase == 0:
                flow_slots[1, per_section + row, which : which + 1] = tile[which]
        for step in range(1 - phase, per_section):
            flow_copy(phase, 0, step).start()

        @pl.when(group + phase + 1 < SECTIONS)
        def _():
            for step in range(per_section):
                flow_copy(phase, 1, step).start()

    def drain(ref, sem):
        pltpu.make_async_copy(ref, ref, sem).wait()

    def end_flow(phase):
        drain(flow_slots.at[0, pl.ds(0, per_section - 1 + phase)], flow_send.at[phase, 0])

        @pl.when(group + phase + 1 < SECTIONS)
        def _():
            drain(flow_slots.at[0, pl.ds(0, per_section)], flow_send.at[phase, 1])

    def masks(slot):
        drain(mask_slots.at[slot, pl.ds(0, per_section - slot)], mask_recv.at[slot])

    def gathered(slot):
        masks(slot)
        drain(flow_slots.at[slot, pl.ds(0, 2 * per_section - slot)], flow_recv.at[slot])
        flow = jnp.zeros(shape, f32)
        mask = jnp.zeros(shape, f32)
        for line in range(per_section):
            both = flow_slots[slot, line] + flow_slots[slot, per_section + line]
            flow = jnp.where(sub == line, both[0:1], flow)
            flow = jnp.where(sub == line + per_section, both[1:2], flow)
            mask = jnp.where(sub_row == line, mask_slots[slot, line], mask)
        return relax(flow, mask)

    @pl.when(group == SECTIONS - 1)
    def _():

        @pl.when(wrapped)
        def _():
            pl.semaphore_wait(go_sem, 1)
            start_bulk(0, relayed[0])


    @pl.when(group >= 1)
    def _():
        for q in range(chunks):
            arrived(0, q)
            for i, found in enumerate(spectra(prev_raw[q], 1, q * pair)):
                down_cross[q * pair + i] = cross(own(q * pair + i), found)

        @pl.when(jnp.logical_and(group == 2, wrapped))
        def _():
            start_bulk(1, relayed[1])

        @pl.when(jnp.logical_and(group == SECTIONS - 1, jnp.logical_not(wrapped)))
        def _():
            forward(1)


        @pl.when(group >= 2)
        def _():
            shift_ref[0] = gathered(0)

        send_flow(0, flows(group, down_cross, 0, 1, shift_ref[0]))

    @pl.when(group < SECTIONS - 1)
    def _():
        for q in range(chunks):
            arrived(1, q)
            for i, found in enumerate(spectra(next_raw[q], 2, q * pair)):
                up_cross[q * pair + i] = cross(found, own(q * pair + i))

    @pl.when(group >= 1)
    def _():
        shift_ref[1] = gathered(1)

    @pl.when(group < SECTIONS - 1)
    def _():
        send_flow(1, flows(group + 1, up_cross, 2, 0, shift_ref[1]))

        @pl.when(jnp.logical_and(group == 0, jnp.logical_not(wrapped)))
        def _():
            pl.delay(REST)
            forward(0)

        @pl.when(jnp.logical_and(group == 0, wrapped))
        def _():
            release()

    home = shift_ref[1]
    lines = [
        jnp.sum(jnp.where(sub == row + which * per_section, home, 0.0), axis=0, keepdims=True)
        for which in range(2)
    ]
    for which in range(2):
        node_ref[which] = lines[which][:, :grid_cols]
    rows = kernel_rows(term_rows(lines[0], lines[1]), tables[2 * SPAN : 2 * SPAN + 8], patches)
    corner = rows[2] * check[:, 0:1]
    for k in range(PIECES):
        for j in range(piece // PATCH):
            i = k * (piece // PATCH) + j
            moved = warp_patch(part(i), rows[0][i : i + 1], rows[1][i : i + 1])
            out[:, i * PATCH : (i + 1) * PATCH] = (
                moved - corner[i : i + 1] * tables[2 * SPAN + 8 :]
            ).astype(bf16)

    @pl.when(group == 0)
    def _():
        masks(1)

    @pl.when(group == 1)
    def _():
        masks(0)

    drain(mask_slots.at[1, pl.ds(0, per_section - 1)], mask_send.at[0])

    @pl.when(group < SECTIONS - 1)
    def _():
        drain(mask_slots.at[1, pl.ds(0, per_section)], mask_send.at[1])
        drain(next_raw, bulk_send.at[1])
        end_flow(1)

    @pl.when(group >= 1)
    def _():
        drain(prev_raw, bulk_send.at[0])
        end_flow(0)

    for way, section in ((0, 0), (1, SECTIONS - 1)):

        @pl.when(jnp.logical_and(group == section, jnp.logical_not(wrapped)))
        def _():
            drain(relay_raw.at[pl.ds(0, relayed[way])], relay_send)


def store_kernel(aligned, shift, out, shift_out, sems):
    stores = [
        pltpu.make_async_copy(shift, shift_out, sems.at[0]),
        pltpu.make_async_copy(aligned, out, sems.at[1]),
    ]
    for copy in stores:
        copy.start()
    for copy in stores:
        copy.wait()


def shards(tile_count, sections, valid_mask, coarse_offsets):
    per_section = tile_count // SECTIONS
    grid_cols = valid_mask.shape[1]
    width = CHUNK * PATCH
    chunks = sections.shape[1] // (2 * width)
    nodes = chunks * CHUNK
    tile_shape = (2 * per_section, LANES)
    vmem = pl.BlockSpec(memory_space=pltpu.VMEM)
    dft, tables = constants()
    hbm = pl.BlockSpec(memory_space=pltpu.HBM)
    raw = pltpu.VMEM((chunks, PATCH, width), bf16)
    spectrum = pltpu.VMEM((nodes, PATCH, PATCH), f32)
    crossed = pltpu.VMEM((nodes, PATCH, 2 * PATCH), bf16)
    dma = pltpu.SemaphoreType.DMA
    patches = sections.shape[1] // PATCH
    pieces = pltpu.VMEM((PIECES, PATCH, sections.shape[1] // PIECES), bf16)
    aligned, shift = pl.pallas_call(
        functools.partial(chain_kernel, tile_count, grid_cols),
        out_shape=(
            pltpu.VMEM(sections.shape, bf16),
            pltpu.VMEM((2, 1, grid_cols), f32),
        ),
        in_specs=[hbm] * 5,
        out_specs=(vmem, vmem),
        scratch_shapes=[
            pltpu.VMEM(dft.shape, bf16),
            pltpu.VMEM(tables.shape, f32),
            pieces,
            pltpu.VMEM((patches, LANES), f32),
            pltpu.SMEM(coarse_offsets.shape[::-1], jnp.int32),
            pltpu.VMEM(valid_mask.shape, jnp.int32),
            dma((6,)),
            raw,
            raw,
            spectrum,
            spectrum,
            crossed,
            crossed,
            pltpu.VMEM((3, 3, nodes, LANES), f32),
            pltpu.VMEM((1, LANES), f32),
            pltpu.VMEM((2, per_section, 1, LANES), f32),
            pltpu.VMEM((2, 2, LANES), f32),
            pltpu.VMEM((2, 2 * per_section, 2, LANES), f32),
            pltpu.VMEM((2,) + tile_shape, f32),
            dma((2,)),
            dma((2, chunks)),
            dma((2,)),
            dma((2,)),
            dma((2, 2)),
            dma((2,)),
            pltpu.SemaphoreType.REGULAR,
            pltpu.SemaphoreType.REGULAR,
            pltpu.VMEM((chunks // 2, PATCH, width), bf16),
            dma(()),
            dma(()),
        ],
        compiler_params=pltpu.CompilerParams(
            collective_id=0, has_side_effects=True
        ),
        name="chain",
    )(coarse_offsets.T, valid_mask, dft, tables, sections)
    return pl.pallas_call(
        store_kernel,
        out_shape=(
            jax.ShapeDtypeStruct(sections.shape, bf16),
            jax.ShapeDtypeStruct((2, 1, grid_cols), f32),
        ),
        in_specs=[vmem, vmem],
        out_specs=(hbm, hbm),
        scratch_shapes=[dma((2,))],
        name="store",
    )(*[pltpu.with_memory_space_constraint(x, pltpu.VMEM) for x in (aligned, shift)])


def solution(mesh):
    placed = (P(("parts", "tile"), None), P(("parts", "tile"), None), P("parts", None))
    return jax.shard_map(
        functools.partial(shards, mesh.shape["tile"]),
        mesh=mesh,
        in_specs=placed,
        out_specs=(P(("parts", "tile"), None), P(None, ("parts", "tile"), None)),
        check_vma=False,
    )
```

```python
import functools

import jax
import jax.numpy as jnp
import numpy as np
from jax import lax
from jax.experimental import pallas as pl
from jax.experimental.pallas import tpu as pltpu
from jax.sharding import PartitionSpec as P

SECTIONS = 4
PATCH = 128
HALF = 4
SWEEPS = 3
REACH = 3
WINDOW = 2 * HALF + 1
PADDED = 16
LANES = 128
CHUNK = 2
SPAN = 24
HUB = 2
REST = 1700
PIECES = 2

sharpness = 12.0
anchor_weight = 2.0
MESH = pl.DeviceIdType.MESH
f32 = jnp.float32
bf16 = jnp.bfloat16


def split(value):
    high = value.astype(bf16)
    return high, (value - high.astype(f32)).astype(bf16)


def mm(a, b):
    return jnp.dot(a, b, preferred_element_type=f32)


def mm_nt(a, b):
    return lax.dot_general(a, b, (((1,), (1,)), ((), ())), preferred_element_type=f32)


def constants():
    n = PATCH
    k = np.arange(n)
    angle = 2 * np.pi * ((k[:, None] * k[None, :]) % n) / n
    cosine, sine = np.cos(angle), np.sin(angle)
    left = []
    for table in (cosine, sine):
        high = np.asarray(table, bf16)
        low = np.asarray(table - high.astype(np.float64), bf16)
        left.append(np.concatenate([high, low], axis=1))
    left = np.concatenate(left, axis=0)
    right = np.block([[cosine, -sine], [-sine, -cosine]])
    right = np.asarray(right, bf16)
    u = np.arange(-HALF - REACH, -HALF - REACH + SPAN)
    window_angle = 2 * np.pi * ((u[:, None] * k[None, :]) % n) / n
    window = np.stack([np.cos(window_angle), np.sin(window_angle)])
    window = window.astype(np.float32)
    half_angle = np.pi * k / n
    sign = 1.0 - 2.0 * (k % 2)
    warp = np.zeros((8, n), np.float32)
    warp[:4] = np.stack([np.sin(half_angle), np.cos(half_angle), sign, k])
    parity = (sign[:, None] * sign[None, :]).astype(np.float32)
    tables = np.concatenate([window[0], window[1], warp, parity], axis=0)
    return np.stack([left, right]), tables


def turn(value):
    small = (value - jnp.round(value)) * np.pi
    square = small * small
    sine = small * (1.0 + square * (-1 / 6 + square * (1 / 120 + square * (
        -1 / 5040 + square * (1 / 362880 - square * (1 / 39916800))))))
    cosine = 1.0 + square * (-1 / 2 + square * (1 / 24 + square * (-1 / 720 + square * (
        1 / 40320 + square * (-1 / 3628800 + square * (1 / 479001600))))))
    return 1.0 - 2.0 * (sine * sine), 2.0 * (sine * cosine)


def shift_terms(d):
    whole = jnp.round(d)
    frac = d - whole
    odd = jnp.abs(whole - 2.0 * jnp.round(whole * 0.5))
    sine = jnp.sin(jnp.pi * frac)
    signed = jnp.where(odd > 0.5, -sine, sine) * (1.0 / PATCH)
    angle = d * (np.pi / PATCH)
    tangent = jnp.sin(angle) / jnp.cos(angle)
    small = frac * (np.pi / PATCH)
    tiny = jnp.abs(frac) < 1e-6
    peak = jnp.where(
        tiny, 1.0, sine * jnp.cos(small) / jnp.where(tiny, 1.0, PATCH * jnp.sin(small))
    )
    return tangent, signed, peak, whole


def kernel_rows(terms, tables, patches):
    columns = jnp.transpose(terms)[:patches]
    sine, cosine, parity, gap = [tables[i : i + 1, :] for i in range(4)]
    found = []
    for base, forward in ((0, False), (4, True)):
        tangent, signed, peak, whole = [columns[:, base + i : base + i + 1] for i in range(4)]
        if forward:
            bottom = cosine * tangent + sine
            top = cosine - sine * tangent
            centre = jnp.where(whole > 0, PATCH - whole, -whole)
        else:
            bottom = cosine * tangent - sine
            top = cosine + sine * tangent
            centre = jnp.where(whole < 0, whole + PATCH, whole)
        found.append(jnp.where(gap == centre, peak, (signed * parity) * (top / bottom)))
    corner = columns[:, 1:2] * columns[:, 5:6]
    return found[0], found[1], corner


def circulant(row):
    spread = jnp.broadcast_to(row, (PATCH, PATCH))
    return split(pltpu.roll(spread, 0, 1, stride=1, stride_axis=0))


def warp_patch(patch, left_row, right_row):
    left = circulant(left_row)
    right = circulant(right_row)
    both = mm(patch, jnp.concatenate(right, axis=1))
    high, low = split(both[:, :PATCH] + both[:, PATCH:])
    lower = jnp.concatenate([high, jnp.zeros_like(low)], axis=1)
    inner = jnp.concatenate([jnp.concatenate([high, low], axis=1), lower], axis=0)
    moved = mm(jnp.concatenate(left, axis=1), inner)
    return moved[:, :PATCH] + moved[:, PATCH:]


def term_rows(d_rows, d_cols):
    both = jnp.concatenate([d_rows, d_cols], axis=0)
    tangent, signed, peak, whole = shift_terms(both)
    pieces = [t[i : i + 1] for i in range(2) for t in (tangent, signed, peak, whole)]
    return jnp.concatenate(pieces, axis=0)


def chain_kernel(
    tile_count,
    grid_cols,
    offsets_in,
    mask_in,
    dft_in,
    tables_in,
    strip,
    out,
    node_ref,
    dft_ref,
    tables,
    whole,
    check,
    offsets,
    mask_ref,
    load_sem,
    prev_raw,
    next_raw,
    own_re,
    own_im,
    down_cross,
    up_cross,
    stats,
    mask_tile,
    mask_slots,
    flow_tile,
    flow_slots,
    shift_ref,
    bulk_send,
    bulk_recv,
    mask_send,
    mask_recv,
    flow_send,
    flow_recv,
    go_sem,
    all_sem,
    relay_raw,
    relay_send,
    relay_recv,
):
    per_section = tile_count // SECTIONS
    me = lax.axis_index("tile")
    lead = per_section // 2
    rotated = lax.rem(me + tile_count - lead, tile_count)
    group = rotated // per_section
    row = lax.rem(rotated, per_section)
    chunks, width = prev_raw.shape[0], prev_raw.shape[2]
    pair = width // PATCH
    nodes = chunks * pair
    half = lax.rem(group, 2)
    base = half * nodes
    piece = whole.shape[2]
    patches = PIECES * piece // PATCH

    def device(section, line):
        return lax.rem(section * per_section + line + lead, tile_count)

    def mate(line_step):
        return lax.rem(row + line_step, per_section)

    barrier = pltpu.get_barrier_semaphore()

    def signal(sem, section, line):
        pl.semaphore_signal(
            sem, inc=1, device_id={"tile": device(section, line)}, device_id_type=MESH
        )

    @pl.when(group <= 1)
    def _():
        signal(barrier, 1 - group, row)

    @pl.when(group == HUB)
    def _():
        signal(barrier, SECTIONS - 1, row)
        for step in range(1, per_section):
            signal(barrier, HUB, mate(step))

    @pl.when(group != HUB)
    def _():
        for step in range(per_section):
            signal(barrier, HUB, mate(step))

    def columns(side, chunk):
        start = pl.multiple_of((side * chunks + chunk) * width, LANES)
        return strip.at[:, pl.ds(start, width)]

    def strip_half(side):
        return strip.at[:, pl.ds(pl.multiple_of(side * piece, LANES), piece)]

    loads = [
        pltpu.make_async_copy(source, target, load_sem.at[i])
        for i, (source, target) in enumerate(
            [(mask_in, mask_ref), (offsets_in, offsets), (dft_in, dft_ref), (tables_in, tables)]
            + [(strip_half(side), whole.at[side]) for side in (half, 1 - half)]
        )
    ]
    for copy in loads:
        copy.start()
    pl.semaphore_wait(barrier, jnp.where(group == HUB, tile_count - 1, 1))

    def bulk(way, chunk):
        peer = lax.rem(me + (per_section if way else tile_count - per_section), tile_count)
        return pltpu.make_async_remote_copy(
            src_ref=columns(1 - half, chunk),
            dst_ref=(prev_raw if way else next_raw).at[chunk],
            send_sem=bulk_send.at[way],
            recv_sem=bulk_recv.at[1 - way, chunk],
            device_id={"tile": peer},
            device_id_type=MESH,
        )

    def start_bulk(way, first=0, last=chunks):
        for chunk in range(first, last):
            bulk(way, chunk).start()

    relayed = (chunks // 2, chunks // 2)
    apart = per_section - per_section // 2
    wrapped = row >= apart

    def detour(way):
        for k in range(relayed[way]):
            pltpu.make_async_remote_copy(
                src_ref=columns(1 - half, k),
                dst_ref=relay_raw.at[k],
                send_sem=bulk_send.at[way],
                recv_sem=relay_recv,
                device_id={"tile": device(SECTIONS - 1 if way else 0, row - apart)},
                device_id_type=MESH,
            ).start()

    def onward(way, k):
        return pltpu.make_async_remote_copy(
            src_ref=relay_raw.at[k],
            dst_ref=(prev_raw if way else next_raw).at[k],
            send_sem=relay_send,
            recv_sem=bulk_recv.at[1 - way, k],
            device_id={"tile": device(SECTIONS - 1 if way else 2, row + apart)},
            device_id_type=MESH,
        )

    def forward(way):
        arrival = relay_raw.at[pl.ds(0, relayed[way])]
        pltpu.make_async_copy(arrival, arrival, relay_recv).wait()
        for k in range(relayed[way]):
            onward(way, k).start()

    def release():
        signal(go_sem, SECTIONS - 1, row)

    @pl.when(group == HUB)
    def _():
        for section in range(SECTIONS):
            if section != HUB:
                signal(all_sem, section, row)

    @pl.when(jnp.logical_or(group == 1, group == 2))
    def _():
        start_bulk(0)

    @pl.when(group == 0)
    def _():
        start_bulk(1)

    for way in range(2):

        @pl.when(jnp.logical_and(group == SECTIONS - 1 - way, jnp.logical_not(wrapped)))
        def _():
            start_bulk(way)

    def mask_copy(ahead, step):
        return pltpu.make_async_remote_copy(
            src_ref=mask_tile,
            dst_ref=mask_slots.at[1 - ahead, row],
            send_sem=mask_send.at[ahead],
            recv_sem=mask_recv.at[1 - ahead],
            device_id={"tile": device(group + ahead, mate(step))},
            device_id_type=MESH,
        )

    loads[0].wait()
    shape = (2 * per_section, LANES)
    sub = lax.broadcasted_iota(jnp.int32, shape, 0)
    lane = lax.broadcasted_iota(jnp.int32, shape, 1)
    sub_row = lax.rem(sub, per_section)
    mask_tile[...] = jnp.zeros((1, LANES), f32)
    mask_tile[:, 0:grid_cols] = mask_ref[...].astype(f32)
    mask_slots[1, row] = mask_tile[...]
    shift_ref[...] = jnp.zeros((2,) + shape, f32)

    for copy in loads[1:-1]:
        copy.wait()

    eight = lax.broadcasted_iota(jnp.int32, (8, LANES), 0)

    def spectra(pixels, kind, first_node):
        table = dft_ref[0]
        first = mm(table, jnp.concatenate([pixels, pixels], axis=0))
        found = []
        for i in range(pair):
            s = slice(i * PATCH, (i + 1) * PATCH)
            level = jnp.sum(first[0:1, s], axis=1, keepdims=True) * (1.0 / PATCH)
            top = jnp.where(eight == 0, first[0:8, s] - level, first[0:8, s])
            body = jnp.concatenate([top, first[8:PATCH, s]], axis=0)
            halves = jnp.concatenate([body, first[PATCH:, s]], axis=1).astype(bf16)
            both = mm(halves, dft_ref[1])
            real, imag = both[:, :PATCH], both[:, PATCH:]
            energy = real * real + imag * imag
            middle = slice(PATCH // 2, PATCH // 2 + 1)
            node = first_node + i
            stats[kind, 0, node : node + 1] = jnp.sum(energy, axis=0, keepdims=True)
            stats[kind, 1, node : node + 1] = energy[middle]
            stats[kind, 2, node : node + 1] = real[middle]
            found.append((real, imag))
        return found

    def cross(a, b):
        real = a[0] * b[0] + a[1] * b[1]
        imag = a[1] * b[0] - a[0] * b[1]
        return jnp.concatenate([real, imag], axis=1).astype(bf16)

    for q in range(chunks):
        for i, (real, imag) in enumerate(spectra(whole[half, :, q * width : (q + 1) * width], 0, q * pair)):
            own_re[q * pair + i] = real
            own_im[q * pair + i] = imag

    def part(i):
        k, j = divmod(i, piece // PATCH)
        return whole[k, :, j * PATCH : (j + 1) * PATCH]

    loads[-1].wait()
    for i in range(patches):
        check[i : i + 1] = jnp.sum(part(i).astype(f32) * tables[2 * SPAN + 8 :], axis=0, keepdims=True)
    sums = jnp.sum(check[...], axis=1, keepdims=True)
    check[...] = jnp.broadcast_to(sums, check.shape)

    @pl.when(group != HUB)
    def _():
        pl.semaphore_wait(all_sem, 1)

    for step in range(1, per_section):
        mask_copy(0, step).start()

    @pl.when(group < SECTIONS - 1)
    def _():
        for step in range(per_section):
            mask_copy(1, step).start()

    @pl.when(group == 1)
    def _():
        start_bulk(1)

    for way in range(2):

        @pl.when(jnp.logical_and(group == SECTIONS - 1 - way, wrapped))
        def _():
            detour(way)

    def arrived(way, chunk):
        buffer = (next_raw if way else prev_raw).at[chunk]
        pltpu.make_async_copy(buffer, buffer, bulk_recv.at[way, chunk]).wait()

    def own(node):
        return own_re[node], own_im[node]

    up_ok = (sub_row > 0).astype(f32)
    down_ok = (sub_row < per_section - 1).astype(f32)
    left_ok = jnp.logical_and(lane > 0, lane < grid_cols).astype(f32)
    right_ok = (lane < grid_cols - 1).astype(f32)
    count = up_ok + down_ok + left_ok + right_ok

    def relax(flow, mask):
        weight = anchor_weight * mask
        pull = weight * flow
        scale = 1.0 / (weight + count)
        d = flow * mask
        for _ in range(SWEEPS):
            near = (
                up_ok * pltpu.roll(d, 1, 0)
                + down_ok * pltpu.roll(d, 2 * per_section - 1, 0)
                + left_ok * pltpu.roll(d, 1, 1)
                + right_ok * pltpu.roll(d, LANES - 1, 1)
            )
            d = (pull + near) * scale
        return jnp.where(lane < grid_cols, d, 0.0)

    node_sub = lax.broadcasted_iota(jnp.int32, (nodes, LANES), 0)
    node_lane = lax.broadcasted_iota(jnp.int32, (nodes, LANES), 1)
    diagonal = node_lane == base + node_sub
    nyquist = node_lane == PATCH // 2
    frequency = jnp.where(node_lane < PATCH // 2, node_lane, node_lane - PATCH).astype(f32)
    frequency = frequency * (1.0 / PATCH)
    corr_row = lax.broadcasted_iota(jnp.int32, (PADDED, PADDED), 0)
    corr_col = lax.broadcasted_iota(jnp.int32, (PADDED, PADDED), 1)
    inside = jnp.logical_and(corr_row < WINDOW, corr_col < WINDOW)
    eight_lane = lax.broadcasted_iota(jnp.int32, (8, LANES), 1)
    middle = slice(PATCH // 2, PATCH // 2 + 1)

    def column(d, which):
        line = jnp.sum(jnp.where(sub == row + which * per_section, d, 0.0), axis=0, keepdims=True)
        return jnp.sum(jnp.where(diagonal, line, 0.0), axis=1, keepdims=True)

    def flows(section, crosses, kind_a, kind_b, d):
        row_offset = offsets[0, section]
        col_offset = offsets[1, section]
        turned = []
        for which in range(2):
            cosine, sine = turn(frequency * column(d, which))
            turned.append((cosine, jnp.where(nyquist, 0.0, sine), cosine[:, middle], sine[:, middle]))
        (cos_y, sin_y, end_cy, end_sy), (cos_x, sin_x, end_cx, end_sx) = turned
        total_a = jnp.sum(stats[kind_a, 0], axis=1, keepdims=True)
        edge_col = stats[kind_b, 0]
        total_b = jnp.sum(edge_col, axis=1, keepdims=True)
        edge_row = jnp.sum(stats[kind_b, 1], axis=1, keepdims=True)
        tip_a = stats[kind_a, 2][:, middle]
        tip_b = stats[kind_b, 2][:, middle]
        tip = tip_b * tip_b
        end_both = end_cy * end_cx - end_sy * end_sx
        lost = (
            (edge_row - tip) * (end_sy * end_sy)
            + (edge_col[:, middle] - tip) * (end_sx * end_sx)
            + tip * (1.0 - end_both * end_both)
        )
        size = 1.0 / float(PATCH) ** 4
        variance_a = total_a * size + 1e-05
        variance_b = jnp.maximum((total_b - lost) * size, 0.0) + 1e-05
        scales = (sharpness * size) * lax.rsqrt(variance_a * variance_b)
        corners = end_sy * end_sx * tip_a * tip_b
        row_cos = tables[pl.ds(row_offset + REACH, PADDED), :]
        row_sin = tables[pl.ds(row_offset + REACH + SPAN, PADDED), :]
        col_cos = tables[pl.ds(col_offset + REACH, PADDED), :]
        col_sin = tables[pl.ds(col_offset + REACH + SPAN, PADDED), :]
        col_high, col_low = split(jnp.concatenate([col_cos, -col_sin], axis=1))
        moved = []
        for i in range(nodes):
            c, s = cos_y[i : i + 1], sin_y[i : i + 1]
            table = jnp.concatenate(
                [row_cos * c + row_sin * s, row_sin * c - row_cos * s], axis=0
            )
            parts = mm(jnp.concatenate(split(table), axis=0), crosses[i])
            parts = parts[: 2 * PADDED] + parts[2 * PADDED :]
            real = parts[:PADDED, :PATCH] - parts[PADDED:, PATCH:]
            imag = parts[:PADDED, PATCH:] + parts[PADDED:, :PATCH]
            c, s = cos_x[i : i + 1], sin_x[i : i + 1]
            moved.append(
                jnp.concatenate([real * c + imag * s, imag * c - real * s], axis=1)
            )
        high, low = split(jnp.concatenate(moved, axis=0))
        correlation = mm_nt(
            jnp.concatenate([high, low, high], axis=1),
            jnp.concatenate([col_high, col_high, col_low], axis=1),
        )
        odd = (corr_row + corr_col + (row_offset + col_offset + 2 * REACH)) & 1
        parity = 1.0 - 2.0 * odd.astype(f32)
        weights = []
        for i in range(nodes):
            here = correlation[i * PADDED : (i + 1) * PADDED] - corners[i : i + 1] * parity
            weights.append(jnp.where(inside, jnp.exp(here * scales[i : i + 1]), 0.0))
        across = (lax.broadcasted_iota(jnp.int32, (8, PADDED), 1) - HALF + col_offset).astype(f32)
        down = (lax.broadcasted_iota(jnp.int32, (8, PADDED), 0) - HALF + row_offset).astype(f32)
        sums = [jnp.zeros((8, LANES), f32) for _ in range(3)]
        for i in range(nodes):
            upper, lower = weights[i][:8], weights[i][8:]
            plain = upper + lower
            parts = (plain, upper * down + lower * (down + 8.0), plain * across)
            here = eight_lane == base + i
            for k in range(3):
                line = jnp.sum(parts[k], axis=1, keepdims=True)
                sums[k] = jnp.where(here, line, sums[k])
        plain, line_row, line_col = [jnp.sum(value, axis=0, keepdims=True) for value in sums]
        inverse = 1.0 / jnp.where(plain > 0.0, plain, 1.0)
        line_row = line_row * inverse
        line_col = line_col * inverse
        return line_row, line_col

    def flow_copy(phase, ahead, step):
        part = 1 - phase
        slot = 1 - ahead
        return pltpu.make_async_remote_copy(
            src_ref=flow_tile.at[phase],
            dst_ref=flow_slots.at[slot, part * per_section + row],
            send_sem=flow_send.at[phase, ahead],
            recv_sem=flow_recv.at[slot],
            device_id={"tile": device(group + phase + ahead, mate(step))},
            device_id_type=MESH,
        )

    def send_flow(phase, tile):
        for which in range(2):
            flow_tile[phase, which : which + 1] = tile[which]
            if phase == 0:
                flow_slots[1, per_section + row, which : which + 1] = tile[which]
        for step in range(1 - phase, per_section):
            flow_copy(phase, 0, step).start()

        @pl.when(group + phase + 1 < SECTIONS)
        def _():
            for step in range(per_section):
                flow_copy(phase, 1, step).start()

    def drain(ref, sem):
        pltpu.make_async_copy(ref, ref, sem).wait()

    def end_flow(phase):
        drain(flow_slots.at[0, pl.ds(0, per_section - 1 + phase)], flow_send.at[phase, 0])

        @pl.when(group + phase + 1 < SECTIONS)
        def _():
            drain(flow_slots.at[0, pl.ds(0, per_section)], flow_send.at[phase, 1])

    def masks(slot):
        drain(mask_slots.at[slot, pl.ds(0, per_section - slot)], mask_recv.at[slot])

    def gathered(slot):
        masks(slot)
        drain(flow_slots.at[slot, pl.ds(0, 2 * per_section - slot)], flow_recv.at[slot])
        flow = jnp.zeros(shape, f32)
        mask = jnp.zeros(shape, f32)
        for line in range(per_section):
            both = flow_slots[slot, line] + flow_slots[slot, per_section + line]
            flow = jnp.where(sub == line, both[0:1], flow)
            flow = jnp.where(sub == line + per_section, both[1:2], flow)
            mask = jnp.where(sub_row == line, mask_slots[slot, line], mask)
        return relax(flow, mask)

    @pl.when(group == SECTIONS - 1)
    def _():

        @pl.when(wrapped)
        def _():
            pl.semaphore_wait(go_sem, 1)
            start_bulk(0, relayed[0])


    @pl.when(group >= 1)
    def _():
        for q in range(chunks):
            arrived(0, q)
            for i, found in enumerate(spectra(prev_raw[q], 1, q * pair)):
                down_cross[q * pair + i] = cross(own(q * pair + i), found)

        @pl.when(jnp.logical_and(group == 2, wrapped))
        def _():
            start_bulk(1, relayed[1])

        @pl.when(jnp.logical_and(group == SECTIONS - 1, jnp.logical_not(wrapped)))
        def _():
            forward(1)


        @pl.when(group >= 2)
        def _():
            shift_ref[0] = gathered(0)

        send_flow(0, flows(group, down_cross, 0, 1, shift_ref[0]))

    @pl.when(group < SECTIONS - 1)
    def _():
        for q in range(chunks):
            arrived(1, q)
            for i, found in enumerate(spectra(next_raw[q], 2, q * pair)):
                up_cross[q * pair + i] = cross(found, own(q * pair + i))

    @pl.when(group >= 1)
    def _():
        shift_ref[1] = gathered(1)

    @pl.when(group < SECTIONS - 1)
    def _():
        send_flow(1, flows(group + 1, up_cross, 2, 0, shift_ref[1]))

        @pl.when(jnp.logical_and(group == 0, jnp.logical_not(wrapped)))
        def _():
            pl.delay(REST)
            forward(0)

        @pl.when(jnp.logical_and(group == 0, wrapped))
        def _():
            release()

    home = shift_ref[1]
    lines = [
        jnp.sum(jnp.where(sub == row + which * per_section, home, 0.0), axis=0, keepdims=True)
        for which in range(2)
    ]
    for which in range(2):
        node_ref[which] = lines[which][:, :grid_cols]
    rows = kernel_rows(term_rows(lines[0], lines[1]), tables[2 * SPAN : 2 * SPAN + 8], patches)
    corner = rows[2] * check[:, 0:1]
    for k in range(PIECES):
        for j in range(piece // PATCH):
            i = k * (piece // PATCH) + j
            moved = warp_patch(part(i), rows[0][i : i + 1], rows[1][i : i + 1])
            out[:, i * PATCH : (i + 1) * PATCH] = (
                moved - corner[i : i + 1] * tables[2 * SPAN + 8 :]
            ).astype(bf16)

    @pl.when(group == 0)
    def _():
        masks(1)

    @pl.when(group == 1)
    def _():
        masks(0)

    drain(mask_slots.at[1, pl.ds(0, per_section - 1)], mask_send.at[0])

    @pl.when(group < SECTIONS - 1)
    def _():
        drain(mask_slots.at[1, pl.ds(0, per_section)], mask_send.at[1])
        drain(next_raw, bulk_send.at[1])
        end_flow(1)

    @pl.when(group >= 1)
    def _():
        drain(prev_raw, bulk_send.at[0])
        end_flow(0)

    for way, section in ((0, 0), (1, SECTIONS - 1)):

        @pl.when(jnp.logical_and(group == section, jnp.logical_not(wrapped)))
        def _():
            drain(relay_raw.at[pl.ds(0, relayed[way])], relay_send)


def store_kernel(aligned, shift, out, shift_out, sems):
    stores = [
        pltpu.make_async_copy(shift, shift_out, sems.at[0]),
        pltpu.make_async_copy(aligned, out, sems.at[1]),
    ]
    for copy in stores:
        copy.start()
    for copy in stores:
        copy.wait()


def shards(tile_count, sections, valid_mask, coarse_offsets):
    per_section = tile_count // SECTIONS
    grid_cols = valid_mask.shape[1]
    width = CHUNK * PATCH
    chunks = sections.shape[1] // (2 * width)
    nodes = chunks * CHUNK
    tile_shape = (2 * per_section, LANES)
    vmem = pl.BlockSpec(memory_space=pltpu.VMEM)
    dft, tables = constants()
    hbm = pl.BlockSpec(memory_space=pltpu.HBM)
    raw = pltpu.VMEM((chunks, PATCH, width), bf16)
    spectrum = pltpu.VMEM((nodes, PATCH, PATCH), f32)
    crossed = pltpu.VMEM((nodes, PATCH, 2 * PATCH), bf16)
    dma = pltpu.SemaphoreType.DMA
    patches = sections.shape[1] // PATCH
    pieces = pltpu.VMEM((PIECES, PATCH, sections.shape[1] // PIECES), bf16)
    aligned, shift = pl.pallas_call(
        functools.partial(chain_kernel, tile_count, grid_cols),
        out_shape=(
            pltpu.VMEM(sections.shape, bf16),
            pltpu.VMEM((2, 1, grid_cols), f32),
        ),
        in_specs=[hbm] * 5,
        out_specs=(vmem, vmem),
        scratch_shapes=[
            pltpu.VMEM(dft.shape, bf16),
            pltpu.VMEM(tables.shape, f32),
            pieces,
            pltpu.VMEM((patches, LANES), f32),
            pltpu.SMEM(coarse_offsets.shape[::-1], jnp.int32),
            pltpu.VMEM(valid_mask.shape, jnp.int32),
            dma((6,)),
            raw,
            raw,
            spectrum,
            spectrum,
            crossed,
            crossed,
            pltpu.VMEM((3, 3, nodes, LANES), f32),
            pltpu.VMEM((1, LANES), f32),
            pltpu.VMEM((2, per_section, 1, LANES), f32),
            pltpu.VMEM((2, 2, LANES), f32),
            pltpu.VMEM((2, 2 * per_section, 2, LANES), f32),
            pltpu.VMEM((2,) + tile_shape, f32),
            dma((2,)),
            dma((2, chunks)),
            dma((2,)),
            dma((2,)),
            dma((2, 2)),
            dma((2,)),
            pltpu.SemaphoreType.REGULAR,
            pltpu.SemaphoreType.REGULAR,
            pltpu.VMEM((chunks // 2, PATCH, width), bf16),
            dma(()),
            dma(()),
        ],
        compiler_params=pltpu.CompilerParams(
            collective_id=0, has_side_effects=True
        ),
        name="chain",
    )(coarse_offsets.T, valid_mask, dft, tables, sections)
    return pl.pallas_call(
        store_kernel,
        out_shape=(
            jax.ShapeDtypeStruct(sections.shape, bf16),
            jax.ShapeDtypeStruct((2, 1, grid_cols), f32),
        ),
        in_specs=[vmem, vmem],
        out_specs=(hbm, hbm),
        scratch_shapes=[dma((2,))],
        name="store",
    )(*[pltpu.with_memory_space_constraint(x, pltpu.VMEM) for x in (aligned, shift)])


def solution(mesh):
    placed = (P(("parts", "tile"), None), P(("parts", "tile"), None), P("parts", None))
    return jax.shard_map(
        functools.partial(shards, mesh.shape["tile"]),
        mesh=mesh,
        in_specs=placed,
        out_specs=(P(("parts", "tile"), None), P(None, ("parts", "tile"), None)),
        check_vma=False,
    )
```

```python
import functools

import jax
import jax.numpy as jnp
import numpy as np
from jax import lax
from jax.experimental import pallas as pl
from jax.experimental.pallas import tpu as pltpu
from jax.sharding import PartitionSpec as P

SECTIONS = 4
PATCH = 128
HALF = 4
SWEEPS = 3
REACH = 3
WINDOW = 2 * HALF + 1
PADDED = 16
LANES = 128
CHUNK = 2
SPAN = 24
HUB = 2
REST = 1400
LAG = 500
PIECES = 2
ORDER = 1

sharpness = 12.0
anchor_weight = 2.0
MESH = pl.DeviceIdType.MESH
f32 = jnp.float32
bf16 = jnp.bfloat16


def split(value):
    high = value.astype(bf16)
    return high, (value - high.astype(f32)).astype(bf16)


def mm(a, b):
    return jnp.dot(a, b, preferred_element_type=f32)


def mm_nt(a, b):
    return lax.dot_general(a, b, (((1,), (1,)), ((), ())), preferred_element_type=f32)


def constants():
    n = PATCH
    k = np.arange(n)
    angle = 2 * np.pi * ((k[:, None] * k[None, :]) % n) / n
    cosine, sine = np.cos(angle), np.sin(angle)
    left = []
    for table in (cosine, sine):
        high = np.asarray(table, bf16)
        low = np.asarray(table - high.astype(np.float64), bf16)
        left.append(np.concatenate([high, low], axis=1))
    left = np.concatenate(left, axis=0)
    right = np.block([[cosine, -sine], [-sine, -cosine]])
    right = np.asarray(right, bf16)
    u = np.arange(-HALF - REACH, -HALF - REACH + SPAN)
    window_angle = 2 * np.pi * ((u[:, None] * k[None, :]) % n) / n
    window = np.stack([np.cos(window_angle), np.sin(window_angle)])
    window = window.astype(np.float32)
    half_angle = np.pi * k / n
    sign = 1.0 - 2.0 * (k % 2)
    warp = np.zeros((8, n), np.float32)
    warp[:4] = np.stack([np.sin(half_angle), np.cos(half_angle), sign, k])
    parity = (sign[:, None] * sign[None, :]).astype(np.float32)
    tables = np.concatenate([window[0], window[1], warp, parity], axis=0)
    return np.stack([left, right]), tables


def turn(value):
    small = (value - jnp.round(value)) * np.pi
    square = small * small
    sine = small * (1.0 + square * (-1 / 6 + square * (1 / 120 + square * (
        -1 / 5040 + square * (1 / 362880 - square * (1 / 39916800))))))
    cosine = 1.0 + square * (-1 / 2 + square * (1 / 24 + square * (-1 / 720 + square * (
        1 / 40320 + square * (-1 / 3628800 + square * (1 / 479001600))))))
    return 1.0 - 2.0 * (sine * sine), 2.0 * (sine * cosine)


def shift_terms(d):
    whole = jnp.round(d)
    frac = d - whole
    odd = jnp.abs(whole - 2.0 * jnp.round(whole * 0.5))
    wide = frac * np.pi
    square = wide * wide
    shape = 1.0 + square * (-1 / 6 + square * (1 / 120 + square * (
        -1 / 5040 + square * (1 / 362880 - square * (1 / 39916800)))))
    sine = wide * shape
    signed = jnp.where(odd > 0.5, -sine, sine) * (1.0 / PATCH)
    angle = d * (np.pi / PATCH)
    square = angle * angle
    tangent = angle * (1.0 + square * (1 / 3 + square * (2 / 15 + square * (
        17 / 315 + square * (62 / 2835 + square * (1382 / 155925))))))
    small = frac * (np.pi / PATCH)
    square = small * small
    peak = shape * (1.0 - square * (1 / 3 + square * (1 / 45)))
    return tangent, signed, peak, whole


def kernel_rows(terms, tables, patches):
    columns = jnp.transpose(terms)[:patches]
    sine, cosine, parity, gap = [tables[i : i + 1, :] for i in range(4)]
    found = []
    for base, forward in ((0, False), (4, True)):
        tangent, signed, peak, whole = [columns[:, base + i : base + i + 1] for i in range(4)]
        if forward:
            bottom = cosine * tangent + sine
            top = cosine - sine * tangent
            centre = jnp.where(whole > 0, PATCH - whole, -whole)
        else:
            bottom = cosine * tangent - sine
            top = cosine + sine * tangent
            centre = jnp.where(whole < 0, whole + PATCH, whole)
        found.append(jnp.where(gap == centre, peak, (signed * parity) * (top / bottom)))
    corner = columns[:, 1:2] * columns[:, 5:6]
    return found[0], found[1], corner


def circulant(row):
    spread = jnp.broadcast_to(row, (PATCH, PATCH))
    return split(pltpu.roll(spread, 0, 1, stride=1, stride_axis=0))


def warp_patch(patch, left_row, right_row):
    left = circulant(left_row)
    right = circulant(right_row)
    both = mm(patch, jnp.concatenate(right, axis=1))
    high, low = split(both[:, :PATCH] + both[:, PATCH:])
    lower = jnp.concatenate([high, jnp.zeros_like(low)], axis=1)
    inner = jnp.concatenate([jnp.concatenate([high, low], axis=1), lower], axis=0)
    moved = mm(jnp.concatenate(left, axis=1), inner)
    return moved[:, :PATCH] + moved[:, PATCH:]


def term_rows(d_rows, d_cols):
    both = jnp.concatenate([d_rows, d_cols], axis=0)
    tangent, signed, peak, whole = shift_terms(both)
    pieces = [t[i : i + 1] for i in range(2) for t in (tangent, signed, peak, whole)]
    return jnp.concatenate(pieces, axis=0)


def chain_kernel(
    tile_count,
    grid_cols,
    offsets_in,
    mask_in,
    dft_in,
    tables_in,
    strip,
    out,
    node_ref,
    dft_ref,
    tables,
    whole,
    check,
    offsets,
    mask_ref,
    load_sem,
    prev_raw,
    next_raw,
    own_re,
    own_im,
    down_cross,
    up_cross,
    stats,
    mask_tile,
    mask_slots,
    flow_tile,
    flow_slots,
    shift_ref,
    bulk_send,
    bulk_recv,
    mask_send,
    mask_recv,
    flow_send,
    flow_recv,
    go_sem,
    all_sem,
    relay_raw,
    relay_send,
    relay_recv,
):
    per_section = tile_count // SECTIONS
    me = lax.axis_index("tile")
    lead = per_section // 2
    rotated = lax.rem(me + tile_count - lead, tile_count)
    group = rotated // per_section
    row = lax.rem(rotated, per_section)
    chunks, width = prev_raw.shape[0], prev_raw.shape[2]
    pair = width // PATCH
    nodes = chunks * pair
    half = lax.rem(group, 2)
    base = half * nodes
    piece = whole.shape[2]
    patches = PIECES * piece // PATCH

    def device(section, line):
        return lax.rem(section * per_section + line + lead, tile_count)

    def mate(line_step):
        return lax.rem(row + line_step, per_section)

    barrier = pltpu.get_barrier_semaphore()

    def signal(sem, section, line):
        pl.semaphore_signal(
            sem, inc=1, device_id={"tile": device(section, line)}, device_id_type=MESH
        )

    @pl.when(group <= 1)
    def _():
        signal(barrier, 1 - group, row)

    @pl.when(group == HUB)
    def _():
        signal(barrier, SECTIONS - 1, row)
        for step in range(1, per_section):
            signal(barrier, HUB, mate(step))

    @pl.when(group != HUB)
    def _():
        for step in range(per_section):
            signal(barrier, HUB, mate(step))

    def columns(side, chunk):
        start = pl.multiple_of((side * chunks + chunk) * width, LANES)
        return strip.at[:, pl.ds(start, width)]

    def strip_half(side):
        return strip.at[:, pl.ds(pl.multiple_of(side * piece, LANES), piece)]

    loads = [
        pltpu.make_async_copy(source, target, load_sem.at[i])
        for i, (source, target) in enumerate(
            [(mask_in, mask_ref), (offsets_in, offsets), (dft_in, dft_ref), (tables_in, tables)]
            + [(strip_half(side), whole.at[side]) for side in (half, 1 - half)]
        )
    ]
    for copy in loads:
        copy.start()
    pl.semaphore_wait(barrier, jnp.where(group == HUB, tile_count - 1, 1))

    def bulk(way, chunk):
        peer = lax.rem(me + (per_section if way else tile_count - per_section), tile_count)
        return pltpu.make_async_remote_copy(
            src_ref=columns(1 - half, chunk),
            dst_ref=(prev_raw if way else next_raw).at[chunk],
            send_sem=bulk_send.at[way],
            recv_sem=bulk_recv.at[1 - way, chunk],
            device_id={"tile": peer},
            device_id_type=MESH,
        )

    def start_bulk(way, first=0, last=chunks):
        for chunk in range(first, last):
            bulk(way, chunk).start()

    relayed = (chunks // 2, chunks // 2)
    arrival = [
        sorted(range(chunks), key=lambda q: (q - n if q >= n else q, ORDER * (q < n)))
        for n in (relayed[1], relayed[0])
    ]
    apart = per_section - per_section // 2
    wrapped = row >= apart

    def detour(way):
        for k in range(relayed[way]):
            pltpu.make_async_remote_copy(
                src_ref=columns(1 - half, k),
                dst_ref=relay_raw.at[k],
                send_sem=bulk_send.at[way],
                recv_sem=relay_recv,
                device_id={"tile": device(SECTIONS - 1 if way else 0, row - apart)},
                device_id_type=MESH,
            ).start()

    def onward(way, k):
        return pltpu.make_async_remote_copy(
            src_ref=relay_raw.at[k],
            dst_ref=(prev_raw if way else next_raw).at[k],
            send_sem=relay_send,
            recv_sem=bulk_recv.at[1 - way, k],
            device_id={"tile": device(SECTIONS - 1 if way else 2, row + apart)},
            device_id_type=MESH,
        )

    def forward(way):
        arrival = relay_raw.at[pl.ds(0, relayed[way])]
        pltpu.make_async_copy(arrival, arrival, relay_recv).wait()
        for k in range(relayed[way]):
            onward(way, k).start()

    def release():
        signal(go_sem, SECTIONS - 1, row)

    @pl.when(group == HUB)
    def _():
        for section in range(SECTIONS):
            if section != HUB:
                signal(all_sem, section, row)

    @pl.when(jnp.logical_or(group == 1, group == 2))
    def _():
        start_bulk(0)

    @pl.when(group == 0)
    def _():
        start_bulk(1)

    for way in range(2):

        @pl.when(jnp.logical_and(group == SECTIONS - 1 - way, jnp.logical_not(wrapped)))
        def _():
            start_bulk(way)

    def mask_copy(ahead, step):
        return pltpu.make_async_remote_copy(
            src_ref=mask_tile,
            dst_ref=mask_slots.at[1 - ahead, row],
            send_sem=mask_send.at[ahead],
            recv_sem=mask_recv.at[1 - ahead],
            device_id={"tile": device(group + ahead, mate(step))},
            device_id_type=MESH,
        )

    loads[0].wait()
    shape = (2 * per_section, LANES)
    sub = lax.broadcasted_iota(jnp.int32, shape, 0)
    lane = lax.broadcasted_iota(jnp.int32, shape, 1)
    sub_row = lax.rem(sub, per_section)
    mask_tile[...] = jnp.zeros((1, LANES), f32)
    mask_tile[:, 0:grid_cols] = mask_ref[...].astype(f32)
    mask_slots[1, row] = mask_tile[...]
    shift_ref[...] = jnp.zeros((2,) + shape, f32)

    for copy in loads[1:-1]:
        copy.wait()

    eight = lax.broadcasted_iota(jnp.int32, (8, LANES), 0)

    def spectra(pixels, kind, first_node):
        table = dft_ref[0]
        first = mm(table, jnp.concatenate([pixels, pixels], axis=0))
        found = []
        for i in range(pair):
            s = slice(i * PATCH, (i + 1) * PATCH)
            level = jnp.sum(pixels[:, s].astype(f32), axis=0, keepdims=True)
            level = jnp.sum(level, axis=1, keepdims=True) * (1.0 / PATCH)
            top = jnp.where(eight == 0, first[0:8, s] - level, first[0:8, s])
            body = jnp.concatenate([top, first[8:PATCH, s]], axis=0)
            halves = jnp.concatenate([body, first[PATCH:, s]], axis=1).astype(bf16)
            both = mm(halves, dft_ref[1])
            real, imag = both[:, :PATCH], both[:, PATCH:]
            energy = real * real + imag * imag
            middle = slice(PATCH // 2, PATCH // 2 + 1)
            node = first_node + i
            where = pl.ds(node, 1)
            stats[kind, 0, where] = jnp.sum(energy, axis=0, keepdims=True)
            stats[kind, 1, where] = energy[middle]
            stats[kind, 2, where] = real[middle]
            found.append((real, imag))
        return found

    def cross(a, b):
        real = a[0] * b[0] + a[1] * b[1]
        imag = a[1] * b[0] - a[0] * b[1]
        return jnp.concatenate([real, imag], axis=1).astype(bf16)

    for q in range(chunks):
        for i, (real, imag) in enumerate(spectra(whole[half, :, q * width : (q + 1) * width], 0, q * pair)):
            own_re[q * pair + i] = real
            own_im[q * pair + i] = imag

    def part(i):
        k, j = divmod(i, piece // PATCH)
        return whole[k, :, j * PATCH : (j + 1) * PATCH]

    loads[-1].wait()
    for i in range(patches):
        check[i : i + 1] = jnp.sum(part(i).astype(f32) * tables[2 * SPAN + 8 :], axis=0, keepdims=True)
    sums = jnp.sum(check[...], axis=1, keepdims=True)
    check[...] = jnp.broadcast_to(sums, check.shape)

    @pl.when(group != HUB)
    def _():
        pl.semaphore_wait(all_sem, 1)

    for step in range(1, per_section):
        mask_copy(0, step).start()

    @pl.when(group < SECTIONS - 1)
    def _():
        for step in range(per_section):
            mask_copy(1, step).start()

    @pl.when(group == 1)
    def _():
        start_bulk(1)

    for way in range(2):

        @pl.when(jnp.logical_and(group == SECTIONS - 1 - way, wrapped))
        def _():
            detour(way)

    def arrived(way, chunk):
        buffer = (next_raw if way else prev_raw).at[chunk]
        pltpu.make_async_copy(buffer, buffer, bulk_recv.at[way, chunk]).wait()

    def own(node):
        return own_re[node], own_im[node]

    up_ok = (sub_row > 0).astype(f32)
    down_ok = (sub_row < per_section - 1).astype(f32)
    left_ok = jnp.logical_and(lane > 0, lane < grid_cols).astype(f32)
    right_ok = (lane < grid_cols - 1).astype(f32)
    count = up_ok + down_ok + left_ok + right_ok

    node_sub = lax.broadcasted_iota(jnp.int32, (nodes, LANES), 0)
    node_lane = lax.broadcasted_iota(jnp.int32, (nodes, LANES), 1)
    diagonal = node_lane == base + node_sub
    nyquist = node_lane == PATCH // 2
    frequency = jnp.where(node_lane < PATCH // 2, node_lane, node_lane - PATCH).astype(f32)
    frequency = frequency * (1.0 / PATCH)
    corr_row = lax.broadcasted_iota(jnp.int32, (PADDED, PADDED), 0)
    corr_col = lax.broadcasted_iota(jnp.int32, (PADDED, PADDED), 1)
    inside = jnp.logical_and(corr_row < WINDOW, corr_col < WINDOW)
    eight_lane = lax.broadcasted_iota(jnp.int32, (8, LANES), 1)
    middle = slice(PATCH // 2, PATCH // 2 + 1)

    def column(d, which):
        line = jnp.sum(jnp.where(sub == row + which * per_section, d, 0.0), axis=0, keepdims=True)
        return jnp.sum(jnp.where(diagonal, line, 0.0), axis=1, keepdims=True)

    def flows(section, crosses, kind_a, kind_b, d):
        row_offset = offsets[0, section]
        col_offset = offsets[1, section]
        turned = []
        for which in range(2):
            cosine, sine = turn(frequency * column(d, which))
            turned.append((cosine, jnp.where(nyquist, 0.0, sine), cosine[:, middle], sine[:, middle]))
        (cos_y, sin_y, end_cy, end_sy), (cos_x, sin_x, end_cx, end_sx) = turned
        total_a = jnp.sum(stats[kind_a, 0], axis=1, keepdims=True)
        edge_col = stats[kind_b, 0]
        total_b = jnp.sum(edge_col, axis=1, keepdims=True)
        edge_row = jnp.sum(stats[kind_b, 1], axis=1, keepdims=True)
        tip_a = stats[kind_a, 2][:, middle]
        tip_b = stats[kind_b, 2][:, middle]
        tip = tip_b * tip_b
        end_both = end_cy * end_cx - end_sy * end_sx
        lost = (
            (edge_row - tip) * (end_sy * end_sy)
            + (edge_col[:, middle] - tip) * (end_sx * end_sx)
            + tip * (1.0 - end_both * end_both)
        )
        size = 1.0 / float(PATCH) ** 4
        variance_a = total_a * size + 1e-05
        variance_b = jnp.maximum((total_b - lost) * size, 0.0) + 1e-05
        scales = (sharpness * size) * lax.rsqrt(variance_a * variance_b)
        corners = end_sy * end_sx * tip_a * tip_b
        row_cos = tables[pl.ds(row_offset + REACH, PADDED), :]
        row_sin = tables[pl.ds(row_offset + REACH + SPAN, PADDED), :]
        col_cos = tables[pl.ds(col_offset + REACH, PADDED), :]
        col_sin = tables[pl.ds(col_offset + REACH + SPAN, PADDED), :]
        col_high, col_low = split(jnp.concatenate([col_cos, -col_sin], axis=1))
        moved = []
        for i in range(nodes):
            c, s = cos_y[i : i + 1], sin_y[i : i + 1]
            table = jnp.concatenate(
                [row_cos * c + row_sin * s, row_sin * c - row_cos * s], axis=0
            )
            parts = mm(jnp.concatenate(split(table), axis=0), crosses[i])
            parts = parts[: 2 * PADDED] + parts[2 * PADDED :]
            real = parts[:PADDED, :PATCH] - parts[PADDED:, PATCH:]
            imag = parts[:PADDED, PATCH:] + parts[PADDED:, :PATCH]
            c, s = cos_x[i : i + 1], sin_x[i : i + 1]
            moved.append(
                jnp.concatenate([real * c + imag * s, imag * c - real * s], axis=1)
            )
        high, low = split(jnp.concatenate(moved, axis=0))
        correlation = mm_nt(
            jnp.concatenate([high, low, high], axis=1),
            jnp.concatenate([col_high, col_high, col_low], axis=1),
        )
        odd = (corr_row + corr_col + (row_offset + col_offset + 2 * REACH)) & 1
        parity = 1.0 - 2.0 * odd.astype(f32)
        weights = []
        for i in range(nodes):
            here = correlation[i * PADDED : (i + 1) * PADDED] - corners[i : i + 1] * parity
            weights.append(jnp.where(inside, jnp.exp(here * scales[i : i + 1]), 0.0))
        across = (lax.broadcasted_iota(jnp.int32, (8, PADDED), 1) - HALF + col_offset).astype(f32)
        down = (lax.broadcasted_iota(jnp.int32, (8, PADDED), 0) - HALF + row_offset).astype(f32)
        sums = [jnp.zeros((8, LANES), f32) for _ in range(3)]
        for i in range(nodes):
            upper, lower = weights[i][:8], weights[i][8:]
            plain = upper + lower
            parts = (plain, upper * down + lower * (down + 8.0), plain * across)
            here = eight_lane == base + i
            for k in range(3):
                line = jnp.sum(parts[k], axis=1, keepdims=True)
                sums[k] = jnp.where(here, line, sums[k])
        plain, line_row, line_col = [jnp.sum(value, axis=0, keepdims=True) for value in sums]
        inverse = 1.0 / jnp.where(plain > 0.0, plain, 1.0)
        line_row = line_row * inverse
        line_col = line_col * inverse
        return line_row, line_col

    def flow_copy(phase, ahead, step):
        part = 1 - phase
        slot = 1 - ahead
        return pltpu.make_async_remote_copy(
            src_ref=flow_tile.at[phase],
            dst_ref=flow_slots.at[slot, part * per_section + row],
            send_sem=flow_send.at[phase, ahead],
            recv_sem=flow_recv.at[slot],
            device_id={"tile": device(group + phase + ahead, mate(step))},
            device_id_type=MESH,
        )

    def send_flow(phase, tile):
        for which in range(2):
            flow_tile[phase, which : which + 1] = tile[which]
            if phase == 0:
                flow_slots[1, per_section + row, which : which + 1] = tile[which]
        for step in range(1 - phase, per_section):
            flow_copy(phase, 0, step).start()

        @pl.when(group + phase + 1 < SECTIONS)
        def _():
            for step in range(per_section):
                flow_copy(phase, 1, step).start()

    def drain(ref, sem):
        pltpu.make_async_copy(ref, ref, sem).wait()

    def end_flow(phase):
        drain(flow_slots.at[0, pl.ds(0, per_section - 1 + phase)], flow_send.at[phase, 0])

        @pl.when(group + phase + 1 < SECTIONS)
        def _():
            drain(flow_slots.at[0, pl.ds(0, per_section)], flow_send.at[phase, 1])

    def masks(slot):
        drain(mask_slots.at[slot, pl.ds(0, per_section - slot)], mask_recv.at[slot])

    def gathered(slot):
        masks(slot)
        mask = jnp.zeros(shape, f32)
        for line in range(per_section):
            mask = jnp.where(sub_row == line, mask_slots[slot, line], mask)
        weight = anchor_weight * mask
        scale = 1.0 / (weight + count)
        weight = weight * scale
        up, down = up_ok * scale, down_ok * scale
        left, right = left_ok * scale, right_ok * scale
        drain(flow_slots.at[slot, pl.ds(0, 2 * per_section - slot)], flow_recv.at[slot])
        flow = jnp.zeros(shape, f32)
        for line in range(per_section):
            both = flow_slots[slot, line] + flow_slots[slot, per_section + line]
            flow = jnp.where(sub == line, both[0:1], flow)
            flow = jnp.where(sub == line + per_section, both[1:2], flow)
        pull = weight * flow
        d = flow * mask
        for _ in range(SWEEPS):
            d = pull + (
                (up * pltpu.roll(d, 1, 0) + down * pltpu.roll(d, 2 * per_section - 1, 0))
                + (left * pltpu.roll(d, 1, 1) + right * pltpu.roll(d, LANES - 1, 1))
            )
        return jnp.where(lane < grid_cols, d, 0.0)

    @pl.when(group == SECTIONS - 1)
    def _():

        @pl.when(wrapped)
        def _():
            pl.semaphore_wait(go_sem, 1)
            start_bulk(0, relayed[0])


    @pl.when(group >= 1)
    def _():
        for q in range(chunks):
            c = jnp.where(group == SECTIONS - 1, arrival[0][q], q)
            arrived(0, c)
            for i, found in enumerate(spectra(prev_raw[c], 1, c * pair)):
                down_cross[c * pair + i] = cross(own(c * pair + i), found)

        @pl.when(jnp.logical_and(group == 2, wrapped))
        def _():
            start_bulk(1, relayed[1])

        @pl.when(jnp.logical_and(group == SECTIONS - 1, jnp.logical_not(wrapped)))
        def _():
            forward(1)


        @pl.when(group >= 2)
        def _():
            shift_ref[0] = gathered(0)

        send_flow(0, flows(group, down_cross, 0, 1, shift_ref[0]))

    @pl.when(group < SECTIONS - 1)
    def _():
        for q in range(chunks):
            c = jnp.where(group == 2, arrival[1][q], q)
            arrived(1, c)
            for i, found in enumerate(spectra(next_raw[c], 2, c * pair)):
                up_cross[c * pair + i] = cross(found, own(c * pair + i))

    @pl.when(group >= 1)
    def _():
        shift_ref[1] = gathered(1)

    @pl.when(group < SECTIONS - 1)
    def _():
        send_flow(1, flows(group + 1, up_cross, 2, 0, shift_ref[1]))

        @pl.when(jnp.logical_and(group == 0, jnp.logical_not(wrapped)))
        def _():
            pl.delay(REST)

            @pl.when(lax.rem(me, 2) == 1)
            def _():
                pl.delay(LAG)

            forward(0)

        @pl.when(jnp.logical_and(group == 0, wrapped))
        def _():
            release()

    home = shift_ref[1]
    lines = [
        jnp.sum(jnp.where(sub == row + which * per_section, home, 0.0), axis=0, keepdims=True)
        for which in range(2)
    ]
    for which in range(2):
        node_ref[which] = lines[which][:, :grid_cols]
    rows = kernel_rows(term_rows(lines[0], lines[1]), tables[2 * SPAN : 2 * SPAN + 8], patches)
    corner = rows[2] * check[:, 0:1]
    for k in range(PIECES):
        for j in range(piece // PATCH):
            i = k * (piece // PATCH) + j
            moved = warp_patch(part(i), rows[0][i : i + 1], rows[1][i : i + 1])
            out[:, i * PATCH : (i + 1) * PATCH] = (
                moved - corner[i : i + 1] * tables[2 * SPAN + 8 :]
            ).astype(bf16)

    @pl.when(group == 0)
    def _():
        masks(1)

    @pl.when(group == 1)
    def _():
        masks(0)

    drain(mask_slots.at[1, pl.ds(0, per_section - 1)], mask_send.at[0])

    @pl.when(group < SECTIONS - 1)
    def _():
        drain(mask_slots.at[1, pl.ds(0, per_section)], mask_send.at[1])
        drain(next_raw, bulk_send.at[1])
        end_flow(1)

    @pl.when(group >= 1)
    def _():
        drain(prev_raw, bulk_send.at[0])
        end_flow(0)

    for way, section in ((0, 0), (1, SECTIONS - 1)):

        @pl.when(jnp.logical_and(group == section, jnp.logical_not(wrapped)))
        def _():
            drain(relay_raw.at[pl.ds(0, relayed[way])], relay_send)


def store_kernel(aligned, shift, out, shift_out, sems):
    stores = [
        pltpu.make_async_copy(shift, shift_out, sems.at[0]),
        pltpu.make_async_copy(aligned, out, sems.at[1]),
    ]
    for copy in stores:
        copy.start()
    for copy in stores:
        copy.wait()


def shards(tile_count, sections, valid_mask, coarse_offsets):
    per_section = tile_count // SECTIONS
    grid_cols = valid_mask.shape[1]
    width = CHUNK * PATCH
    chunks = sections.shape[1] // (2 * width)
    nodes = chunks * CHUNK
    tile_shape = (2 * per_section, LANES)
    vmem = pl.BlockSpec(memory_space=pltpu.VMEM)
    dft, tables = constants()
    hbm = pl.BlockSpec(memory_space=pltpu.HBM)
    raw = pltpu.VMEM((chunks, PATCH, width), bf16)
    spectrum = pltpu.VMEM((nodes, PATCH, PATCH), f32)
    crossed = pltpu.VMEM((nodes, PATCH, 2 * PATCH), bf16)
    dma = pltpu.SemaphoreType.DMA
    patches = sections.shape[1] // PATCH
    pieces = pltpu.VMEM((PIECES, PATCH, sections.shape[1] // PIECES), bf16)
    aligned, shift = pl.pallas_call(
        functools.partial(chain_kernel, tile_count, grid_cols),
        out_shape=(
            pltpu.VMEM(sections.shape, bf16),
            pltpu.VMEM((2, 1, grid_cols), f32),
        ),
        in_specs=[hbm] * 5,
        out_specs=(vmem, vmem),
        scratch_shapes=[
            pltpu.VMEM(dft.shape, bf16),
            pltpu.VMEM(tables.shape, f32),
            pieces,
            pltpu.VMEM((patches, LANES), f32),
            pltpu.SMEM(coarse_offsets.shape[::-1], jnp.int32),
            pltpu.VMEM(valid_mask.shape, jnp.int32),
            dma((6,)),
            raw,
            raw,
            spectrum,
            spectrum,
            crossed,
            crossed,
            pltpu.VMEM((3, 3, nodes, LANES), f32),
            pltpu.VMEM((1, LANES), f32),
            pltpu.VMEM((2, per_section, 1, LANES), f32),
            pltpu.VMEM((2, 2, LANES), f32),
            pltpu.VMEM((2, 2 * per_section, 2, LANES), f32),
            pltpu.VMEM((2,) + tile_shape, f32),
            dma((2,)),
            dma((2, chunks)),
            dma((2,)),
            dma((2,)),
            dma((2, 2)),
            dma((2,)),
            pltpu.SemaphoreType.REGULAR,
            pltpu.SemaphoreType.REGULAR,
            pltpu.VMEM((chunks // 2, PATCH, width), bf16),
            dma(()),
            dma(()),
        ],
        compiler_params=pltpu.CompilerParams(
            collective_id=0, has_side_effects=True
        ),
        name="chain",
    )(coarse_offsets.T, valid_mask, dft, tables, sections)
    return pl.pallas_call(
        store_kernel,
        out_shape=(
            jax.ShapeDtypeStruct(sections.shape, bf16),
            jax.ShapeDtypeStruct((2, 1, grid_cols), f32),
        ),
        in_specs=[vmem, vmem],
        out_specs=(hbm, hbm),
        scratch_shapes=[dma((2,))],
        name="store",
    )(*[pltpu.with_memory_space_constraint(x, pltpu.VMEM) for x in (aligned, shift)])


def solution(mesh):
    placed = (P(("parts", "tile"), None), P(("parts", "tile"), None), P("parts", None))
    return jax.shard_map(
        functools.partial(shards, mesh.shape["tile"]),
        mesh=mesh,
        in_specs=placed,
        out_specs=(P(("parts", "tile"), None), P(None, ("parts", "tile"), None)),
        check_vma=False,
    )
```

```python
import functools

import jax
import jax.numpy as jnp
import numpy as np
from jax import lax
from jax.experimental import pallas as pl
from jax.experimental.pallas import tpu as pltpu
from jax.sharding import PartitionSpec as P

SECTIONS = 4
PATCH = 128
HALF = 4
SWEEPS = 3
REACH = 3
WINDOW = 2 * HALF + 1
PADDED = 16
LANES = 128
CHUNK = 2
SPAN = 24
HUB = 2
REST = 1400
LAG = 500
PIECES = 2
ORDER = 1

sharpness = 12.0
anchor_weight = 2.0
MESH = pl.DeviceIdType.MESH
f32 = jnp.float32
bf16 = jnp.bfloat16


def split(value):
    high = value.astype(bf16)
    return high, (value - high.astype(f32)).astype(bf16)


def mm(a, b):
    return jnp.dot(a, b, preferred_element_type=f32)


def mm_nt(a, b):
    return lax.dot_general(a, b, (((1,), (1,)), ((), ())), preferred_element_type=f32)


def constants():
    n = PATCH
    k = np.arange(n)
    angle = 2 * np.pi * ((k[:, None] * k[None, :]) % n) / n
    cosine, sine = np.cos(angle), np.sin(angle)
    left = []
    for table in (cosine, sine):
        high = np.asarray(table, bf16)
        low = np.asarray(table - high.astype(np.float64), bf16)
        left.append(np.concatenate([high, low], axis=1))
    left = np.concatenate(left, axis=0)
    right = np.block([[cosine, -sine], [-sine, -cosine]])
    right = np.asarray(right, bf16)
    u = np.arange(-HALF - REACH, -HALF - REACH + SPAN)
    window_angle = 2 * np.pi * ((u[:, None] * k[None, :]) % n) / n
    window = np.stack([np.cos(window_angle), np.sin(window_angle)])
    window = window.astype(np.float32)
    half_angle = np.pi * k / n
    sign = 1.0 - 2.0 * (k % 2)
    warp = np.zeros((8, n), np.float32)
    warp[:4] = np.stack([np.sin(half_angle), np.cos(half_angle), sign, k])
    parity = (sign[:, None] * sign[None, :]).astype(np.float32)
    tables = np.concatenate([window[0], window[1], warp, parity], axis=0)
    return np.stack([left, right]), tables


def turn(value):
    small = (value - jnp.round(value)) * np.pi
    square = small * small
    sine = small * (1.0 + square * (-1 / 6 + square * (1 / 120 + square * (
        -1 / 5040 + square * (1 / 362880 - square * (1 / 39916800))))))
    cosine = 1.0 + square * (-1 / 2 + square * (1 / 24 + square * (-1 / 720 + square * (
        1 / 40320 + square * (-1 / 3628800 + square * (1 / 479001600))))))
    return 1.0 - 2.0 * (sine * sine), 2.0 * (sine * cosine)


def shift_terms(d):
    whole = jnp.round(d)
    frac = d - whole
    odd = jnp.abs(whole - 2.0 * jnp.round(whole * 0.5))
    wide = frac * np.pi
    square = wide * wide
    shape = 1.0 + square * (-1 / 6 + square * (1 / 120 + square * (
        -1 / 5040 + square * (1 / 362880 - square * (1 / 39916800)))))
    sine = wide * shape
    signed = jnp.where(odd > 0.5, -sine, sine) * (1.0 / PATCH)
    angle = d * (np.pi / PATCH)
    square = angle * angle
    tangent = angle * (1.0 + square * (1 / 3 + square * (2 / 15 + square * (
        17 / 315 + square * (62 / 2835 + square * (1382 / 155925))))))
    small = frac * (np.pi / PATCH)
    square = small * small
    peak = shape * (1.0 - square * (1 / 3 + square * (1 / 45)))
    return tangent, signed, peak, whole


def kernel_rows(terms, tables, patches):
    columns = jnp.transpose(terms)[:patches]
    sine, cosine, parity, gap = [tables[i : i + 1, :] for i in range(4)]
    found = []
    for base, forward in ((0, False), (4, True)):
        tangent, signed, peak, whole = [columns[:, base + i : base + i + 1] for i in range(4)]
        if forward:
            bottom = cosine * tangent + sine
            top = cosine - sine * tangent
            centre = jnp.where(whole > 0, PATCH - whole, -whole)
        else:
            bottom = cosine * tangent - sine
            top = cosine + sine * tangent
            centre = jnp.where(whole < 0, whole + PATCH, whole)
        found.append(jnp.where(gap == centre, peak, (signed * parity) * (top / bottom)))
    corner = columns[:, 1:2] * columns[:, 5:6]
    return found[0], found[1], corner


def circulant(row):
    spread = jnp.broadcast_to(row, (PATCH, PATCH))
    return split(pltpu.roll(spread, 0, 1, stride=1, stride_axis=0))


def warp_patch(patch, left_row, right_row):
    left = circulant(left_row)
    right = circulant(right_row)
    both = mm(patch, jnp.concatenate(right, axis=1))
    high, low = split(both[:, :PATCH] + both[:, PATCH:])
    lower = jnp.concatenate([high, jnp.zeros_like(low)], axis=1)
    inner = jnp.concatenate([jnp.concatenate([high, low], axis=1), lower], axis=0)
    moved = mm(jnp.concatenate(left, axis=1), inner)
    return moved[:, :PATCH] + moved[:, PATCH:]


def term_rows(d_rows, d_cols):
    both = jnp.concatenate([d_rows, d_cols], axis=0)
    tangent, signed, peak, whole = shift_terms(both)
    pieces = [t[i : i + 1] for i in range(2) for t in (tangent, signed, peak, whole)]
    return jnp.concatenate(pieces, axis=0)


def chain_kernel(
    tile_count,
    grid_cols,
    offsets_in,
    mask_in,
    dft_in,
    tables_in,
    strip,
    out,
    node_ref,
    dft_ref,
    tables,
    whole,
    check,
    offsets,
    mask_ref,
    load_sem,
    prev_raw,
    next_raw,
    own_re,
    own_im,
    down_cross,
    up_cross,
    stats,
    mask_tile,
    mask_slots,
    flow_tile,
    flow_slots,
    shift_ref,
    bulk_send,
    bulk_recv,
    mask_send,
    mask_recv,
    flow_send,
    flow_recv,
    go_sem,
    all_sem,
    relay_raw,
    relay_send,
    relay_recv,
):
    per_section = tile_count // SECTIONS
    me = lax.axis_index("tile")
    lead = per_section // 2
    rotated = lax.rem(me + tile_count - lead, tile_count)
    group = rotated // per_section
    row = lax.rem(rotated, per_section)
    chunks, width = prev_raw.shape[0], prev_raw.shape[2]
    pair = width // PATCH
    nodes = chunks * pair
    half = lax.rem(group, 2)
    base = half * nodes
    piece = whole.shape[2]
    patches = PIECES * piece // PATCH

    def device(section, line):
        return lax.rem(section * per_section + line + lead, tile_count)

    def mate(line_step):
        return lax.rem(row + line_step, per_section)

    barrier = pltpu.get_barrier_semaphore()

    def signal(sem, section, line):
        pl.semaphore_signal(
            sem, inc=1, device_id={"tile": device(section, line)}, device_id_type=MESH
        )

    @pl.when(group <= 1)
    def _():
        signal(barrier, 1 - group, row)

    @pl.when(group == HUB)
    def _():
        signal(barrier, SECTIONS - 1, row)
        for step in range(1, per_section):
            signal(barrier, HUB, mate(step))

    @pl.when(group != HUB)
    def _():
        for step in range(per_section):
            signal(barrier, HUB, mate(step))

    def columns(side, chunk):
        start = pl.multiple_of((side * chunks + chunk) * width, LANES)
        return strip.at[:, pl.ds(start, width)]

    def strip_half(side):
        return strip.at[:, pl.ds(pl.multiple_of(side * piece, LANES), piece)]

    loads = [
        pltpu.make_async_copy(source, target, load_sem.at[i])
        for i, (source, target) in enumerate(
            [(mask_in, mask_ref), (offsets_in, offsets), (dft_in, dft_ref), (tables_in, tables)]
            + [(strip_half(side), whole.at[side]) for side in (half, 1 - half)]
        )
    ]
    for copy in loads:
        copy.start()
    pl.semaphore_wait(barrier, jnp.where(group == HUB, tile_count - 1, 1))

    def bulk(way, chunk):
        peer = lax.rem(me + (per_section if way else tile_count - per_section), tile_count)
        return pltpu.make_async_remote_copy(
            src_ref=columns(1 - half, chunk),
            dst_ref=(prev_raw if way else next_raw).at[chunk],
            send_sem=bulk_send.at[way],
            recv_sem=bulk_recv.at[1 - way, chunk],
            device_id={"tile": peer},
            device_id_type=MESH,
        )

    def start_bulk(way, first=0, last=chunks):
        for chunk in range(first, last):
            bulk(way, chunk).start()

    relayed = (chunks // 2, chunks // 2)
    arrival = [
        sorted(range(chunks), key=lambda q: (q - n if q >= n else q, ORDER * (q < n)))
        for n in (relayed[1], relayed[0])
    ]
    apart = per_section - per_section // 2
    wrapped = row >= apart

    def detour(way):
        for k in range(relayed[way]):
            pltpu.make_async_remote_copy(
                src_ref=columns(1 - half, k),
                dst_ref=relay_raw.at[k],
                send_sem=bulk_send.at[way],
                recv_sem=relay_recv,
                device_id={"tile": device(SECTIONS - 1 if way else 0, row - apart)},
                device_id_type=MESH,
            ).start()

    def onward(way, k):
        return pltpu.make_async_remote_copy(
            src_ref=relay_raw.at[k],
            dst_ref=(prev_raw if way else next_raw).at[k],
            send_sem=relay_send,
            recv_sem=bulk_recv.at[1 - way, k],
            device_id={"tile": device(SECTIONS - 1 if way else 2, row + apart)},
            device_id_type=MESH,
        )

    def forward(way):
        arrival = relay_raw.at[pl.ds(0, relayed[way])]
        pltpu.make_async_copy(arrival, arrival, relay_recv).wait()
        for k in range(relayed[way]):
            onward(way, k).start()

    def release():
        signal(go_sem, SECTIONS - 1, row)

    @pl.when(group == HUB)
    def _():
        for section in range(SECTIONS):
            if section != HUB:
                signal(all_sem, section, row)

    @pl.when(jnp.logical_or(group == 1, group == 2))
    def _():
        start_bulk(0)

    @pl.when(group == 0)
    def _():
        start_bulk(1)

    for way in range(2):

        @pl.when(jnp.logical_and(group == SECTIONS - 1 - way, jnp.logical_not(wrapped)))
        def _():
            start_bulk(way)

    def mask_copy(ahead, step):
        return pltpu.make_async_remote_copy(
            src_ref=mask_tile,
            dst_ref=mask_slots.at[1 - ahead, row],
            send_sem=mask_send.at[ahead],
            recv_sem=mask_recv.at[1 - ahead],
            device_id={"tile": device(group + ahead, mate(step))},
            device_id_type=MESH,
        )

    loads[0].wait()
    shape = (2 * per_section, LANES)
    sub = lax.broadcasted_iota(jnp.int32, shape, 0)
    lane = lax.broadcasted_iota(jnp.int32, shape, 1)
    sub_row = lax.rem(sub, per_section)
    mask_tile[...] = jnp.zeros((1, LANES), f32)
    mask_tile[:, 0:grid_cols] = mask_ref[...].astype(f32)
    mask_slots[1, row] = mask_tile[...]
    shift_ref[...] = jnp.zeros((2,) + shape, f32)

    for copy in loads[1:-1]:
        copy.wait()

    eight = lax.broadcasted_iota(jnp.int32, (8, LANES), 0)

    def spectra(pixels, kind, first_node):
        table = dft_ref[0]
        first = mm(table, jnp.concatenate([pixels, pixels], axis=0))
        found, rows = [], []
        for i in range(pair):
            s = slice(i * PATCH, (i + 1) * PATCH)
            level = jnp.sum(pixels[:, s].astype(f32), axis=0, keepdims=True)
            level = jnp.sum(level, axis=1, keepdims=True) * (1.0 / PATCH)
            top = jnp.where(eight == 0, first[0:8, s] - level, first[0:8, s])
            body = jnp.concatenate([top, first[8:PATCH, s]], axis=0)
            rows.append(jnp.concatenate([body, first[PATCH:, s]], axis=1).astype(bf16))
        every = mm(jnp.concatenate(rows, axis=0), dft_ref[1])
        for i in range(pair):
            both = every[i * PATCH : (i + 1) * PATCH]
            real, imag = both[:, :PATCH], both[:, PATCH:]
            energy = real * real + imag * imag
            middle = slice(PATCH // 2, PATCH // 2 + 1)
            node = first_node + i
            where = pl.ds(node, 1)
            stats[kind, 0, where] = jnp.sum(energy, axis=0, keepdims=True)
            stats[kind, 1, where] = energy[middle]
            stats[kind, 2, where] = real[middle]
            found.append((real, imag))
        return found

    def cross(a, b):
        real = a[0] * b[0] + a[1] * b[1]
        imag = a[1] * b[0] - a[0] * b[1]
        return jnp.concatenate([real, imag], axis=1).astype(bf16)

    for q in range(chunks):
        for i, (real, imag) in enumerate(spectra(whole[half, :, q * width : (q + 1) * width], 0, q * pair)):
            own_re[q * pair + i] = real
            own_im[q * pair + i] = imag

    def part(i):
        k, j = divmod(i, piece // PATCH)
        return whole[k, :, j * PATCH : (j + 1) * PATCH]

    loads[-1].wait()
    for i in range(patches):
        check[i : i + 1] = jnp.sum(part(i).astype(f32) * tables[2 * SPAN + 8 :], axis=0, keepdims=True)
    sums = jnp.sum(check[...], axis=1, keepdims=True)
    check[...] = jnp.broadcast_to(sums, check.shape)

    @pl.when(group != HUB)
    def _():
        pl.semaphore_wait(all_sem, 1)

    for step in range(1, per_section):
        mask_copy(0, step).start()

    @pl.when(group < SECTIONS - 1)
    def _():
        for step in range(per_section):
            mask_copy(1, step).start()

    @pl.when(group == 1)
    def _():
        start_bulk(1)

    for way in range(2):

        @pl.when(jnp.logical_and(group == SECTIONS - 1 - way, wrapped))
        def _():
            detour(way)

    def arrived(way, chunk):
        buffer = (next_raw if way else prev_raw).at[chunk]
        pltpu.make_async_copy(buffer, buffer, bulk_recv.at[way, chunk]).wait()

    def own(node):
        return own_re[node], own_im[node]

    up_ok = (sub_row > 0).astype(f32)
    down_ok = (sub_row < per_section - 1).astype(f32)
    left_ok = jnp.logical_and(lane > 0, lane < grid_cols).astype(f32)
    right_ok = (lane < grid_cols - 1).astype(f32)
    count = up_ok + down_ok + left_ok + right_ok

    node_sub = lax.broadcasted_iota(jnp.int32, (nodes, LANES), 0)
    node_lane = lax.broadcasted_iota(jnp.int32, (nodes, LANES), 1)
    diagonal = node_lane == base + node_sub
    nyquist = node_lane == PATCH // 2
    frequency = jnp.where(node_lane < PATCH // 2, node_lane, node_lane - PATCH).astype(f32)
    frequency = frequency * (1.0 / PATCH)
    corr_row = lax.broadcasted_iota(jnp.int32, (PADDED, PADDED), 0)
    corr_col = lax.broadcasted_iota(jnp.int32, (PADDED, PADDED), 1)
    inside = jnp.logical_and(corr_row < WINDOW, corr_col < WINDOW)
    eight_lane = lax.broadcasted_iota(jnp.int32, (8, LANES), 1)
    middle = slice(PATCH // 2, PATCH // 2 + 1)

    def column(d, which):
        line = jnp.sum(jnp.where(sub == row + which * per_section, d, 0.0), axis=0, keepdims=True)
        return jnp.sum(jnp.where(diagonal, line, 0.0), axis=1, keepdims=True)

    def flows(section, crosses, kind_a, kind_b, d):
        row_offset = offsets[0, section]
        col_offset = offsets[1, section]
        turned = []
        for which in range(2):
            cosine, sine = turn(frequency * column(d, which))
            turned.append((cosine, jnp.where(nyquist, 0.0, sine), cosine[:, middle], sine[:, middle]))
        (cos_y, sin_y, end_cy, end_sy), (cos_x, sin_x, end_cx, end_sx) = turned
        total_a = jnp.sum(stats[kind_a, 0], axis=1, keepdims=True)
        edge_col = stats[kind_b, 0]
        total_b = jnp.sum(edge_col, axis=1, keepdims=True)
        edge_row = jnp.sum(stats[kind_b, 1], axis=1, keepdims=True)
        tip_a = stats[kind_a, 2][:, middle]
        tip_b = stats[kind_b, 2][:, middle]
        tip = tip_b * tip_b
        end_both = end_cy * end_cx - end_sy * end_sx
        lost = (
            (edge_row - tip) * (end_sy * end_sy)
            + (edge_col[:, middle] - tip) * (end_sx * end_sx)
            + tip * (1.0 - end_both * end_both)
        )
        size = 1.0 / float(PATCH) ** 4
        variance_a = total_a * size + 1e-05
        variance_b = jnp.maximum((total_b - lost) * size, 0.0) + 1e-05
        scales = (sharpness * size) * lax.rsqrt(variance_a * variance_b)
        corners = end_sy * end_sx * tip_a * tip_b
        row_cos = tables[pl.ds(row_offset + REACH, PADDED), :]
        row_sin = tables[pl.ds(row_offset + REACH + SPAN, PADDED), :]
        col_cos = tables[pl.ds(col_offset + REACH, PADDED), :]
        col_sin = tables[pl.ds(col_offset + REACH + SPAN, PADDED), :]
        col_high, col_low = split(jnp.concatenate([col_cos, -col_sin], axis=1))
        moved = []
        for i in range(nodes):
            c, s = cos_y[i : i + 1], sin_y[i : i + 1]
            table = jnp.concatenate(
                [row_cos * c + row_sin * s, row_sin * c - row_cos * s], axis=0
            )
            parts = mm(jnp.concatenate(split(table), axis=0), crosses[i])
            parts = parts[: 2 * PADDED] + parts[2 * PADDED :]
            real = parts[:PADDED, :PATCH] - parts[PADDED:, PATCH:]
            imag = parts[:PADDED, PATCH:] + parts[PADDED:, :PATCH]
            c, s = cos_x[i : i + 1], sin_x[i : i + 1]
            moved.append(
                jnp.concatenate([real * c + imag * s, imag * c - real * s], axis=1)
            )
        high, low = split(jnp.concatenate(moved, axis=0))
        correlation = mm_nt(
            jnp.concatenate([high, low, high], axis=1),
            jnp.concatenate([col_high, col_high, col_low], axis=1),
        )
        odd = (corr_row + corr_col + (row_offset + col_offset + 2 * REACH)) & 1
        parity = 1.0 - 2.0 * odd.astype(f32)
        weights = []
        for i in range(nodes):
            here = correlation[i * PADDED : (i + 1) * PADDED] - corners[i : i + 1] * parity
            weights.append(jnp.where(inside, jnp.exp(here * scales[i : i + 1]), 0.0))
        across = (lax.broadcasted_iota(jnp.int32, (8, PADDED), 1) - HALF + col_offset).astype(f32)
        down = (lax.broadcasted_iota(jnp.int32, (8, PADDED), 0) - HALF + row_offset).astype(f32)
        sums = [jnp.zeros((8, LANES), f32) for _ in range(3)]
        for i in range(nodes):
            upper, lower = weights[i][:8], weights[i][8:]
            plain = upper + lower
            parts = (plain, upper * down + lower * (down + 8.0), plain * across)
            here = eight_lane == base + i
            for k in range(3):
                line = jnp.sum(parts[k], axis=1, keepdims=True)
                sums[k] = jnp.where(here, line, sums[k])
        plain, line_row, line_col = [jnp.sum(value, axis=0, keepdims=True) for value in sums]
        inverse = 1.0 / jnp.where(plain > 0.0, plain, 1.0)
        line_row = line_row * inverse
        line_col = line_col * inverse
        return line_row, line_col

    def flow_copy(phase, ahead, step):
        part = 1 - phase
        slot = 1 - ahead
        return pltpu.make_async_remote_copy(
            src_ref=flow_tile.at[phase],
            dst_ref=flow_slots.at[slot, part * per_section + row],
            send_sem=flow_send.at[phase, ahead],
            recv_sem=flow_recv.at[slot],
            device_id={"tile": device(group + phase + ahead, mate(step))},
            device_id_type=MESH,
        )

    def send_flow(phase, tile):
        for which in range(2):
            flow_tile[phase, which : which + 1] = tile[which]
            if phase == 0:
                flow_slots[1, per_section + row, which : which + 1] = tile[which]
        for step in range(1 - phase, per_section):
            flow_copy(phase, 0, step).start()

        @pl.when(group + phase + 1 < SECTIONS)
        def _():
            for step in range(per_section):
                flow_copy(phase, 1, step).start()

    def drain(ref, sem):
        pltpu.make_async_copy(ref, ref, sem).wait()

    def end_flow(phase):
        drain(flow_slots.at[0, pl.ds(0, per_section - 1 + phase)], flow_send.at[phase, 0])

        @pl.when(group + phase + 1 < SECTIONS)
        def _():
            drain(flow_slots.at[0, pl.ds(0, per_section)], flow_send.at[phase, 1])

    def masks(slot):
        drain(mask_slots.at[slot, pl.ds(0, per_section - slot)], mask_recv.at[slot])

    def gathered(slot):
        masks(slot)
        mask = jnp.zeros(shape, f32)
        for line in range(per_section):
            mask = jnp.where(sub_row == line, mask_slots[slot, line], mask)
        weight = anchor_weight * mask
        scale = 1.0 / (weight + count)
        weight = weight * scale
        up, down = up_ok * scale, down_ok * scale
        left, right = left_ok * scale, right_ok * scale
        drain(flow_slots.at[slot, pl.ds(0, 2 * per_section - slot)], flow_recv.at[slot])
        flow = jnp.zeros(shape, f32)
        for line in range(per_section):
            both = flow_slots[slot, line] + flow_slots[slot, per_section + line]
            flow = jnp.where(sub == line, both[0:1], flow)
            flow = jnp.where(sub == line + per_section, both[1:2], flow)
        pull = weight * flow
        d = flow * mask
        for _ in range(SWEEPS):
            d = pull + (
                (up * pltpu.roll(d, 1, 0) + down * pltpu.roll(d, 2 * per_section - 1, 0))
                + (left * pltpu.roll(d, 1, 1) + right * pltpu.roll(d, LANES - 1, 1))
            )
        return jnp.where(lane < grid_cols, d, 0.0)

    @pl.when(group == SECTIONS - 1)
    def _():

        @pl.when(wrapped)
        def _():
            pl.semaphore_wait(go_sem, 1)
            start_bulk(0, relayed[0])


    @pl.when(group >= 1)
    def _():
        for q in range(chunks):
            c = jnp.where(group == SECTIONS - 1, arrival[0][q], q)
            arrived(0, c)
            for i, found in enumerate(spectra(prev_raw[c], 1, c * pair)):
                down_cross[c * pair + i] = cross(own(c * pair + i), found)

        @pl.when(jnp.logical_and(group == 2, wrapped))
        def _():
            start_bulk(1, relayed[1])

        @pl.when(jnp.logical_and(group == SECTIONS - 1, jnp.logical_not(wrapped)))
        def _():
            forward(1)


        @pl.when(group >= 2)
        def _():
            shift_ref[0] = gathered(0)

        send_flow(0, flows(group, down_cross, 0, 1, shift_ref[0]))

    @pl.when(group < SECTIONS - 1)
    def _():
        for q in range(chunks):
            c = jnp.where(group == 2, arrival[1][q], q)
            arrived(1, c)
            for i, found in enumerate(spectra(next_raw[c], 2, c * pair)):
                up_cross[c * pair + i] = cross(found, own(c * pair + i))

    @pl.when(group >= 1)
    def _():
        shift_ref[1] = gathered(1)

    @pl.when(group < SECTIONS - 1)
    def _():
        send_flow(1, flows(group + 1, up_cross, 2, 0, shift_ref[1]))

        @pl.when(jnp.logical_and(group == 0, jnp.logical_not(wrapped)))
        def _():
            pl.delay(REST)

            @pl.when(lax.rem(me, 2) == 1)
            def _():
                pl.delay(LAG)

            forward(0)

        @pl.when(jnp.logical_and(group == 0, wrapped))
        def _():
            release()

    home = shift_ref[1]
    lines = [
        jnp.sum(jnp.where(sub == row + which * per_section, home, 0.0), axis=0, keepdims=True)
        for which in range(2)
    ]
    for which in range(2):
        node_ref[which] = lines[which][:, :grid_cols]
    rows = kernel_rows(term_rows(lines[0], lines[1]), tables[2 * SPAN : 2 * SPAN + 8], patches)
    corner = rows[2] * check[:, 0:1]
    for k in range(PIECES):
        for j in range(piece // PATCH):
            i = k * (piece // PATCH) + j
            moved = warp_patch(part(i), rows[0][i : i + 1], rows[1][i : i + 1])
            out[:, i * PATCH : (i + 1) * PATCH] = (
                moved - corner[i : i + 1] * tables[2 * SPAN + 8 :]
            ).astype(bf16)

    @pl.when(group == 0)
    def _():
        masks(1)

    @pl.when(group == 1)
    def _():
        masks(0)

    drain(mask_slots.at[1, pl.ds(0, per_section - 1)], mask_send.at[0])

    @pl.when(group < SECTIONS - 1)
    def _():
        drain(mask_slots.at[1, pl.ds(0, per_section)], mask_send.at[1])
        drain(next_raw, bulk_send.at[1])
        end_flow(1)

    @pl.when(group >= 1)
    def _():
        drain(prev_raw, bulk_send.at[0])
        end_flow(0)

    for way, section in ((0, 0), (1, SECTIONS - 1)):

        @pl.when(jnp.logical_and(group == section, jnp.logical_not(wrapped)))
        def _():
            drain(relay_raw.at[pl.ds(0, relayed[way])], relay_send)


def store_kernel(aligned, shift, out, shift_out, sems):
    stores = [
        pltpu.make_async_copy(shift, shift_out, sems.at[0]),
        pltpu.make_async_copy(aligned, out, sems.at[1]),
    ]
    for copy in stores:
        copy.start()
    for copy in stores:
        copy.wait()


def shards(tile_count, sections, valid_mask, coarse_offsets):
    per_section = tile_count // SECTIONS
    grid_cols = valid_mask.shape[1]
    width = CHUNK * PATCH
    chunks = sections.shape[1] // (2 * width)
    nodes = chunks * CHUNK
    tile_shape = (2 * per_section, LANES)
    vmem = pl.BlockSpec(memory_space=pltpu.VMEM)
    dft, tables = constants()
    hbm = pl.BlockSpec(memory_space=pltpu.HBM)
    raw = pltpu.VMEM((chunks, PATCH, width), bf16)
    spectrum = pltpu.VMEM((nodes, PATCH, PATCH), f32)
    crossed = pltpu.VMEM((nodes, PATCH, 2 * PATCH), bf16)
    dma = pltpu.SemaphoreType.DMA
    patches = sections.shape[1] // PATCH
    pieces = pltpu.VMEM((PIECES, PATCH, sections.shape[1] // PIECES), bf16)
    aligned, shift = pl.pallas_call(
        functools.partial(chain_kernel, tile_count, grid_cols),
        out_shape=(
            pltpu.VMEM(sections.shape, bf16),
            pltpu.VMEM((2, 1, grid_cols), f32),
        ),
        in_specs=[hbm] * 5,
        out_specs=(vmem, vmem),
        scratch_shapes=[
            pltpu.VMEM(dft.shape, bf16),
            pltpu.VMEM(tables.shape, f32),
            pieces,
            pltpu.VMEM((patches, LANES), f32),
            pltpu.SMEM(coarse_offsets.shape[::-1], jnp.int32),
            pltpu.VMEM(valid_mask.shape, jnp.int32),
            dma((6,)),
            raw,
            raw,
            spectrum,
            spectrum,
            crossed,
            crossed,
            pltpu.VMEM((3, 3, nodes, LANES), f32),
            pltpu.VMEM((1, LANES), f32),
            pltpu.VMEM((2, per_section, 1, LANES), f32),
            pltpu.VMEM((2, 2, LANES), f32),
            pltpu.VMEM((2, 2 * per_section, 2, LANES), f32),
            pltpu.VMEM((2,) + tile_shape, f32),
            dma((2,)),
            dma((2, chunks)),
            dma((2,)),
            dma((2,)),
            dma((2, 2)),
            dma((2,)),
            pltpu.SemaphoreType.REGULAR,
            pltpu.SemaphoreType.REGULAR,
            pltpu.VMEM((chunks // 2, PATCH, width), bf16),
            dma(()),
            dma(()),
        ],
        compiler_params=pltpu.CompilerParams(
            collective_id=0, has_side_effects=True
        ),
        name="chain",
    )(coarse_offsets.T, valid_mask, dft, tables, sections)
    return pl.pallas_call(
        store_kernel,
        out_shape=(
            jax.ShapeDtypeStruct(sections.shape, bf16),
            jax.ShapeDtypeStruct((2, 1, grid_cols), f32),
        ),
        in_specs=[vmem, vmem],
        out_specs=(hbm, hbm),
        scratch_shapes=[dma((2,))],
        name="store",
    )(*[pltpu.with_memory_space_constraint(x, pltpu.VMEM) for x in (aligned, shift)])


def solution(mesh):
    placed = (P(("parts", "tile"), None), P(("parts", "tile"), None), P("parts", None))
    return jax.shard_map(
        functools.partial(shards, mesh.shape["tile"]),
        mesh=mesh,
        in_specs=placed,
        out_specs=(P(("parts", "tile"), None), P(None, ("parts", "tile"), None)),
        check_vma=False,
    )
```

```python
import functools

import jax
import jax.numpy as jnp
import numpy as np
from jax import lax
from jax.experimental import pallas as pl
from jax.experimental.pallas import tpu as pltpu
from jax.sharding import PartitionSpec as P

SECTIONS = 4
PATCH = 128
HALF = 4
SWEEPS = 3
REACH = 3
WINDOW = 2 * HALF + 1
PADDED = 16
LANES = 128
CHUNK = 2
SPAN = 24
HUB = 2
REST = 1400
LAG = 500
PIECES = 2
ORDER = 1

sharpness = 12.0
anchor_weight = 2.0
MESH = pl.DeviceIdType.MESH
f32 = jnp.float32
bf16 = jnp.bfloat16


def split(value):
    high = value.astype(bf16)
    return high, (value - high.astype(f32)).astype(bf16)


def mm(a, b):
    return jnp.dot(a, b, preferred_element_type=f32)


def mm_nt(a, b):
    return lax.dot_general(a, b, (((1,), (1,)), ((), ())), preferred_element_type=f32)


def constants():
    n = PATCH
    k = np.arange(n)
    angle = 2 * np.pi * ((k[:, None] * k[None, :]) % n) / n
    cosine, sine = np.cos(angle), np.sin(angle)
    left = []
    for table in (cosine, sine):
        high = np.asarray(table, bf16)
        low = np.asarray(table - high.astype(np.float64), bf16)
        left.append(np.concatenate([high, low], axis=1))
    left = np.concatenate(left, axis=0)
    right = np.block([[cosine, -sine], [-sine, -cosine]])
    right = np.asarray(right, bf16)
    u = np.arange(-HALF - REACH, -HALF - REACH + SPAN)
    window_angle = 2 * np.pi * ((u[:, None] * k[None, :]) % n) / n
    window = np.stack([np.cos(window_angle), np.sin(window_angle)])
    window = window.astype(np.float32)
    half_angle = np.pi * k / n
    sign = 1.0 - 2.0 * (k % 2)
    warp = np.zeros((8, n), np.float32)
    warp[:4] = np.stack([np.sin(half_angle), np.cos(half_angle), sign, k])
    parity = (sign[:, None] * sign[None, :]).astype(np.float32)
    tables = np.concatenate([window[0], window[1], warp, parity], axis=0)
    return np.stack([left, right]), tables


def turn(value):
    small = (value - jnp.round(value)) * np.pi
    square = small * small
    sine = small * (1.0 + square * (-1 / 6 + square * (1 / 120 + square * (
        -1 / 5040 + square * (1 / 362880 - square * (1 / 39916800))))))
    cosine = 1.0 + square * (-1 / 2 + square * (1 / 24 + square * (-1 / 720 + square * (
        1 / 40320 + square * (-1 / 3628800 + square * (1 / 479001600))))))
    return 1.0 - 2.0 * (sine * sine), 2.0 * (sine * cosine)


def shift_terms(d):
    whole = jnp.round(d)
    frac = d - whole
    odd = jnp.abs(whole - 2.0 * jnp.round(whole * 0.5))
    wide = frac * np.pi
    square = wide * wide
    shape = 1.0 + square * (-1 / 6 + square * (1 / 120 + square * (
        -1 / 5040 + square * (1 / 362880 - square * (1 / 39916800)))))
    sine = wide * shape
    signed = jnp.where(odd > 0.5, -sine, sine) * (1.0 / PATCH)
    angle = d * (np.pi / PATCH)
    square = angle * angle
    tangent = angle * (1.0 + square * (1 / 3 + square * (2 / 15 + square * (
        17 / 315 + square * (62 / 2835 + square * (1382 / 155925))))))
    small = frac * (np.pi / PATCH)
    square = small * small
    peak = shape * (1.0 - square * (1 / 3 + square * (1 / 45)))
    return tangent, signed, peak, whole


def kernel_rows(terms, tables, patches):
    columns = jnp.transpose(terms)[:patches]
    sine, cosine, parity, gap = [tables[i : i + 1, :] for i in range(4)]
    found = []
    for base, forward in ((0, False), (4, True)):
        tangent, signed, peak, whole = [columns[:, base + i : base + i + 1] for i in range(4)]
        if forward:
            bottom = cosine * tangent + sine
            top = cosine - sine * tangent
            centre = jnp.where(whole > 0, PATCH - whole, -whole)
        else:
            bottom = cosine * tangent - sine
            top = cosine + sine * tangent
            centre = jnp.where(whole < 0, whole + PATCH, whole)
        found.append(jnp.where(gap == centre, peak, (signed * parity) * (top / bottom)))
    corner = columns[:, 1:2] * columns[:, 5:6]
    return found[0], found[1], corner


def circulant(row):
    spread = jnp.broadcast_to(row, (PATCH, PATCH))
    return split(pltpu.roll(spread, 0, 1, stride=1, stride_axis=0))


def warp_patch(patch, left_row, right_row):
    left = circulant(left_row)
    right = circulant(right_row)
    both = mm(patch, jnp.concatenate(right, axis=1))
    high, low = split(both[:, :PATCH] + both[:, PATCH:])
    lower = jnp.concatenate([high, jnp.zeros_like(low)], axis=1)
    inner = jnp.concatenate([jnp.concatenate([high, low], axis=1), lower], axis=0)
    moved = mm(jnp.concatenate(left, axis=1), inner)
    return moved[:, :PATCH] + moved[:, PATCH:]


def term_rows(d_rows, d_cols):
    both = jnp.concatenate([d_rows, d_cols], axis=0)
    tangent, signed, peak, whole = shift_terms(both)
    pieces = [t[i : i + 1] for i in range(2) for t in (tangent, signed, peak, whole)]
    return jnp.concatenate(pieces, axis=0)


def chain_kernel(
    tile_count,
    grid_cols,
    offsets_in,
    mask_in,
    dft_in,
    tables_in,
    strip,
    out,
    node_ref,
    dft_ref,
    tables,
    whole,
    check,
    offsets,
    mask_ref,
    load_sem,
    prev_raw,
    next_raw,
    own_re,
    own_im,
    down_cross,
    up_cross,
    stats,
    mask_tile,
    mask_slots,
    flow_tile,
    flow_slots,
    shift_ref,
    bulk_send,
    bulk_recv,
    mask_send,
    mask_recv,
    flow_send,
    flow_recv,
    go_sem,
    all_sem,
    relay_raw,
    relay_send,
    relay_recv,
):
    per_section = tile_count // SECTIONS
    me = lax.axis_index("tile")
    lead = per_section // 2
    rotated = lax.rem(me + tile_count - lead, tile_count)
    group = rotated // per_section
    row = lax.rem(rotated, per_section)
    chunks, width = prev_raw.shape[0], prev_raw.shape[2]
    pair = width // PATCH
    nodes = chunks * pair
    half = lax.rem(group, 2)
    base = half * nodes
    piece = whole.shape[2]
    patches = PIECES * piece // PATCH

    def device(section, line):
        return lax.rem(section * per_section + line + lead, tile_count)

    def mate(line_step):
        return lax.rem(row + line_step, per_section)

    barrier = pltpu.get_barrier_semaphore()

    def signal(sem, section, line):
        pl.semaphore_signal(
            sem, inc=1, device_id={"tile": device(section, line)}, device_id_type=MESH
        )

    @pl.when(group <= 1)
    def _():
        signal(barrier, 1 - group, row)

    @pl.when(group == HUB)
    def _():
        signal(barrier, SECTIONS - 1, row)
        for step in range(1, per_section):
            signal(barrier, HUB, mate(step))

    @pl.when(group != HUB)
    def _():
        for step in range(per_section):
            signal(barrier, HUB, mate(step))

    def columns(side, chunk):
        start = pl.multiple_of((side * chunks + chunk) * width, LANES)
        return strip.at[:, pl.ds(start, width)]

    def strip_half(side):
        return strip.at[:, pl.ds(pl.multiple_of(side * piece, LANES), piece)]

    loads = [
        pltpu.make_async_copy(source, target, load_sem.at[i])
        for i, (source, target) in enumerate(
            [(mask_in, mask_ref), (offsets_in, offsets), (dft_in, dft_ref), (tables_in, tables)]
            + [(strip_half(side), whole.at[side]) for side in (half, 1 - half)]
        )
    ]
    for copy in loads:
        copy.start()
    pl.semaphore_wait(barrier, jnp.where(group == HUB, tile_count - 1, 1))

    def bulk(way, chunk):
        peer = lax.rem(me + (per_section if way else tile_count - per_section), tile_count)
        return pltpu.make_async_remote_copy(
            src_ref=columns(1 - half, chunk),
            dst_ref=(prev_raw if way else next_raw).at[chunk],
            send_sem=bulk_send.at[way],
            recv_sem=bulk_recv.at[1 - way, chunk],
            device_id={"tile": peer},
            device_id_type=MESH,
        )

    def start_bulk(way, first=0, last=chunks):
        for chunk in range(first, last):
            bulk(way, chunk).start()

    relayed = (chunks // 2, chunks // 2)
    arrival = [
        sorted(range(chunks), key=lambda q: (q - n if q >= n else q, ORDER * (q < n)))
        for n in (relayed[1], relayed[0])
    ]
    apart = per_section - per_section // 2
    wrapped = row >= apart

    def detour(way):
        for k in range(relayed[way]):
            pltpu.make_async_remote_copy(
                src_ref=columns(1 - half, k),
                dst_ref=relay_raw.at[k],
                send_sem=bulk_send.at[way],
                recv_sem=relay_recv,
                device_id={"tile": device(SECTIONS - 1 if way else 0, row - apart)},
                device_id_type=MESH,
            ).start()

    def onward(way, k):
        return pltpu.make_async_remote_copy(
            src_ref=relay_raw.at[k],
            dst_ref=(prev_raw if way else next_raw).at[k],
            send_sem=relay_send,
            recv_sem=bulk_recv.at[1 - way, k],
            device_id={"tile": device(SECTIONS - 1 if way else 2, row + apart)},
            device_id_type=MESH,
        )

    def forward(way):
        arrival = relay_raw.at[pl.ds(0, relayed[way])]
        pltpu.make_async_copy(arrival, arrival, relay_recv).wait()
        for k in range(relayed[way]):
            onward(way, k).start()

    def release():
        signal(go_sem, SECTIONS - 1, row)

    @pl.when(group == HUB)
    def _():
        for section in range(SECTIONS):
            if section != HUB:
                signal(all_sem, section, row)

    @pl.when(jnp.logical_or(group == 1, group == 2))
    def _():
        start_bulk(0)

    @pl.when(group == 0)
    def _():
        start_bulk(1)

    for way in range(2):

        @pl.when(jnp.logical_and(group == SECTIONS - 1 - way, jnp.logical_not(wrapped)))
        def _():
            start_bulk(way)

    def mask_copy(ahead, step):
        return pltpu.make_async_remote_copy(
            src_ref=mask_tile,
            dst_ref=mask_slots.at[1 - ahead, row],
            send_sem=mask_send.at[ahead],
            recv_sem=mask_recv.at[1 - ahead],
            device_id={"tile": device(group + ahead, mate(step))},
            device_id_type=MESH,
        )

    loads[0].wait()
    shape = (2 * per_section, LANES)
    sub = lax.broadcasted_iota(jnp.int32, shape, 0)
    lane = lax.broadcasted_iota(jnp.int32, shape, 1)
    sub_row = lax.rem(sub, per_section)
    mask_tile[...] = jnp.zeros((1, LANES), f32)
    mask_tile[:, 0:grid_cols] = mask_ref[...].astype(f32)
    mask_slots[1, row] = mask_tile[...]
    shift_ref[...] = jnp.zeros((2,) + shape, f32)

    for copy in loads[1:-1]:
        copy.wait()

    eight = lax.broadcasted_iota(jnp.int32, (8, LANES), 0)

    def spectra(pixels, kind, first_node):
        table = dft_ref[0]
        first = mm(table, jnp.concatenate([pixels, pixels], axis=0))
        found, rows = [], []
        for i in range(pair):
            s = slice(i * PATCH, (i + 1) * PATCH)
            level = jnp.sum(pixels[:, s].astype(f32), axis=0, keepdims=True)
            level = jnp.sum(level, axis=1, keepdims=True) * (1.0 / PATCH)
            top = jnp.where(eight == 0, first[0:8, s] - level, first[0:8, s])
            body = jnp.concatenate([top, first[8:PATCH, s]], axis=0)
            rows.append(jnp.concatenate([body, first[PATCH:, s]], axis=1).astype(bf16))
        every = mm(jnp.concatenate(rows, axis=0), dft_ref[1])
        for i in range(pair):
            both = every[i * PATCH : (i + 1) * PATCH]
            real, imag = both[:, :PATCH], both[:, PATCH:]
            energy = real * real + imag * imag
            middle = slice(PATCH // 2, PATCH // 2 + 1)
            node = first_node + i
            where = pl.ds(node, 1)
            stats[kind, 0, where] = jnp.sum(energy, axis=0, keepdims=True)
            stats[kind, 1, where] = energy[middle]
            stats[kind, 2, where] = real[middle]
            found.append((real, imag))
        return found

    def cross(a, b):
        real = a[0] * b[0] + a[1] * b[1]
        imag = a[1] * b[0] - a[0] * b[1]
        return jnp.concatenate([real, imag], axis=1).astype(bf16)

    for q in range(chunks):
        for i, (real, imag) in enumerate(spectra(whole[half, :, q * width : (q + 1) * width], 0, q * pair)):
            own_re[q * pair + i] = real
            own_im[q * pair + i] = imag

    def part(i):
        k, j = divmod(i, piece // PATCH)
        return whole[k, :, j * PATCH : (j + 1) * PATCH]

    loads[-1].wait()
    for i in range(patches):
        check[i : i + 1] = jnp.sum(part(i).astype(f32) * tables[2 * SPAN + 8 :], axis=0, keepdims=True)
    sums = jnp.sum(check[...], axis=1, keepdims=True)
    check[...] = jnp.broadcast_to(sums, check.shape)

    @pl.when(group != HUB)
    def _():
        pl.semaphore_wait(all_sem, 1)

    for step in range(1, per_section):
        mask_copy(0, step).start()

    @pl.when(group < SECTIONS - 1)
    def _():
        for step in range(per_section):
            mask_copy(1, step).start()

    @pl.when(group == 1)
    def _():
        start_bulk(1)

    for way in range(2):

        @pl.when(jnp.logical_and(group == SECTIONS - 1 - way, wrapped))
        def _():
            detour(way)

    def arrived(way, chunk):
        buffer = (next_raw if way else prev_raw).at[chunk]
        pltpu.make_async_copy(buffer, buffer, bulk_recv.at[way, chunk]).wait()

    def own(node):
        return own_re[node], own_im[node]

    up_ok = (sub_row > 0).astype(f32)
    down_ok = (sub_row < per_section - 1).astype(f32)
    left_ok = jnp.logical_and(lane > 0, lane < grid_cols).astype(f32)
    right_ok = (lane < grid_cols - 1).astype(f32)
    count = up_ok + down_ok + left_ok + right_ok

    node_sub = lax.broadcasted_iota(jnp.int32, (nodes, LANES), 0)
    node_lane = lax.broadcasted_iota(jnp.int32, (nodes, LANES), 1)
    diagonal = node_lane == base + node_sub
    nyquist = node_lane == PATCH // 2
    frequency = jnp.where(node_lane < PATCH // 2, node_lane, node_lane - PATCH).astype(f32)
    frequency = frequency * (1.0 / PATCH)
    corr_row = lax.broadcasted_iota(jnp.int32, (PADDED, PADDED), 0)
    corr_col = lax.broadcasted_iota(jnp.int32, (PADDED, PADDED), 1)
    inside = jnp.logical_and(corr_row < WINDOW, corr_col < WINDOW)
    eight_lane = lax.broadcasted_iota(jnp.int32, (8, LANES), 1)
    middle = slice(PATCH // 2, PATCH // 2 + 1)

    def column(d, which):
        line = jnp.sum(jnp.where(sub == row + which * per_section, d, 0.0), axis=0, keepdims=True)
        return jnp.sum(jnp.where(diagonal, line, 0.0), axis=1, keepdims=True)

    def flows(section, crosses, kind_a, kind_b, d):
        row_offset = offsets[0, section]
        col_offset = offsets[1, section]
        turned = []
        for which in range(2):
            cosine, sine = turn(frequency * column(d, which))
            turned.append((cosine, jnp.where(nyquist, 0.0, sine), cosine[:, middle], sine[:, middle]))
        (cos_y, sin_y, end_cy, end_sy), (cos_x, sin_x, end_cx, end_sx) = turned
        total_a = jnp.sum(stats[kind_a, 0], axis=1, keepdims=True)
        edge_col = stats[kind_b, 0]
        total_b = jnp.sum(edge_col, axis=1, keepdims=True)
        edge_row = jnp.sum(stats[kind_b, 1], axis=1, keepdims=True)
        tip_a = stats[kind_a, 2][:, middle]
        tip_b = stats[kind_b, 2][:, middle]
        tip = tip_b * tip_b
        end_both = end_cy * end_cx - end_sy * end_sx
        lost = (
            (edge_row - tip) * (end_sy * end_sy)
            + (edge_col[:, middle] - tip) * (end_sx * end_sx)
            + tip * (1.0 - end_both * end_both)
        )
        size = 1.0 / float(PATCH) ** 4
        variance_a = total_a * size + 1e-05
        variance_b = jnp.maximum((total_b - lost) * size, 0.0) + 1e-05
        scales = (sharpness * size) * lax.rsqrt(variance_a * variance_b)
        corners = end_sy * end_sx * tip_a * tip_b
        row_cos = tables[pl.ds(row_offset + REACH, PADDED), :]
        row_sin = tables[pl.ds(row_offset + REACH + SPAN, PADDED), :]
        col_cos = tables[pl.ds(col_offset + REACH, PADDED), :]
        col_sin = tables[pl.ds(col_offset + REACH + SPAN, PADDED), :]
        col_high, col_low = split(jnp.concatenate([col_cos, -col_sin], axis=1))
        moved = []
        for i in range(nodes):
            c, s = cos_y[i : i + 1], sin_y[i : i + 1]
            table = jnp.concatenate(
                [row_cos * c + row_sin * s, row_sin * c - row_cos * s], axis=0
            )
            parts = mm(jnp.concatenate(split(table), axis=0), crosses[i])
            parts = parts[: 2 * PADDED] + parts[2 * PADDED :]
            real = parts[:PADDED, :PATCH] - parts[PADDED:, PATCH:]
            imag = parts[:PADDED, PATCH:] + parts[PADDED:, :PATCH]
            c, s = cos_x[i : i + 1], sin_x[i : i + 1]
            moved.append(
                jnp.concatenate([real * c + imag * s, imag * c - real * s], axis=1)
            )
        high, low = split(jnp.concatenate(moved, axis=0))
        correlation = mm_nt(
            jnp.concatenate([high, low, high], axis=1),
            jnp.concatenate([col_high, col_high, col_low], axis=1),
        )
        odd = (corr_row + corr_col + (row_offset + col_offset + 2 * REACH)) & 1
        parity = 1.0 - 2.0 * odd.astype(f32)
        weights = []
        for i in range(nodes):
            here = correlation[i * PADDED : (i + 1) * PADDED] - corners[i : i + 1] * parity
            weights.append(jnp.where(inside, jnp.exp(here * scales[i : i + 1]), 0.0))
        across = (lax.broadcasted_iota(jnp.int32, (8, PADDED), 1) - HALF + col_offset).astype(f32)
        down = (lax.broadcasted_iota(jnp.int32, (8, PADDED), 0) - HALF + row_offset).astype(f32)
        sums = [jnp.zeros((8, LANES), f32) for _ in range(3)]
        for i in range(nodes):
            upper, lower = weights[i][:8], weights[i][8:]
            plain = upper + lower
            parts = (plain, upper * down + lower * (down + 8.0), plain * across)
            here = eight_lane == base + i
            for k in range(3):
                line = jnp.sum(parts[k], axis=1, keepdims=True)
                sums[k] = jnp.where(here, line, sums[k])
        plain, line_row, line_col = [jnp.sum(value, axis=0, keepdims=True) for value in sums]
        inverse = 1.0 / jnp.where(plain > 0.0, plain, 1.0)
        line_row = line_row * inverse
        line_col = line_col * inverse
        return line_row, line_col

    def flow_copy(phase, ahead, step):
        part = 1 - phase
        slot = 1 - ahead
        return pltpu.make_async_remote_copy(
            src_ref=flow_tile.at[phase],
            dst_ref=flow_slots.at[slot, part * per_section + row],
            send_sem=flow_send.at[phase],
            recv_sem=flow_recv.at[slot],
            device_id={"tile": device(group + phase + ahead, mate(step))},
            device_id_type=MESH,
        )

    def send_flow(phase, tile):
        for which in range(2):
            flow_tile[phase, which : which + 1] = tile[which]
            if phase == 0:
                flow_slots[1, per_section + row, which : which + 1] = tile[which]
        for step in range(1 - phase, per_section):
            flow_copy(phase, 0, step).start()

        @pl.when(group + phase + 1 < SECTIONS)
        def _():
            for step in range(per_section):
                flow_copy(phase, 1, step).start()

    def drain(ref, sem):
        pltpu.make_async_copy(ref, ref, sem).wait()

    def end_flow(phase):
        near = per_section - 1 + phase

        @pl.when(group + phase + 1 < SECTIONS)
        def _():
            drain(flow_slots.at[0, pl.ds(0, near + per_section)], flow_send.at[phase])

        @pl.when(group + phase + 1 >= SECTIONS)
        def _():
            drain(flow_slots.at[0, pl.ds(0, near)], flow_send.at[phase])

    def masks(slot):
        drain(mask_slots.at[slot, pl.ds(0, per_section - slot)], mask_recv.at[slot])

    def gathered(slot):
        masks(slot)
        mask = jnp.zeros(shape, f32)
        for line in range(per_section):
            mask = jnp.where(sub_row == line, mask_slots[slot, line], mask)
        weight = anchor_weight * mask
        scale = 1.0 / (weight + count)
        weight = weight * scale
        up, down = up_ok * scale, down_ok * scale
        left, right = left_ok * scale, right_ok * scale
        drain(flow_slots.at[slot, pl.ds(0, 2 * per_section - slot)], flow_recv.at[slot])
        flow = jnp.zeros(shape, f32)
        for line in range(per_section):
            both = flow_slots[slot, line] + flow_slots[slot, per_section + line]
            flow = jnp.where(sub == line, both[0:1], flow)
            flow = jnp.where(sub == line + per_section, both[1:2], flow)
        pull = weight * flow
        d = flow * mask
        for _ in range(SWEEPS):
            d = pull + (
                (up * pltpu.roll(d, 1, 0) + down * pltpu.roll(d, 2 * per_section - 1, 0))
                + (left * pltpu.roll(d, 1, 1) + right * pltpu.roll(d, LANES - 1, 1))
            )
        return jnp.where(lane < grid_cols, d, 0.0)

    @pl.when(group == SECTIONS - 1)
    def _():

        @pl.when(wrapped)
        def _():
            pl.semaphore_wait(go_sem, 1)
            start_bulk(0, relayed[0])


    @pl.when(group >= 1)
    def _():
        for q in range(chunks):
            c = jnp.where(group == SECTIONS - 1, arrival[0][q], q)
            arrived(0, c)
            for i, found in enumerate(spectra(prev_raw[c], 1, c * pair)):
                down_cross[c * pair + i] = cross(own(c * pair + i), found)

        @pl.when(jnp.logical_and(group == 2, wrapped))
        def _():
            start_bulk(1, relayed[1])

        @pl.when(jnp.logical_and(group == SECTIONS - 1, jnp.logical_not(wrapped)))
        def _():
            forward(1)


        @pl.when(group >= 2)
        def _():
            shift_ref[0] = gathered(0)

        send_flow(0, flows(group, down_cross, 0, 1, shift_ref[0]))

    @pl.when(group < SECTIONS - 1)
    def _():
        for q in range(chunks):
            c = jnp.where(group == 2, arrival[1][q], q)
            arrived(1, c)
            for i, found in enumerate(spectra(next_raw[c], 2, c * pair)):
                up_cross[c * pair + i] = cross(found, own(c * pair + i))

    @pl.when(group >= 1)
    def _():
        shift_ref[1] = gathered(1)

    @pl.when(group < SECTIONS - 1)
    def _():
        send_flow(1, flows(group + 1, up_cross, 2, 0, shift_ref[1]))

        @pl.when(jnp.logical_and(group == 0, jnp.logical_not(wrapped)))
        def _():
            pl.delay(REST)

            @pl.when(lax.rem(me, 2) == 1)
            def _():
                pl.delay(LAG)

            forward(0)

        @pl.when(jnp.logical_and(group == 0, wrapped))
        def _():
            release()

    home = shift_ref[1]
    lines = [
        jnp.sum(jnp.where(sub == row + which * per_section, home, 0.0), axis=0, keepdims=True)
        for which in range(2)
    ]
    for which in range(2):
        node_ref[which] = lines[which][:, :grid_cols]
    rows = kernel_rows(term_rows(lines[0], lines[1]), tables[2 * SPAN : 2 * SPAN + 8], patches)
    corner = rows[2] * check[:, 0:1]
    for k in range(PIECES):
        for j in range(piece // PATCH):
            i = k * (piece // PATCH) + j
            moved = warp_patch(part(i), rows[0][i : i + 1], rows[1][i : i + 1])
            out[:, i * PATCH : (i + 1) * PATCH] = (
                moved - corner[i : i + 1] * tables[2 * SPAN + 8 :]
            ).astype(bf16)

    @pl.when(group == 0)
    def _():
        masks(1)

    @pl.when(group == 1)
    def _():
        masks(0)

    drain(mask_slots.at[1, pl.ds(0, per_section - 1)], mask_send.at[0])

    @pl.when(group < SECTIONS - 1)
    def _():
        drain(mask_slots.at[1, pl.ds(0, per_section)], mask_send.at[1])
        drain(next_raw, bulk_send.at[1])
        end_flow(1)

    @pl.when(group >= 1)
    def _():
        drain(prev_raw, bulk_send.at[0])
        end_flow(0)

    for way, section in ((0, 0), (1, SECTIONS - 1)):

        @pl.when(jnp.logical_and(group == section, jnp.logical_not(wrapped)))
        def _():
            drain(relay_raw.at[pl.ds(0, relayed[way])], relay_send)


def store_kernel(aligned, shift, out, shift_out, sems):
    stores = [
        pltpu.make_async_copy(shift, shift_out, sems.at[0]),
        pltpu.make_async_copy(aligned, out, sems.at[1]),
    ]
    for copy in stores:
        copy.start()
    for copy in stores:
        copy.wait()


def shards(tile_count, sections, valid_mask, coarse_offsets):
    per_section = tile_count // SECTIONS
    grid_cols = valid_mask.shape[1]
    width = CHUNK * PATCH
    chunks = sections.shape[1] // (2 * width)
    nodes = chunks * CHUNK
    tile_shape = (2 * per_section, LANES)
    vmem = pl.BlockSpec(memory_space=pltpu.VMEM)
    dft, tables = constants()
    hbm = pl.BlockSpec(memory_space=pltpu.HBM)
    raw = pltpu.VMEM((chunks, PATCH, width), bf16)
    spectrum = pltpu.VMEM((nodes, PATCH, PATCH), f32)
    crossed = pltpu.VMEM((nodes, PATCH, 2 * PATCH), bf16)
    dma = pltpu.SemaphoreType.DMA
    patches = sections.shape[1] // PATCH
    pieces = pltpu.VMEM((PIECES, PATCH, sections.shape[1] // PIECES), bf16)
    aligned, shift = pl.pallas_call(
        functools.partial(chain_kernel, tile_count, grid_cols),
        out_shape=(
            pltpu.VMEM(sections.shape, bf16),
            pltpu.VMEM((2, 1, grid_cols), f32),
        ),
        in_specs=[hbm] * 5,
        out_specs=(vmem, vmem),
        scratch_shapes=[
            pltpu.VMEM(dft.shape, bf16),
            pltpu.VMEM(tables.shape, f32),
            pieces,
            pltpu.VMEM((patches, LANES), f32),
            pltpu.SMEM(coarse_offsets.shape[::-1], jnp.int32),
            pltpu.VMEM(valid_mask.shape, jnp.int32),
            dma((6,)),
            raw,
            raw,
            spectrum,
            spectrum,
            crossed,
            crossed,
            pltpu.VMEM((3, 3, nodes, LANES), f32),
            pltpu.VMEM((1, LANES), f32),
            pltpu.VMEM((2, per_section, 1, LANES), f32),
            pltpu.VMEM((2, 2, LANES), f32),
            pltpu.VMEM((2, 2 * per_section, 2, LANES), f32),
            pltpu.VMEM((2,) + tile_shape, f32),
            dma((2,)),
            dma((2, chunks)),
            dma((2,)),
            dma((2,)),
            dma((2,)),
            dma((2,)),
            pltpu.SemaphoreType.REGULAR,
            pltpu.SemaphoreType.REGULAR,
            pltpu.VMEM((chunks // 2, PATCH, width), bf16),
            dma(()),
            dma(()),
        ],
        compiler_params=pltpu.CompilerParams(
            collective_id=0, has_side_effects=True
        ),
        name="chain",
    )(coarse_offsets.T, valid_mask, dft, tables, sections)
    return pl.pallas_call(
        store_kernel,
        out_shape=(
            jax.ShapeDtypeStruct(sections.shape, bf16),
            jax.ShapeDtypeStruct((2, 1, grid_cols), f32),
        ),
        in_specs=[vmem, vmem],
        out_specs=(hbm, hbm),
        scratch_shapes=[dma((2,))],
        name="store",
    )(*[pltpu.with_memory_space_constraint(x, pltpu.VMEM) for x in (aligned, shift)])


def solution(mesh):
    placed = (P(("parts", "tile"), None), P(("parts", "tile"), None), P("parts", None))
    return jax.shard_map(
        functools.partial(shards, mesh.shape["tile"]),
        mesh=mesh,
        in_specs=placed,
        out_specs=(P(("parts", "tile"), None), P(None, ("parts", "tile"), None)),
        check_vma=False,
    )
```
